32 devices in a mesh: fsdp: 8 (over z, y), tp: 4 (over x, core).
Axes of the slice: x: 2, y: 2, z: 4, core: 2. Of those that a mesh axis runs over, the one named last changes fastest.
Arguments:
- layer_in: bfloat16 [8192, 2048], P(('fsdp', 'tp')), may hold values from -6 to 6
- lengths: int32 [4], replicated, may hold values from 1537 to 2048, as said below
- clip_level: int32 [1], replicated, may hold values from 32 to 80
- attn_gain: bfloat16 [2048], replicated, may hold values from 0.5 to 1.5
- w_query: bfloat16 [2048, 2048], P('fsdp', 'tp'), may hold values from -0.70710678 to 0.70710678
- w_key: bfloat16 [2048, 512], P('fsdp', 'tp'), may hold values from -0.375 to 0.375
- w_value: bfloat16 [2048, 512], P('fsdp', 'tp'), may hold values from -0.125 to 0.125
- w_out: bfloat16 [2048, 2048], P('tp', 'fsdp'), may hold values from -6 to 6
- mlp_gain: bfloat16 [2048], replicated, may hold values from 0.5 to 1.5
- w_gate: bfloat16 [2048, 8192], P('fsdp', 'tp'), may hold values from -0.125 to 0.125
- w_up: bfloat16 [2048, 8192], P('fsdp', 'tp'), may hold values from -0.125 to 0.125
- w_down: bfloat16 [8192, 2048], P('tp', 'fsdp'), may hold values from -0.5 to 0.5
- cotangent: bfloat16 [8192, 2048], P(('fsdp', 'tp')), may hold values from -6 to 6
Outputs:
- layer_out: bfloat16 [8192, 2048], P(('fsdp', 'tp'))
- input_grad: bfloat16 [8192, 2048], P(('fsdp', 'tp'))
- attn_gain_grad: float32 [2048], P(('fsdp', 'tp'))
- query_grad: float32 [2048, 2048], P('fsdp', 'tp')
- key_grad: float32 [2048, 512], P('fsdp', 'tp')
- value_grad: float32 [2048, 512], P('fsdp', 'tp')
- out_grad: float32 [2048, 2048], P('tp', 'fsdp')
- mlp_gain_grad: float32 [2048], P(('fsdp', 'tp'))
- gate_grad: float32 [2048, 8192], P('fsdp', 'tp')
- up_grad: float32 [2048, 8192], P('fsdp', 'tp')
- down_grad: float32 [8192, 2048], P('tp', 'fsdp')
- query_clipped: float32 [2048, 2048], P('fsdp', 'tp')
- key_clipped: float32 [2048, 512], P('fsdp', 'tp')
The draws below stay inside these ranges and needn't reach their ends.
Inputs may be any that keep to these rules, and one draw needn't show every extreme that they name: lengths of the 4 slots; one slot has all 2048 tokens live.
All inputs are finite; a program needn't handle non-finite values.
Results may differ from the reference program's by a relative error of at most 0.02.
The reference program's roundings to bfloat16 on the way count: a program that leaves them out, or rounds other values in their place, can miss the bound.
Values may be sent and summed in bfloat16 or wider, within the bound.
No kernel may reach another device: no remote copies, remote signals or barrier semaphores. Data moves between devices by JAX's collectives and lax.ppermute only.
A program may use at most 320 MiB of HBM per device.

```python
import math
import jax
import jax.numpy as jnp
from jax import lax

D = 2048
H = 32
KV = 8
HD = 64
FF = 8192
SLOT_LEN = 2048
LEAD = 512
TOKENS = 8192
SLOTS = 4


def draw_lengths(key, part):
    first_key, second_key, third_key = jax.random.split(key, 3)
    least = SLOT_LEN - LEAD + 1
    values = jax.random.randint(first_key, (SLOTS,), least, SLOT_LEN + 1)
    longest = jax.random.randint(second_key, (), 0, SLOTS)
    shortest = (longest + 1 + jax.random.randint(third_key, (), 0, max(SLOTS - 1, 1))) % SLOTS
    slot_ids = jnp.arange(SLOTS)
    values = jnp.where(slot_ids == shortest, least, values)
    values = jnp.where(slot_ids == longest, SLOT_LEN, values)
    return values.astype(jnp.int32)


def draw_w_query(key, part):
    scale_key, value_key = jax.random.split(jax.random.fold_in(key, 17))
    head_scale = jnp.exp(jax.random.uniform(scale_key, (H,), jnp.float32, math.log(0.5), math.log(2.0)))
    values = jax.random.truncated_normal(value_key, -4.0, 4.0, (D, H * HD), jnp.float32)
    columns = jnp.repeat(head_scale, HD)
    return (values * columns[None, :] * (4.0 / math.sqrt(D))).astype(jnp.bfloat16)


def spiked(drawn, rng, source, target, shards_of, factor):
    def block_of(axis_at):
        return (jnp.arange(drawn.shape[axis_at]) // (drawn.shape[axis_at] // shards_of)).reshape((-1,) + (1,) * (drawn.ndim - 1 - axis_at))

    first = jax.random.permutation(rng, shards_of)[block_of(target)]
    other_side = (block_of(target) + shards_of // 2) % shards_of
    return jnp.where((block_of(source) == first) | (block_of(source) == other_side), factor * drawn, drawn)


def block_levels(stream_key, shape, cuts, low, high):
    level, own = 1.0, jax.random.fold_in(stream_key, 6)
    for position, parts in cuts:
        steps = jnp.exp(jax.random.uniform(jax.random.fold_in(own, position), (parts,), jnp.float32, low / len(cuts), high / len(cuts)))
        level = level * jnp.repeat(steps, shape[position] // parts).reshape([-1 if axis == position else 1 for axis in range(len(shape))])
    return level


def noise(rng, dims, spread, bound, pieces=(), kind=jnp.bfloat16):
    drawn = spread * jax.random.normal(rng, dims, jnp.float32)
    if pieces:
        drawn = drawn * block_levels(rng, dims, pieces, -0.22, 0.18)
    return jnp.clip(drawn, -bound, bound).astype(kind)


def noise_with(rng, shape, spread, most, pieces, heavy, held_as=jnp.bfloat16):
    entries = spread * jax.random.normal(rng, shape, jnp.float32)
    if pieces:
        entries = entries * block_levels(rng, shape, pieces, -0.22, 0.18)
    return jnp.clip(spiked(entries, jax.random.fold_in(rng, 3), *heavy), -most, most).astype(held_as)


def setup_inputs(seed: int = 0) -> dict:
    key_list = jax.random.split(jax.random.key(seed), 14)
    layer_in = noise(key_list[0], (TOKENS, D), 1.0, 6.0, ((0, 32),))
    lengths = draw_lengths(jax.random.fold_in(key_list[13], 71), 0)
    clip_level = jax.random.randint(key_list[2], (1,), HD // 2, HD * 5 // 4 + 1).astype(jnp.int32)
    attn_gain = jnp.clip(1.0 + 0.1 * jax.random.normal(key_list[3], (D,), jnp.float32), 0.5, 1.5).astype(jnp.bfloat16)
    w_query = draw_w_query(jax.random.fold_in(key_list[13], 71), 0)
    w_key = noise(key_list[5], (D, KV * HD), (D // 9) ** -0.5, 0.375, ((0, 8), (1, 4)))
    w_value = noise(key_list[6], (D, KV * HD), D ** -0.5, 0.125, ((0, 8), (1, 4)))
    w_out = noise(key_list[7], (H * HD, D), 1.0, 6.0, ((0, 4), (1, 8)))
    mlp_gain = jnp.clip(1.0 + 0.1 * jax.random.normal(key_list[8], (D,), jnp.float32), 0.5, 1.5).astype(jnp.bfloat16)
    w_gate = noise(key_list[9], (D, FF), D ** -0.5, 0.125, ((0, 8), (1, 4)))
    w_up = noise(key_list[10], (D, FF), D ** -0.5, 0.125, ((0, 8), (1, 4)))
    w_down = noise(key_list[11], (FF, D), (FF // 64) ** -0.5, 0.5, ((0, 4), (1, 8)))
    cotangent = noise_with(key_list[12], (TOKENS, D), 1.0, 6.0, ((0, 32),), (0, 1, 32, 2.75))
    return {"layer_in": layer_in, "lengths": lengths, "clip_level": clip_level, "attn_gain": attn_gain, "w_query": w_query, "w_key": w_key, "w_value": w_value, "w_out": w_out, "mlp_gain": mlp_gain, "w_gate": w_gate, "w_up": w_up, "w_down": w_down, "cotangent": cotangent}


EPSILON = 1e-05
THETA = 10000000.0
MULTIPLIER = 0.015625
RESIDUAL = 0.22
LEVEL_UNIT = 0.125
NEGATIVE = -1e+30
PRECISION = lax.Precision.HIGHEST

@jax.custom_vjp
def low(v):
    return lax.optimization_barrier(v.astype(jnp.bfloat16)).astype(jnp.float32)

@jax.custom_vjp
def low_back(v):
    return v

def low_keep(v):
    return (low(v), None)

def low_pass(kept, grad):
    return (grad,)

def back_keep(v):
    return (v, None)

def back_low(kept, grad):
    return (low(grad),)
low.defvjp(low_keep, low_pass)
low_back.defvjp(back_keep, back_low)

def rotation_tables(positions):
    half_dim = HD // 2
    freq_table = THETA ** (-(jnp.arange(half_dim, dtype=jnp.float32) * 2.0 / HD))
    angle_table = positions.astype(jnp.float32)[:, None] * freq_table[None, :]
    return (jnp.cos(angle_table), jnp.sin(angle_table))

def rotate(flat_rows, cosine_table, sine_table, direction):
    row_count = flat_rows.shape[0]
    halves = flat_rows.reshape(row_count, -1, 2, HD // 2)
    first_half = halves[:, :, 0, :]
    second_half = halves[:, :, 1, :]
    cos_part = cosine_table[:, None, :]
    sin_part = sine_table[:, None, :]
    turned = jnp.stack((first_half * cos_part - direction * second_half * sin_part, second_half * cos_part + direction * first_half * sin_part), axis=2)
    return turned.reshape(row_count, -1)

def matmul(left, right):
    return jnp.dot(left, right, preferred_element_type=jnp.float32, precision=PRECISION)

def attend(query_slot, key_slot, value_slot, live_len):
    rep_count = H // KV
    slot_pos = jnp.arange(SLOT_LEN, dtype=jnp.int32)
    allowed = slot_pos[None, :] <= slot_pos[:, None]
    counted = allowed & (slot_pos < live_len)[:, None]

    def one_group(group_index):
        query_part = lax.dynamic_slice_in_dim(query_slot, group_index * (rep_count * HD), rep_count * HD, 1)
        query_part = query_part.reshape(SLOT_LEN, rep_count, HD)
        key_part = lax.dynamic_slice_in_dim(key_slot, group_index * HD, HD, 1)
        value_part = lax.dynamic_slice_in_dim(value_slot, group_index * HD, HD, 1)
        raw_scores = jnp.einsum('qrd,kd->rqk', query_part, key_part, precision=PRECISION)
        scores = jnp.where(allowed[None], MULTIPLIER * low_back(raw_scores), NEGATIVE)
        row_top = lax.optimization_barrier(jnp.max(scores, axis=2, keepdims=True))
        row_total = lax.optimization_barrier(jnp.sum(jnp.exp(scores - row_top), axis=2, keepdims=True))
        log_total = row_top + jnp.log(row_total)
        attn_probs = low(jnp.exp(scores - log_total))
        mixed = jnp.einsum('rqk,kd->qrd', attn_probs, value_part, precision=PRECISION)
        head_peak = lax.optimization_barrier(jnp.max(jnp.where(counted[None], scores, NEGATIVE), axis=(1, 2)))
        return (mixed.reshape(SLOT_LEN, rep_count * HD), head_peak)
    mixed_all, peaks = lax.map(jax.checkpoint(one_group), jnp.arange(KV, dtype=jnp.int32))
    return (jnp.transpose(mixed_all, (1, 0, 2)).reshape(SLOT_LEN, H * HD), peaks.reshape(H))

def slot_step(packed):
    query_slot, key_slot, value_slot, live_len = packed
    return jax.checkpoint(attend)(query_slot, key_slot, value_slot, live_len)

def layer_fwd(layer_f, attn_g, query_w, key_w, value_w, out_w, mlp_g, gate_w, up_w, down_w, live_mask, cosine_table, sine_table, lengths):
    scale_one = lax.rsqrt(lax.optimization_barrier(jnp.mean(layer_f * layer_f, axis=1, keepdims=True)) + EPSILON)
    normed_one = low(layer_f * scale_one)
    acts_one = low(normed_one * attn_g[None, :])
    queries = low(rotate(low_back(matmul(acts_one, query_w)), cosine_table, sine_table, 1.0))
    keys = low(rotate(low_back(matmul(acts_one, key_w)), cosine_table, sine_table, 1.0))
    values = low_back(low(matmul(acts_one, value_w)))
    packed_q = jnp.roll(queries, LEAD, axis=0).reshape(SLOTS, SLOT_LEN, H * HD)
    packed_k = jnp.roll(keys, LEAD, axis=0).reshape(SLOTS, SLOT_LEN, KV * HD)
    packed_v = jnp.roll(values, LEAD, axis=0).reshape(SLOTS, SLOT_LEN, KV * HD)
    mixed, peaks = lax.map(slot_step, (packed_q, packed_k, packed_v, lengths))
    mixed = jnp.roll(mixed.reshape(TOKENS, H * HD), -LEAD, axis=0)
    attn_heads = low_back(low(mixed))
    branch_one = low_back(matmul(attn_heads, out_w))
    resid = layer_f + RESIDUAL * live_mask * branch_one
    scale_two = lax.rsqrt(lax.optimization_barrier(jnp.mean(resid * resid, axis=1, keepdims=True)) + EPSILON)
    normed_two = low(resid * scale_two)
    acts_two = low(normed_two * mlp_g[None, :])
    gate_proj = low_back(matmul(acts_two, gate_w))
    up_proj = low_back(matmul(acts_two, up_w))
    hidden = low(jax.nn.silu(gate_proj) * up_proj)
    branch_two = low_back(matmul(hidden, down_w))
    result = resid + RESIDUAL * live_mask * branch_two
    return (result, lax.optimization_barrier(jnp.max(peaks, axis=0)))

def reference(layer_in, lengths, clip_level, attn_gain, w_query, w_key, w_value, w_out, mlp_gain, w_gate, w_up, w_down, cotangent):
    token_ids = jnp.arange(TOKENS, dtype=jnp.int32)
    packed_ids = (token_ids + LEAD) % TOKENS
    positions = packed_ids % SLOT_LEN
    slot_ids = packed_ids // SLOT_LEN
    live_mask = (positions < lengths[slot_ids]).astype(jnp.float32)[:, None]
    cosine_table, sine_table = rotation_tables(positions)

    def forward(layer_f, attn_g, query_w, key_w, value_w, out_w, mlp_g, gate_w, up_w, down_w):
        return layer_fwd(layer_f, attn_g, query_w, key_w, value_w, out_w, mlp_g, gate_w, up_w, down_w, live_mask, cosine_table, sine_table, lengths)
    result, pullback, peak = jax.vjp(forward, layer_in.astype(jnp.float32), attn_gain.astype(jnp.float32), w_query.astype(jnp.float32), w_key.astype(jnp.float32), w_value.astype(jnp.float32), w_out.astype(jnp.float32), mlp_gain.astype(jnp.float32), w_gate.astype(jnp.float32), w_up.astype(jnp.float32), w_down.astype(jnp.float32), has_aux=True)
    grads = pullback(cotangent.astype(jnp.float32))
    level = clip_level[0].astype(jnp.float32) * LEVEL_UNIT
    factor = level / jnp.maximum(level, peak)
    query_clipped = w_query.astype(jnp.float32) * jnp.repeat(jnp.sqrt(factor), HD)[None, :]
    kv_factor = lax.optimization_barrier(jnp.min(factor.reshape(KV, H // KV), axis=1))
    key_clipped = w_key.astype(jnp.float32) * jnp.repeat(jnp.sqrt(kv_factor), HD)[None, :]
    return (result.astype(jnp.bfloat16), grads[0].astype(jnp.bfloat16), grads[1], grads[2], grads[3], grads[4], grads[5], grads[6], grads[7], grads[8], grads[9], query_clipped, key_clipped)
```

```python
import jax
import jax.numpy as jnp
import numpy as np
from jax import lax
from jax.experimental import pallas as pl
from jax.experimental.pallas import tpu as pltpu
from jax.sharding import Mesh
from jax.sharding import PartitionSpec as P

HD = 64
HALF = HD // 2
SLOT_LEN = 2048
LEAD = 512
CHUNK = 512
BLOCK = 256
HEADS = 4

EPSILON = 1e-05
THETA = 10000000.0
MULTIPLIER = 0.015625
RESIDUAL = 0.22
LEVEL_UNIT = 0.125
NEGATIVE = -1e30
GROUP = ("y", "x", "c")
EVERY = ("z", "y", "x", "c")
F32 = jnp.float32
BF16 = jnp.bfloat16


def swap(x, axis):
    return lax.ppermute(x, axis, [(0, 1), (1, 0)])


def along(x, by):
    peers = lax.axis_size("z")
    return lax.ppermute(x, "z", [(i, (i + by) % peers) for i in range(peers)])


def dot(left, right, left_dim, right_dim):
    return lax.dot_general(
        left, right, (((left_dim,), (right_dim,)), ((), ())), preferred_element_type=F32
    )


def half_of(x, which, axis):
    size = x.shape[axis] // 2
    return lax.dynamic_slice_in_dim(x, which * size, size, axis)


def ordered(own, other, rank, axis):
    return jnp.where(
        rank == 0,
        jnp.concatenate((own, other), axis=axis),
        jnp.concatenate((other, own), axis=axis),
    )


def gather_rows(v):
    half = v.shape[0] // 2
    a00, b00 = v[:half], v[half:]
    a01 = swap(a00, "x")
    b10 = swap(b00, "y")
    a1 = swap(jnp.concatenate((a00, a01)), "y")
    b1 = swap(jnp.concatenate((b00, b10)), "x")
    own = jnp.concatenate((v, a01, b1[:half], a1[:half], b10, a1[half:], b1[half:]))
    return jnp.concatenate((own, swap(own, "c")))


def scatter_rows(low, high):
    sent = swap(high().astype(BF16), "c")
    total = low() + sent.astype(F32)
    rows = total.shape[0] // 4
    cols = total.shape[1] // 2
    blocks = total.reshape(2, 2, rows, 2 * cols)
    left, right = blocks[..., :cols], blocks[..., cols:]
    left_x = swap(left[:, 1].astype(BF16), "x").astype(F32)
    right_y = swap(right[1].astype(BF16), "y").astype(F32)
    left_y = swap((left[1, 0] + left_x[1]).astype(BF16), "y").astype(F32)
    right_x = swap((right[0, 1] + right_y[1]).astype(BF16), "x").astype(F32)
    return jnp.concatenate(
        (left[0, 0] + left_x[0] + left_y, right[0, 0] + right_y[0] + right_x), axis=1
    )


def place_of(block, rank):
    j = jnp.bitwise_xor(block, rank)
    return jnp.bitwise_or(jnp.left_shift(jnp.bitwise_and(j, 1), 2), jnp.right_shift(j, 1))


def lanes_of(block, rank):
    return pl.ds(pl.multiple_of(place_of(block, rank) * BLOCK, BLOCK), BLOCK)


def rope_kernel(info, qkv, cos, sin, out):
    rank = info[0]

    @pl.loop(0, SLOT_LEN // BLOCK)
    def _(block):
        source = lanes_of(block, rank)
        target = pl.ds(pl.multiple_of(block * BLOCK, BLOCK), BLOCK)
        c, s = cos[:, target], sin[:, target]
        for head in range(HEADS + 1):
            first = qkv[pl.ds(head * HD, HALF), source]
            second = qkv[pl.ds(head * HD + HALF, HALF), source]
            scale = MULTIPLIER if head < HEADS else 1.0
            out[pl.ds(head * HD, HALF), target] = ((first * c - second * s).astype(BF16) * scale).astype(BF16)
            out[pl.ds(head * HD + HALF, HALF), target] = ((second * c + first * s).astype(BF16) * scale).astype(BF16)
        rest = (HEADS + 1) * HD
        out[pl.ds(rest, HD), target] = qkv[pl.ds(rest, HD), source].astype(BF16)


KEYS = SLOT_LEN + LEAD
K_AT = HEADS * HD
V_AT = K_AT + HD


def upright(x):
    return x.astype(F32).T.astype(BF16)


def causal():
    keys = lax.broadcasted_iota(jnp.int32, (CHUNK, CHUNK), 0)
    queries = lax.broadcasted_iota(jnp.int32, (CHUNK, CHUNK), 1)
    return keys <= queries


def key_range(step):
    last = step == SLOT_LEN // CHUNK - 1
    low = jnp.where(last, KEYS // CHUNK - 1, 0)
    high = jnp.where(last, KEYS // CHUNK, step + 2)
    return low, high


def chunk_of(i):
    return pl.ds(pl.multiple_of(i * CHUNK, CHUNK), CHUNK)


def head_rows(h):
    return pl.ds(pl.multiple_of(h * HD, HD), HD)


def attend_kernel(info, qkv, halo, heads_out, lse_out, peak_out, k_up, v_flat, scores):
    rank = info[0]
    k_up[pl.ds(0, LEAD), :] = upright(halo[pl.ds(0, HD), :])
    v_flat[:, pl.ds(0, LEAD)] = halo[pl.ds(HD, HD), :]
    v_flat[:, pl.ds(LEAD, SLOT_LEN)] = qkv[pl.ds(V_AT, HD), :]

    @pl.loop(0, SLOT_LEN // CHUNK)
    def _(i):
        k_up[pl.ds(pl.multiple_of(LEAD + i * CHUNK, CHUNK), CHUNK), :] = upright(
            qkv[pl.ds(K_AT, HD), chunk_of(i)]
        )

    peak_out[...] = jnp.full(peak_out.shape, NEGATIVE, F32)
    lse_out[...] = jnp.zeros(lse_out.shape, F32)

    @pl.loop(0, HEADS)
    def _(h):
        @pl.loop(0, SLOT_LEN // CHUNK)
        def _(step):
            low, high = key_range(step)
            query = qkv[head_rows(h), chunk_of(step)]

            def raw(kc):
                return jnp.dot(k_up[chunk_of(kc), :], query, preferred_element_type=F32)

            def first(kc, top):
                s = raw(kc)
                scores[chunk_of(kc - low), :] = s
                return jnp.maximum(top, jnp.max(s, axis=0, keepdims=True))

            s = jnp.where(causal(), raw(high - 1), NEGATIVE)
            scores[chunk_of(high - 1 - low), :] = s
            top = lax.fori_loop(low, high - 1, first, jnp.max(s, axis=0, keepdims=True))

            def second(kc, total):
                e = jnp.exp(scores[chunk_of(kc), :] - top)
                scores[chunk_of(kc), :] = e
                return total + jnp.sum(e, axis=0, keepdims=True)

            total = lax.fori_loop(0, high - low, second, jnp.zeros((1, CHUNK), F32))
            inverse = 1.0 / total

            def third(kc, mixed):
                probs = (scores[chunk_of(kc), :] * inverse).astype(BF16)
                return mixed + jnp.dot(
                    v_flat[:, chunk_of(kc + low)], probs, preferred_element_type=F32
                )

            mixed = lax.fori_loop(0, high - low, third, jnp.zeros((HD, CHUNK), F32))
            mixed = mixed.astype(BF16)
            for part in range(CHUNK // BLOCK):
                heads_out[head_rows(h), lanes_of(step * (CHUNK // BLOCK) + part, rank)] = mixed[
                    :, part * BLOCK : (part + 1) * BLOCK
                ]
            lse_out[pl.ds(h, 1), chunk_of(step)] = top + jnp.log(total)
            last = step == SLOT_LEN // CHUNK - 1
            start = jnp.where(last, 0, LEAD + step * CHUNK)
            alive = jnp.where(last, info[2], info[1])
            spots = lax.broadcasted_iota(jnp.int32, (1, CHUNK), 1) + start
            best = jnp.max(jnp.where(spots < alive, top, NEGATIVE), axis=1, keepdims=True)
            peak_out[pl.ds(h, 1), :] = jnp.maximum(peak_out[pl.ds(h, 1), :], best)


def attend_back_kernel(
    info, qkv, halo, upstream, lse, cos, sin, dq_out, dkv_out, halo_out,
    k_up, v_up, k_flat, probs_s, grads_s, dk_s, dv_s, up_abs,
):
    rank = info[0]
    k_up[pl.ds(0, LEAD), :] = upright(halo[pl.ds(0, HD), :])
    v_up[pl.ds(0, LEAD), :] = upright(halo[pl.ds(HD, HD), :])
    k_flat[:, pl.ds(0, LEAD)] = halo[pl.ds(0, HD), :]
    k_flat[:, pl.ds(LEAD, SLOT_LEN)] = qkv[pl.ds(K_AT, HD), :]

    @pl.loop(0, SLOT_LEN // CHUNK)
    def _(i):
        rows = pl.ds(pl.multiple_of(LEAD + i * CHUNK, CHUNK), CHUNK)
        k_up[rows, :] = upright(qkv[pl.ds(K_AT, HD), chunk_of(i)])
        v_up[rows, :] = upright(qkv[pl.ds(V_AT, HD), chunk_of(i)])

    @pl.loop(0, SLOT_LEN // BLOCK)
    def _(block):
        target = pl.ds(pl.multiple_of(block * BLOCK, BLOCK), BLOCK)
        up_abs[:, target] = upstream[:, lanes_of(block, rank)]

    dk_s[...] = jnp.zeros(dk_s.shape, F32)
    dv_s[...] = jnp.zeros(dv_s.shape, F32)

    @pl.loop(0, HEADS)
    def _(h):
        @pl.loop(0, SLOT_LEN // CHUNK)
        def _(step):
            low, high = key_range(step)
            here = chunk_of(step)
            query = qkv[head_rows(h), here]
            grad = up_abs[head_rows(h), here]
            query_up, grad_up = upright(query), upright(grad)
            logs = lse[pl.ds(h, 1), here]

            def one(kc, masked):
                s = jnp.dot(k_up[chunk_of(kc), :], query, preferred_element_type=F32)
                p = jnp.exp(s - logs)
                if masked:
                    p = jnp.where(causal(), p, 0.0)
                g = jnp.dot(v_up[chunk_of(kc), :], grad, preferred_element_type=F32)
                probs_s[chunk_of(kc - low), :] = p
                grads_s[chunk_of(kc - low), :] = g
                dv_s[chunk_of(kc), :] += jnp.dot(
                    p.astype(BF16), grad_up, preferred_element_type=F32
                )
                return jnp.sum(p * g, axis=0, keepdims=True)

            delta = one(high - 1, True)
            delta = lax.fori_loop(low, high - 1, lambda kc, d: d + one(kc, False), delta)

            def two(kc, dq):
                p, g = probs_s[chunk_of(kc - low), :], grads_s[chunk_of(kc - low), :]
                ds = (p * (g - delta)).astype(BF16)
                dk_s[chunk_of(kc), :] += jnp.dot(ds, query_up, preferred_element_type=F32)
                return dq + jnp.dot(k_flat[:, chunk_of(kc)], ds, preferred_element_type=F32)

            dq = lax.fori_loop(low, high, two, jnp.zeros((HD, CHUNK), F32)) * MULTIPLIER
            c, s = cos[:, here], sin[:, here]
            u1, u2 = dq[:HALF], dq[HALF:]
            t1, t2 = (u1 * c + u2 * s).astype(BF16), (u2 * c - u1 * s).astype(BF16)
            for part in range(CHUNK // BLOCK):
                there = lanes_of(step * (CHUNK // BLOCK) + part, rank)
                cut = slice(part * BLOCK, (part + 1) * BLOCK)
                dq_out[pl.ds(pl.multiple_of(h * HD, HD), HALF), there] = t1[:, cut]
                dq_out[pl.ds(pl.multiple_of(h * HD + HALF, HALF), HALF), there] = t2[:, cut]

    halo_out[pl.ds(0, HD), :] = dk_s[pl.ds(0, LEAD), :].T.astype(BF16)
    halo_out[pl.ds(HD, HD), :] = dv_s[pl.ds(0, LEAD), :].T.astype(BF16)

    @pl.loop(0, SLOT_LEN // CHUNK)
    def _(i):
        rows = pl.ds(pl.multiple_of(LEAD + i * CHUNK, CHUNK), CHUNK)
        dkv_out[pl.ds(0, HD), chunk_of(i)] = dk_s[rows, :].T
        dkv_out[pl.ds(HD, HD), chunk_of(i)] = dv_s[rows, :].T


def finish_kernel(info, dkv, halo, cos, sin, out):
    rank = info[0]
    owned = (SLOT_LEN - LEAD) // BLOCK
    for block in range(SLOT_LEN // BLOCK):
        source = pl.ds(block * BLOCK, BLOCK)
        target = lanes_of(block, rank)
        c, s = cos[:, source], sin[:, source]
        u1, u2 = dkv[pl.ds(0, HALF), source], dkv[pl.ds(HALF, HALF), source]
        rest = dkv[pl.ds(HD, HD), source]
        if block >= owned:
            part = pl.ds((block - owned) * BLOCK, BLOCK)
            u1 = u1 + halo[pl.ds(0, HALF), part].astype(F32)
            u2 = u2 + halo[pl.ds(HALF, HALF), part].astype(F32)
            rest = rest + halo[pl.ds(HD, HD), part].astype(F32)
        out[pl.ds(0, HALF), target] = (u1 * c + u2 * s).astype(BF16)
        out[pl.ds(HALF, HALF), target] = (u2 * c - u1 * s).astype(BF16)
        out[pl.ds(HD, HD), target] = rest.astype(BF16)


def call(kernel, info, args, outs, scratch, flops, name):
    moved = sum(a.size * a.dtype.itemsize for a in args)
    moved += sum(int(np.prod(s)) * np.dtype(d).itemsize for s, d in outs)
    spec = pl.BlockSpec(memory_space=pltpu.VMEM)
    return pl.pallas_call(
        kernel,
        out_shape=[jax.ShapeDtypeStruct(s, d) for s, d in outs],
        in_specs=[pl.BlockSpec(memory_space=pltpu.SMEM)] + [spec] * len(args),
        out_specs=[spec] * len(outs),
        scratch_shapes=[pltpu.VMEM(s, d) for s, d in scratch],
        compiler_params=pltpu.CompilerParams(vmem_limit_bytes=40 * 2**20),
        cost_estimate=pl.CostEstimate(flops=flops, bytes_accessed=moved, transcendentals=0),
        name=name,
    )(info, *args)


def norm_back(values, scale, upstream):
    mean_term = jnp.mean(values * upstream, axis=1, keepdims=True)
    return scale * upstream - values * (scale * scale * scale) * mean_term


def shards(
    layer_in, lengths, clip_level, attn_gain, w_query, w_key, w_value, w_out,
    mlp_gain, w_gate, w_up, w_down, cotangent,
):
    tok_rows, width = layer_in.shape
    z_rank, y_rank = lax.axis_index("z"), lax.axis_index("y")
    rank = (y_rank * 2 + lax.axis_index("x")) * 2 + lax.axis_index("c")
    slots = lengths.shape[0]
    next_slot = (z_rank + 1) % slots
    info = jnp.stack(
        (rank, lax.dynamic_index_in_dim(lengths, z_rank, keepdims=False),
         lax.dynamic_index_in_dim(lengths, next_slot, keepdims=False))
    ).astype(jnp.int32)
    inner = rank * tok_rows + jnp.arange(tok_rows, dtype=jnp.int32) + LEAD
    own_mask = jnp.where(inner < SLOT_LEN, inner < info[1], inner - SLOT_LEN < info[2])
    own_mask = own_mask.astype(F32)[:, None]
    spots = ((jnp.arange(SLOT_LEN, dtype=jnp.int32) + LEAD) % SLOT_LEN).astype(F32)
    freq = THETA ** (-(jnp.arange(HALF, dtype=F32) * 2.0 / HD))
    angles = spots[None, :] * freq[:, None]
    cos, sin = jnp.cos(angles), jnp.sin(angles)
    q_half = w_query.shape[1] // 2

    def heads_part(which):
        return jnp.concatenate(
            (half_of(w_query, which, 1), half_of(w_key, which, 1), half_of(w_value, which, 1)), 1
        )

    other_y = 1 - y_rank
    qkv_part = ordered(heads_part(y_rank), swap(heads_part(other_y), "y"), y_rank, 0)
    out_part = ordered(half_of(w_out, y_rank, 0), swap(half_of(w_out, other_y, 0), "y"), y_rank, 1)
    down_part = ordered(half_of(w_down, y_rank, 0), swap(half_of(w_down, other_y, 0), "y"), y_rank, 1)
    gate_part = ordered(half_of(w_gate, y_rank, 1), swap(half_of(w_gate, other_y, 1), "y"), y_rank, 0)
    up_part = ordered(half_of(w_up, y_rank, 1), swap(half_of(w_up, other_y, 1), "y"), y_rank, 0)
    full_qkv = lax.all_gather(qkv_part, "z", axis=0, tiled=True)
    full_out = lax.all_gather(out_part, "z", axis=1, tiled=True)
    full_down = lax.all_gather(down_part, "z", axis=1, tiled=True)
    full_gate = lax.all_gather(gate_part, "z", axis=0, tiled=True)
    full_up = lax.all_gather(up_part, "z", axis=0, tiled=True)

    layer_f = layer_in.astype(F32)
    scale_one = lax.rsqrt(jnp.mean(layer_f * layer_f, axis=1, keepdims=True) + EPSILON)
    normal_one = (layer_f * scale_one).astype(BF16)
    gain_one = attn_gain.astype(F32)
    acts_one = gather_rows((normal_one.astype(F32) * gain_one[None, :]).astype(BF16))
    grad_out = cotangent.astype(F32)
    down_rows = gather_rows((RESIDUAL * own_mask * grad_out).astype(BF16))

    rows = acts_one.shape[0]
    half_rows = rows // 2
    flat = dot(full_qkv, acts_one, 0, 1)
    (qkv,) = call(
        rope_kernel, info, (flat, cos, sin), [((flat.shape[0], rows), BF16)], [],
        4 * flat.size, "rope",
    )
    halo = along(qkv[K_AT:, SLOT_LEN - LEAD :], 1)
    work = 2 * HEADS * HD * 10 * CHUNK * CHUNK * 4
    heads, lse, peak = call(
        attend_kernel, info, (qkv, halo),
        [((HEADS * HD, rows), BF16), ((8, rows), F32), ((8, 128), F32)],
        [((KEYS, HD), BF16), ((HD, KEYS), BF16), ((SLOT_LEN, CHUNK), F32)],
        4 * work, "attend",
    )
    branch_one = scatter_rows(
        lambda: dot(heads[:, :half_rows], full_out, 0, 0),
        lambda: dot(heads[:, half_rows:], full_out, 0, 0),
    )
    resid = layer_f + RESIDUAL * own_mask * branch_one
    scale_two = lax.rsqrt(jnp.mean(resid * resid, axis=1, keepdims=True) + EPSILON)
    normal_two = (resid * scale_two).astype(BF16)
    gain_two = mlp_gain.astype(F32)
    acts_two = gather_rows((normal_two.astype(F32) * gain_two[None, :]).astype(BF16))

    hidden_grad = dot(down_rows, full_down, 1, 1)
    gate_proj = dot(acts_two, full_gate, 1, 0)
    up_proj = dot(acts_two, full_up, 1, 0)
    sigmoid_gate = jax.nn.sigmoid(gate_proj)
    hidden = (gate_proj * sigmoid_gate * up_proj).astype(BF16)
    gate_grad = (
        hidden_grad * up_proj * sigmoid_gate * (1.0 + gate_proj * (1.0 - sigmoid_gate))
    ).astype(BF16)
    up_grad = (hidden_grad * gate_proj * sigmoid_gate).astype(BF16)

    def reduced(grad, axis):
        return lax.psum_scatter(grad.astype(BF16), "z", scatter_dimension=axis, tiled=True)

    down_sum = reduced(dot(hidden, down_rows, 0, 0), 1)
    gate_sum = reduced(dot(acts_two, gate_grad, 0, 0), 0)
    up_sum = reduced(dot(acts_two, up_grad, 0, 0), 0)

    def acts_two_back(part):
        return dot(gate_grad[part], full_gate, 1, 1) + dot(up_grad[part], full_up, 1, 1)

    norm_two_grad = scatter_rows(
        lambda: acts_two_back(slice(None, half_rows)), lambda: acts_two_back(slice(half_rows, None))
    )
    gain_two_part = jnp.sum(normal_two.astype(F32) * norm_two_grad, axis=0)
    grad_resid = grad_out + norm_back(resid, scale_two, gain_two[None, :] * norm_two_grad)
    mixed_rows = gather_rows((RESIDUAL * own_mask * grad_resid).astype(BF16))
    branch_two = scatter_rows(
        lambda: dot(hidden[:half_rows], full_down, 1, 0),
        lambda: dot(hidden[half_rows:], full_down, 1, 0),
    )
    result = resid + RESIDUAL * own_mask * branch_two

    heads_grad = dot(full_out, mixed_rows, 1, 1).astype(BF16)
    dq, dkv, back = call(
        attend_back_kernel, info, (qkv, halo, heads_grad, lse, cos, sin),
        [((HEADS * HD, rows), BF16), ((2 * HD, rows), F32), ((2 * HD, LEAD), BF16)],
        [((KEYS, HD), BF16), ((KEYS, HD), BF16), ((HD, KEYS), BF16),
         ((SLOT_LEN, CHUNK), F32), ((SLOT_LEN, CHUNK), F32),
         ((KEYS, HD), F32), ((KEYS, HD), F32), ((HEADS * HD, SLOT_LEN), BF16)],
        10 * work, "attend_back",
    )
    (dkv_done,) = call(
        finish_kernel, info, (dkv, along(back, -1), cos, sin), [((2 * HD, rows), BF16)], [],
        4 * dkv.size, "finish",
    )
    dqkv = jnp.concatenate((dq, dkv_done))
    out_sum = reduced(dot(heads, mixed_rows, 1, 0), 1)
    qkv_sum = reduced(dot(acts_one, dqkv, 0, 1), 0)
    norm_one_grad = scatter_rows(
        lambda: dot(dqkv[:, :half_rows], full_qkv, 0, 1),
        lambda: dot(dqkv[:, half_rows:], full_qkv, 0, 1),
    )
    gain_one_part = jnp.sum(normal_one.astype(F32) * norm_one_grad, axis=0)
    grad_input = grad_resid + norm_back(layer_f, scale_one, gain_one[None, :] * norm_one_grad)

    def owned_rows(total):
        return half_of(total, y_rank, 0), swap(half_of(total, other_y, 0), "y")

    def owned_cols(total):
        return half_of(total, y_rank, 1), swap(half_of(total, other_y, 1), "y")

    down_grad = ordered(*owned_cols(down_sum), y_rank, 0).astype(F32)
    gate_w_grad = ordered(*owned_rows(gate_sum), y_rank, 1).astype(F32)
    up_w_grad = ordered(*owned_rows(up_sum), y_rank, 1).astype(F32)
    out_grad = ordered(*owned_cols(out_sum), y_rank, 0).astype(F32)
    own, other = owned_rows(qkv_sum)

    def columns(start, stop):
        return ordered(own[:, start:stop], other[:, start:stop], y_rank, 1).astype(F32)

    query_grad = columns(0, K_AT)
    key_grad = columns(K_AT, V_AT)
    value_grad = columns(V_AT, V_AT + HD)

    gains = jnp.stack((gain_one_part, gain_two_part))
    devices = lax.axis_size(EVERY)
    gains = lax.psum_scatter(
        gains.reshape(2, devices, -1).transpose(1, 0, 2), EVERY, scatter_dimension=0, tiled=True
    )[0]

    local = peak[:HEADS, 0]
    empty = jnp.full((HEADS,), NEGATIVE, F32)
    head_peak = lax.pmax(ordered(local, empty, y_rank, 0), ("z", "y"))
    level = clip_level[0].astype(F32) * LEVEL_UNIT
    factor = level / jnp.maximum(level, head_peak)
    query_clipped = w_query.astype(F32) * jnp.repeat(jnp.sqrt(factor), HD)[None, :]
    kv_factor = jnp.min(factor.reshape(-1, HEADS), axis=1)
    key_clipped = w_key.astype(F32) * jnp.repeat(jnp.sqrt(kv_factor), HD)[None, :]
    return (
        result.astype(BF16),
        grad_input.astype(BF16),
        gains[0],
        query_grad,
        key_grad,
        value_grad,
        out_grad,
        gains[1],
        gate_w_grad,
        up_w_grad,
        down_grad,
        query_clipped,
        key_clipped,
    )


def solution(mesh):
    fsdp, tp = mesh.shape["fsdp"], mesh.shape["tp"]
    fine = Mesh(mesh.devices.reshape(fsdp // 2, 2, tp // 2, 2), EVERY)
    rows, cols = ("z", "y"), ("x", "c")
    tokens, down, across = P(EVERY, None), P(rows, cols), P(cols, rows)
    in_specs = (
        tokens, P(), P(), P(), down, down, down, across, P(), down, down, across, tokens,
    )
    out_specs = (
        tokens, tokens, P(EVERY), down, down, down, across, P(EVERY), down, down, across,
        down, down,
    )
    return jax.shard_map(shards, mesh=fine, in_specs=in_specs, out_specs=out_specs, check_vma=False)
```

```python
import jax
import jax.numpy as jnp
from jax import lax
from jax.experimental import pallas as pl
from jax.experimental.pallas import tpu as pltpu
from jax.sharding import Mesh
from jax.sharding import PartitionSpec as P

HD = 64
HALF = HD // 2
SLOT_LEN = 2048
LEAD = 512
CHUNK = 512
BLOCK = 256
HEADS = 4

EPSILON = 1e-05
THETA = 10000000.0
MULTIPLIER = 0.015625
RESIDUAL = 0.22
LEVEL_UNIT = 0.125
NEGATIVE = -1e30
GROUP = ("y", "x", "c")
EVERY = ("z", "y", "x", "c")
F32 = jnp.float32
BF16 = jnp.bfloat16


def rounded(x):
    return lax.reduce_precision(x, exponent_bits=8, mantissa_bits=7)


def swap(x, axis):
    return lax.ppermute(x, axis, [(0, 1), (1, 0)])


def along(x, by):
    peers = lax.axis_size("z")
    return lax.ppermute(x, "z", [(i, (i + by) % peers) for i in range(peers)])


def dot(left, right, left_dim, right_dim):
    return lax.dot_general(
        left, right, (((left_dim,), (right_dim,)), ((), ())), preferred_element_type=F32
    )


def half_of(x, which, axis):
    size = x.shape[axis] // 2
    return lax.dynamic_slice_in_dim(x, which * size, size, axis)


def ordered(own, other, rank, axis):
    return jnp.where(
        rank == 0,
        jnp.concatenate((own, other), axis=axis),
        jnp.concatenate((other, own), axis=axis),
    )


def after(x, *others):
    return lax.optimization_barrier((x, *others))[0]


def tie(*xs):
    return lax.optimization_barrier(xs)


def gather_one(v):
    half = v.shape[0] // 2
    return v, swap(v, "c"), swap(v[:half], "x"), swap(v[half:], "y")


def gather_two(state):
    v, near, a01, b10 = state
    half = v.shape[0] // 2
    a1 = swap(jnp.concatenate((v[:half], a01)), "y")
    b1 = swap(jnp.concatenate((v[half:], b10)), "x")
    second = swap(jnp.concatenate((a01, b10)), "c")
    return v, near, a01, b10, second, a1, b1


def gather_three(state):
    v, near, a01, b10, second, a1, b1 = state
    half = v.shape[0] // 2
    third = swap(jnp.concatenate((a1, b1)), "c")

    def block(own, one, two):
        return (own, one[:half], two[2 * half : 3 * half], two[:half], one[half:],
                two[half : 2 * half], two[3 * half :])

    own = (v, a01, b1[:half], a1[:half], b10, a1[half:], b1[half:])
    return jnp.concatenate(own + block(near, second, third))


def fold_rows(low, high):
    return low() + swap(high().astype(BF16), "c").astype(F32)


def spread_one(total):
    rows, cols = total.shape[0] // 4, total.shape[1] // 2
    blocks = total.reshape(2, 2, rows, 2 * cols)
    left, right = blocks[..., :cols], blocks[..., cols:]
    send_x, send_y = left[:, 1].astype(BF16), right[1].astype(BF16)
    return left[:, 0], right[0], swap(send_x, "x"), swap(send_y, "y"), (send_x, send_y)


def spread_two(state):
    left, right, left_x, right_y = state[:4]
    left = left + left_x.astype(F32)
    right = right + right_y.astype(F32)
    send_y, send_x = left[1].astype(BF16), right[1].astype(BF16)
    return left[0], right[0], swap(send_y, "y"), swap(send_x, "x"), (send_x, send_y)


def spread_three(state):
    left, right, left_y, right_x = state[:4]
    return jnp.concatenate((left + left_y.astype(F32), right + right_x.astype(F32)), axis=1)


def over_z(x, combine):
    peers, step = lax.axis_size("z"), 1
    assert peers & (peers - 1) == 0
    while step < peers:
        x = combine(x, along(x, step))
        step *= 2
    return x


def place_of(block, rank):
    j = jnp.bitwise_xor(block, rank)
    return jnp.bitwise_or(jnp.left_shift(jnp.bitwise_and(j, 1), 2), jnp.right_shift(j, 1))


def lanes_of(block, rank):
    return pl.ds(pl.multiple_of(place_of(block, rank) * BLOCK, BLOCK), BLOCK)


def rope_kernel(info, qkv, cos, sin, out):
    rank = info[0]

    @pl.loop(0, SLOT_LEN // BLOCK)
    def _(block):
        source = lanes_of(block, rank)
        target = pl.ds(pl.multiple_of(block * BLOCK, BLOCK), BLOCK)
        c, s = cos[:, target], sin[:, target]
        for head in range(HEADS + 1):
            first = qkv[pl.ds(head * HD, HALF), source]
            second = qkv[pl.ds(head * HD + HALF, HALF), source]
            scale = MULTIPLIER if head < HEADS else 1.0
            out[pl.ds(head * HD, HALF), target] = ((first * c - second * s).astype(BF16) * scale).astype(BF16)
            out[pl.ds(head * HD + HALF, HALF), target] = ((second * c + first * s).astype(BF16) * scale).astype(BF16)
        rest = (HEADS + 1) * HD
        out[pl.ds(rest, HD), target] = qkv[pl.ds(rest, HD), source].astype(BF16)


KEYS = SLOT_LEN + LEAD
K_AT = HEADS * HD
V_AT = K_AT + HD


def upright(x):
    return x.astype(F32).T.astype(BF16)


def causal():
    keys = lax.broadcasted_iota(jnp.int32, (CHUNK, CHUNK), 0)
    queries = lax.broadcasted_iota(jnp.int32, (CHUNK, CHUNK), 1)
    return keys <= queries


def key_range(step):
    last = step == SLOT_LEN // CHUNK - 1
    low = jnp.where(last, KEYS // CHUNK - 1, 0)
    high = jnp.where(last, KEYS // CHUNK, step + 2)
    return low, high


def chunk_of(i):
    return pl.ds(pl.multiple_of(i * CHUNK, CHUNK), CHUNK)


def head_rows(h):
    return pl.ds(pl.multiple_of(h * HD, HD), HD)


def attend_kernel(info, qkv, halo, heads_out, lse_out, peak_out, k_up, v_flat, scores):
    rank = info[0]
    k_up[pl.ds(0, LEAD), :] = upright(halo[pl.ds(0, HD), :])
    v_flat[:, pl.ds(0, LEAD)] = halo[pl.ds(HD, HD), :]
    v_flat[:, pl.ds(LEAD, SLOT_LEN)] = qkv[pl.ds(V_AT, HD), :]

    @pl.loop(0, SLOT_LEN // CHUNK)
    def _(i):
        k_up[pl.ds(pl.multiple_of(LEAD + i * CHUNK, CHUNK), CHUNK), :] = upright(
            qkv[pl.ds(K_AT, HD), chunk_of(i)]
        )

    peak_out[...] = jnp.full(peak_out.shape, NEGATIVE, F32)
    lse_out[...] = jnp.zeros(lse_out.shape, F32)

    @pl.loop(0, HEADS)
    def _(h):
        @pl.loop(0, SLOT_LEN // CHUNK)
        def _(step):
            low, high = key_range(step)
            query = qkv[head_rows(h), chunk_of(step)]

            def raw(kc):
                return jnp.dot(k_up[chunk_of(kc), :], query, preferred_element_type=F32)

            def first(kc, top):
                s = raw(kc)
                scores[chunk_of(kc - low), :] = s
                return jnp.maximum(top, jnp.max(s, axis=0, keepdims=True))

            s = jnp.where(causal(), raw(high - 1), NEGATIVE)
            scores[chunk_of(high - 1 - low), :] = s
            top = lax.fori_loop(low, high - 1, first, jnp.max(s, axis=0, keepdims=True))

            def second(kc, total):
                e = jnp.exp(scores[chunk_of(kc), :] - top)
                scores[chunk_of(kc), :] = e
                return total + jnp.sum(e, axis=0, keepdims=True)

            total = lax.fori_loop(0, high - low, second, jnp.zeros((1, CHUNK), F32))
            inverse = 1.0 / total

            def third(kc, mixed):
                probs = (scores[chunk_of(kc), :] * inverse).astype(BF16)
                return mixed + jnp.dot(
                    v_flat[:, chunk_of(kc + low)], probs, preferred_element_type=F32
                )

            mixed = lax.fori_loop(0, high - low, third, jnp.zeros((HD, CHUNK), F32))
            mixed = mixed.astype(BF16)
            for part in range(CHUNK // BLOCK):
                heads_out[head_rows(h), lanes_of(step * (CHUNK // BLOCK) + part, rank)] = mixed[
                    :, part * BLOCK : (part + 1) * BLOCK
                ]
            lse_out[pl.ds(h, 1), chunk_of(step)] = top + jnp.log(total)
            last = step == SLOT_LEN // CHUNK - 1
            start = jnp.where(last, 0, LEAD + step * CHUNK)
            alive = jnp.where(last, info[2], info[1])
            spots = lax.broadcasted_iota(jnp.int32, (1, CHUNK), 1) + start
            best = jnp.max(jnp.where(spots < alive, top, NEGATIVE), axis=1, keepdims=True)
            peak_out[pl.ds(h, 1), :] = jnp.maximum(peak_out[pl.ds(h, 1), :], best)


def attend_back_kernel(
    info, qkv, halo, upstream, lse, cos, sin, dq_out, dkv_out, halo_out,
    k_up, v_up, k_flat, probs_s, grads_s, dk_s, dv_s, up_abs,
):
    rank = info[0]
    k_up[pl.ds(0, LEAD), :] = upright(halo[pl.ds(0, HD), :])
    v_up[pl.ds(0, LEAD), :] = upright(halo[pl.ds(HD, HD), :])
    k_flat[:, pl.ds(0, LEAD)] = halo[pl.ds(0, HD), :]
    k_flat[:, pl.ds(LEAD, SLOT_LEN)] = qkv[pl.ds(K_AT, HD), :]

    @pl.loop(0, SLOT_LEN // CHUNK)
    def _(i):
        rows = pl.ds(pl.multiple_of(LEAD + i * CHUNK, CHUNK), CHUNK)
        k_up[rows, :] = upright(qkv[pl.ds(K_AT, HD), chunk_of(i)])
        v_up[rows, :] = upright(qkv[pl.ds(V_AT, HD), chunk_of(i)])

    @pl.loop(0, SLOT_LEN // BLOCK)
    def _(block):
        target = pl.ds(pl.multiple_of(block * BLOCK, BLOCK), BLOCK)
        up_abs[:, target] = upstream[:, lanes_of(block, rank)]

    dk_s[...] = jnp.zeros(dk_s.shape, F32)
    dv_s[...] = jnp.zeros(dv_s.shape, F32)

    @pl.loop(0, HEADS)
    def _(h):
        @pl.loop(0, SLOT_LEN // CHUNK)
        def _(step):
            low, high = key_range(step)
            here = chunk_of(step)
            query = qkv[head_rows(h), here]
            grad = up_abs[head_rows(h), here]
            query_up, grad_up = upright(query), upright(grad)
            logs = lse[pl.ds(h, 1), here]

            def one(kc, masked):
                s = jnp.dot(k_up[chunk_of(kc), :], query, preferred_element_type=F32)
                p = jnp.exp(s - logs)
                if masked:
                    p = jnp.where(causal(), p, 0.0)
                g = jnp.dot(v_up[chunk_of(kc), :], grad, preferred_element_type=F32)
                probs_s[chunk_of(kc - low), :] = p
                grads_s[chunk_of(kc - low), :] = g
                dv_s[chunk_of(kc), :] += jnp.dot(
                    p.astype(BF16), grad_up, preferred_element_type=F32
                )
                return jnp.sum(p * g, axis=0, keepdims=True)

            delta = one(high - 1, True)
            delta = lax.fori_loop(low, high - 1, lambda kc, d: d + one(kc, False), delta)

            def two(kc, dq):
                p, g = probs_s[chunk_of(kc - low), :], grads_s[chunk_of(kc - low), :]
                ds = (p * (g - delta)).astype(BF16)
                dk_s[chunk_of(kc), :] += jnp.dot(ds, query_up, preferred_element_type=F32)
                return dq + jnp.dot(k_flat[:, chunk_of(kc)], ds, preferred_element_type=F32)

            dq = lax.fori_loop(low, high, two, jnp.zeros((HD, CHUNK), F32)) * MULTIPLIER
            c, s = cos[:, here], sin[:, here]
            u1, u2 = dq[:HALF], dq[HALF:]
            t1, t2 = (u1 * c + u2 * s).astype(BF16), (u2 * c - u1 * s).astype(BF16)
            for part in range(CHUNK // BLOCK):
                there = lanes_of(step * (CHUNK // BLOCK) + part, rank)
                cut = slice(part * BLOCK, (part + 1) * BLOCK)
                dq_out[pl.ds(pl.multiple_of(h * HD, HD), HALF), there] = t1[:, cut]
                dq_out[pl.ds(pl.multiple_of(h * HD + HALF, HALF), HALF), there] = t2[:, cut]

    halo_out[pl.ds(0, HD), :] = dk_s[pl.ds(0, LEAD), :].T.astype(BF16)
    halo_out[pl.ds(HD, HD), :] = dv_s[pl.ds(0, LEAD), :].T.astype(BF16)

    @pl.loop(0, SLOT_LEN // CHUNK)
    def _(i):
        rows = pl.ds(pl.multiple_of(LEAD + i * CHUNK, CHUNK), CHUNK)
        dkv_out[pl.ds(0, HD), chunk_of(i)] = dk_s[rows, :].T
        dkv_out[pl.ds(HD, HD), chunk_of(i)] = dv_s[rows, :].T


def finish_kernel(info, dkv, halo, cos, sin, out):
    rank = info[0]
    owned = (SLOT_LEN - LEAD) // BLOCK
    for block in range(SLOT_LEN // BLOCK):
        source = pl.ds(block * BLOCK, BLOCK)
        target = lanes_of(block, rank)
        c, s = cos[:, source], sin[:, source]
        u1, u2 = dkv[pl.ds(0, HALF), source], dkv[pl.ds(HALF, HALF), source]
        rest = dkv[pl.ds(HD, HD), source]
        if block >= owned:
            part = pl.ds((block - owned) * BLOCK, BLOCK)
            u1 = u1 + halo[pl.ds(0, HALF), part].astype(F32)
            u2 = u2 + halo[pl.ds(HALF, HALF), part].astype(F32)
            rest = rest + halo[pl.ds(HD, HD), part].astype(F32)
        out[pl.ds(0, HALF), target] = (u1 * c + u2 * s).astype(BF16)
        out[pl.ds(HALF, HALF), target] = (u2 * c - u1 * s).astype(BF16)
        out[pl.ds(HD, HD), target] = rest.astype(BF16)


def call(kernel, info, args, outs, scratch, name):
    spec = pl.BlockSpec(memory_space=pltpu.VMEM)
    return pl.pallas_call(
        kernel,
        out_shape=[jax.ShapeDtypeStruct(s, d) for s, d in outs],
        in_specs=[pl.BlockSpec(memory_space=pltpu.SMEM)] + [spec] * len(args),
        out_specs=[spec] * len(outs),
        scratch_shapes=[pltpu.VMEM(s, d) for s, d in scratch],
        compiler_params=pltpu.CompilerParams(vmem_limit_bytes=40 * 2**20),
        cost_estimate=pl.CostEstimate(flops=0, bytes_accessed=0, transcendentals=0),
        name=name,
    )(info, *args)


def norm_back(values, scale, upstream):
    mean_term = jnp.mean(values * upstream, axis=1, keepdims=True)
    return scale * upstream - values * (scale * scale * scale) * mean_term


def shards(
    layer_in, lengths, clip_level, attn_gain, w_query, w_key, w_value, w_out,
    mlp_gain, w_gate, w_up, w_down, cotangent,
):
    tok_rows, width = layer_in.shape
    z_rank, y_rank = lax.axis_index("z"), lax.axis_index("y")
    rank = (y_rank * 2 + lax.axis_index("x")) * 2 + lax.axis_index("c")
    slots = lengths.shape[0]
    next_slot = (z_rank + 1) % slots
    info = jnp.stack(
        (rank, lax.dynamic_index_in_dim(lengths, z_rank, keepdims=False),
         lax.dynamic_index_in_dim(lengths, next_slot, keepdims=False))
    ).astype(jnp.int32)
    inner = rank * tok_rows + jnp.arange(tok_rows, dtype=jnp.int32) + LEAD
    own_mask = jnp.where(inner < SLOT_LEN, inner < info[1], inner - SLOT_LEN < info[2])
    own_mask = own_mask.astype(F32)[:, None]
    spots = ((jnp.arange(SLOT_LEN, dtype=jnp.int32) + LEAD) % SLOT_LEN).astype(F32)
    freq = THETA ** (-(jnp.arange(HALF, dtype=F32) * 2.0 / HD))
    angles = spots[None, :] * freq[:, None]
    cos, sin = jnp.cos(angles), jnp.sin(angles)
    def heads_part(which):
        return jnp.concatenate(
            (half_of(w_query, which, 1), half_of(w_key, which, 1), half_of(w_value, which, 1),
             half_of(w_out, which, 0).T), 1
        )

    other_y = 1 - y_rank
    heads_w = ordered(heads_part(y_rank), swap(heads_part(other_y), "y"), y_rank, 0)
    full_heads = lax.all_gather(heads_w, "z", axis=0, tiled=True)
    qkv_cols = V_AT + HD

    layer_f = layer_in.astype(F32)
    scale_one = lax.rsqrt(jnp.mean(layer_f * layer_f, axis=1, keepdims=True) + EPSILON)
    normal_one = rounded(layer_f * scale_one)
    gain_one = attn_gain.astype(F32)
    acts = gather_one(after((normal_one * gain_one[None, :]).astype(BF16), heads_w))
    acts = gather_two(acts)
    gate_other = swap(after(half_of(w_gate, other_y, 1), acts[2], acts[3]), "y")
    full_heads, *got = tie(full_heads, *acts[5:], gate_other)
    gate_other = got[2]
    full_qkv, full_out = full_heads[:, :qkv_cols], full_heads[:, qkv_cols:]
    acts_one = gather_three((*acts[:5], *got[:2]))
    gate_w = ordered(half_of(w_gate, y_rank, 1), gate_other, y_rank, 0)
    full_gate = lax.all_gather(gate_w, "z", axis=0, tiled=True)
    up_other = swap(after(half_of(w_up, other_y, 1), gate_w), "y")

    grad_out = cotangent.astype(F32)
    down_in = (RESIDUAL * own_mask * grad_out).astype(BF16)
    back_rows = gather_one(after(down_in, gate_w))
    rows = acts_one.shape[0]
    half_rows = rows // 2
    flat = dot(full_qkv, acts_one, 0, 1)
    (qkv,) = call(
        rope_kernel, info, (flat, cos, sin), [((flat.shape[0], rows), BF16)], [], "rope"
    )
    halo = along(qkv[K_AT:, SLOT_LEN - LEAD :], 1)
    qkv, halo, up_other, *back_rows = tie(qkv, halo, up_other, *back_rows)
    up_w = ordered(half_of(w_up, y_rank, 1), up_other, y_rank, 0)
    full_up = lax.all_gather(up_w, "z", axis=0, tiled=True)
    back_rows = gather_two(back_rows)
    down_other = swap(after(half_of(w_down, other_y, 0), back_rows[2], back_rows[3]), "y")
    heads, lse, peak = call(
        attend_kernel, info, (qkv, halo),
        [((HEADS * HD, rows), BF16), ((8, rows), F32), ((8, 128), F32)],
        [((KEYS, HD), BF16), ((HD, KEYS), BF16), ((SLOT_LEN, CHUNK), F32)],
        "attend",
    )
    heads, down_other, up_w, *back_rows = tie(heads, down_other, up_w, *back_rows)
    down_w = ordered(half_of(w_down, y_rank, 0), down_other, y_rank, 1)
    full_down = lax.all_gather(down_w, "z", axis=1, tiled=True)

    branch = fold_rows(
        lambda: dot(heads[:, :half_rows], full_out, 0, 1),
        lambda: dot(heads[:, half_rows:], full_out, 0, 1),
    )
    branch = spread_one(branch)
    down_rows = gather_three((*back_rows[:5], *after((back_rows[5], back_rows[6]), branch[4])))
    *got, down_rows, full_gate = tie(*branch[2:4], down_rows, full_gate)
    branch = spread_two((*branch[:2], *got))
    branch_one = spread_three(branch)
    resid = layer_f + RESIDUAL * own_mask * branch_one
    scale_two = lax.rsqrt(jnp.mean(resid * resid, axis=1, keepdims=True) + EPSILON)
    normal_two = rounded(resid * scale_two)
    gain_two = mlp_gain.astype(F32)
    acts = gather_two(gather_one((normal_two * gain_two[None, :]).astype(BF16)))
    acts_two = gather_three((*acts[:5], *after((acts[5], acts[6]), down_w)))
    acts_two, full_up = tie(acts_two, full_up)

    gate_proj = dot(acts_two, full_gate, 1, 0)
    up_proj = dot(acts_two, full_up, 1, 0)
    sigmoid_gate = jax.nn.sigmoid(gate_proj)
    hidden = (gate_proj * sigmoid_gate * up_proj).astype(BF16)

    def reduced(grad, axis):
        return lax.psum_scatter(grad, "z", scatter_dimension=axis, tiled=True)

    def traded(total, axis, *behind):
        total = after(total, *behind)
        return half_of(total, y_rank, axis), swap(half_of(total, other_y, axis), "y")

    down_part = dot(hidden, down_rows, 0, 0).astype(BF16)
    down_sum = reduced(down_part, 1)
    own_peak = jnp.max(after(peak, down_part)[:HEADS], axis=1, keepdims=True)
    own_peak = jnp.broadcast_to(own_peak, (HEADS, 128))
    head_peak = over_z(ordered(own_peak, swap(own_peak, "y"), y_rank, 0), jnp.maximum)
    down_rows, head_peak = tie(down_rows, head_peak)
    head_peak = head_peak[:, 0]
    hidden_grad = dot(down_rows, full_down, 1, 1)
    gate_grad = (
        hidden_grad * up_proj * sigmoid_gate * (1.0 + gate_proj * (1.0 - sigmoid_gate))
    ).astype(BF16)
    up_grad = (hidden_grad * gate_proj * sigmoid_gate).astype(BF16)

    def acts_two_back(part):
        return dot(gate_grad[part], full_gate, 1, 1) + dot(up_grad[part], full_up, 1, 1)

    norm_two = spread_one(
        fold_rows(
            lambda: acts_two_back(slice(None, half_rows)),
            lambda: acts_two_back(slice(half_rows, None)),
        )
    )
    held = after(acts_two, *norm_two[4])
    gate_part = dot(held, gate_grad, 0, 0).astype(BF16)
    up_part = dot(held, up_grad, 0, 0).astype(BF16)
    gate_sum, up_sum = reduced(gate_part, 0), reduced(up_part, 0)
    got = tie(*norm_two[2:4], gate_part, up_part)[:2]
    norm_two = spread_two((*norm_two[:2], *got))
    held = after(hidden, *norm_two[4])
    high_part = dot(held[half_rows:], full_down, 1, 0).astype(BF16)
    got = tie(*norm_two[2:4], high_part)[:2]
    norm_two_grad = spread_three((*norm_two[:2], *got))
    grad_resid = grad_out + norm_back(resid, scale_two, gain_two[None, :] * norm_two_grad)
    mixed = gather_one((RESIDUAL * own_mask * grad_resid).astype(BF16))
    held = after(hidden, mixed[0])
    folded = fold_rows(lambda: dot(held[:half_rows], full_down, 1, 0), lambda: high_part)
    gain_two_part = jnp.sum(normal_two * norm_two_grad, axis=0)
    got = tie(*mixed[2:4], folded, gain_two_part)
    folded, gain_two_part = got[2:]
    mixed = gather_two((*mixed[:2], *got[:2]))
    mixed_rows = gather_three(mixed)
    mixed_rows, down_sum, gate_sum = tie(mixed_rows, down_sum, gate_sum)
    second = spread_one(after(folded, mixed[5], mixed[6]))
    down_own, down_other = traded(down_sum, 1)
    gate_own, gate_other = traded(gate_sum, 0)

    heads_grad = dot(full_out, mixed_rows, 0, 1).astype(BF16)
    dq, dkv, back = call(
        attend_back_kernel, info, (qkv, halo, heads_grad, lse, cos, sin),
        [((HEADS * HD, rows), BF16), ((2 * HD, rows), F32), ((2 * HD, LEAD), BF16)],
        [((KEYS, HD), BF16), ((KEYS, HD), BF16), ((HD, KEYS), BF16),
         ((SLOT_LEN, CHUNK), F32), ((SLOT_LEN, CHUNK), F32),
         ((KEYS, HD), F32), ((KEYS, HD), F32), ((HEADS * HD, SLOT_LEN), BF16)],
        "attend_back",
    )
    back, down_other, gate_other, *got = tie(back, down_other, gate_other, *second[2:4])
    back_sent = along(back, -1)
    second = spread_two((*second[:2], *got))
    out_part = dot(after(mixed_rows, back), heads, 0, 1).astype(BF16)
    out_sum = reduced(out_part, 0)
    dkv, back_sent, out_part, up_sum = tie(dkv, back_sent, out_part, up_sum)
    up_own, up_other = traded(up_sum, 0)
    (dkv_done,) = call(
        finish_kernel, info, (dkv, back_sent, cos, sin), [((2 * HD, rows), BF16)], [], "finish"
    )
    dqkv = jnp.concatenate((dq, dkv_done))
    folded = fold_rows(
        lambda: dot(dqkv[:, :half_rows], full_qkv, 0, 1),
        lambda: dot(dqkv[:, half_rows:], full_qkv, 0, 1),
    )
    folded, up_other, *got = tie(folded, up_other, *second[2:4])
    branch_two = spread_three((*second[:2], *got))
    result = resid + RESIDUAL * own_mask * branch_two

    norm_one = spread_one(folded)
    part = dot(after(acts_one, *norm_one[4]), dqkv, 0, 1)
    gain_one_part = jnp.sum(part * full_qkv.astype(F32), axis=1) / gain_one
    qkv_part = part.astype(BF16)
    qkv_sum = reduced(qkv_part, 0)
    *got, gain_one_part = tie(*norm_one[2:4], gain_one_part, qkv_part)[:3]
    norm_one = spread_two((*norm_one[:2], *got))
    norm_one_grad = spread_three(norm_one)
    grad_input = grad_resid + norm_back(layer_f, scale_one, gain_one[None, :] * norm_one_grad)
    gain_one_part = after(gain_one_part, norm_one_grad)
    out_own, out_other = traded(out_sum, 0, norm_one_grad)
    own, other = traded(qkv_sum, 0, norm_one_grad)

    gains = jnp.stack((gain_one_part, gain_two_part))
    gains = gains.reshape(2, lax.axis_size("z"), 2, 2, 2, -1)
    for dim, axis in ((4, "c"), (3, "x"), (2, "y")):
        at = lax.axis_index(axis)
        other_at = lax.dynamic_index_in_dim(gains, 1 - at, dim, keepdims=False)
        gains = lax.dynamic_index_in_dim(gains, at, dim, keepdims=False) + swap(other_at, axis)
    gains = lax.dynamic_index_in_dim(over_z(gains, jnp.add), z_rank, 1, keepdims=False)

    down_grad = ordered(down_own, down_other, y_rank, 0).astype(F32)
    gate_w_grad = ordered(gate_own, gate_other, y_rank, 1).astype(F32)
    up_w_grad = ordered(up_own, up_other, y_rank, 1).astype(F32)
    out_grad = ordered(out_own.T, out_other.T, y_rank, 0).astype(F32)

    def columns(start, stop):
        return ordered(own[:, start:stop], other[:, start:stop], y_rank, 1).astype(F32)

    query_grad = columns(0, K_AT)
    key_grad = columns(K_AT, V_AT)
    value_grad = columns(V_AT, V_AT + HD)

    level = clip_level[0].astype(F32) * LEVEL_UNIT
    factor = level / jnp.maximum(level, head_peak)
    query_clipped = w_query.astype(F32) * jnp.repeat(jnp.sqrt(factor), HD)[None, :]
    kv_factor = jnp.min(factor.reshape(-1, HEADS), axis=1)
    key_clipped = w_key.astype(F32) * jnp.repeat(jnp.sqrt(kv_factor), HD)[None, :]
    return (
        result.astype(BF16),
        grad_input.astype(BF16),
        gains[0],
        query_grad,
        key_grad,
        value_grad,
        out_grad,
        gains[1],
        gate_w_grad,
        up_w_grad,
        down_grad,
        query_clipped,
        key_clipped,
    )


def solution(mesh):
    fsdp, tp = mesh.shape["fsdp"], mesh.shape["tp"]
    fine = Mesh(mesh.devices.reshape(fsdp // 2, 2, tp // 2, 2), EVERY)
    rows, cols = ("z", "y"), ("x", "c")
    tokens, down, across = P(EVERY, None), P(rows, cols), P(cols, rows)
    in_specs = (
        tokens, P(), P(), P(), down, down, down, across, P(), down, down, across, tokens,
    )
    out_specs = (
        tokens, tokens, P(EVERY), down, down, down, across, P(EVERY), down, down, across,
        down, down,
    )
    return jax.shard_map(shards, mesh=fine, in_specs=in_specs, out_specs=out_specs, check_vma=False)
```

```python
import functools

import jax
import jax.numpy as jnp
from jax import lax
from jax.experimental import pallas as pl
from jax.experimental.pallas import tpu as pltpu
from jax.sharding import Mesh
from jax.sharding import PartitionSpec as P

HD = 64
HALF = HD // 2
SLOT_LEN = 2048
LEAD = 512
CHUNK = 512
BLOCK = 256
HEADS = 4

EPSILON = 1e-05
THETA = 10000000.0
MULTIPLIER = 0.015625
RESIDUAL = 0.22
LEVEL_UNIT = 0.125
NEGATIVE = -1e30
GROUP = ("y", "x", "c")
EVERY = ("z", "y", "x", "c")
F32 = jnp.float32
BF16 = jnp.bfloat16
FREE = pl.CostEstimate(flops=0, bytes_accessed=0, transcendentals=0)


def rounded(x):
    return lax.reduce_precision(x, exponent_bits=8, mantissa_bits=7)


def swap(x, axis):
    return lax.ppermute(x, axis, [(0, 1), (1, 0)])


def along(x, by):
    peers = lax.axis_size("z")
    return lax.ppermute(x, "z", [(i, (i + by) % peers) for i in range(peers)])


def dot(left, right, left_dim, right_dim):
    return lax.dot_general(
        left, right, (((left_dim,), (right_dim,)), ((), ())), preferred_element_type=F32
    )


def half_of(x, which, axis):
    size = x.shape[axis] // 2
    return lax.dynamic_slice_in_dim(x, which * size, size, axis)


def ordered(own, other, rank, axis):
    return jnp.where(
        rank == 0,
        jnp.concatenate((own, other), axis=axis),
        jnp.concatenate((other, own), axis=axis),
    )


def after(x, *others):
    return lax.optimization_barrier((x, *others))[0]


def tie(*xs):
    return lax.optimization_barrier(xs)


def gather_one(v):
    half = v.shape[1] // 2
    return v, swap(v, "c"), swap(v[:, :half], "x"), swap(v[:, half:], "y")


def gather_two(state):
    v, near, a01, b10 = state
    half = v.shape[1] // 2
    a1 = swap(jnp.concatenate((v[:, :half], a01)), "y")
    b1 = swap(jnp.concatenate((v[:, half:], b10)), "x")
    second = swap(jnp.concatenate((a01, b10)), "c")
    return v, near, a01, b10, second, a1, b1


def gather_three(state):
    size, half = state[0].shape[0], state[0].shape[1] // 2
    state = (state[0], *tie(*state[1:]))
    third = swap(jnp.concatenate(state[5:]), "c")
    spots = (
        (0, 0, size, 0, 0), (1, 0, size, 4 * size, 0), (2, 0, size, size, 0),
        (3, 0, size, 2 * size, half), (4, 0, size, 5 * size, 0),
        (4, size, size, 6 * size, half), (5, 0, 2 * size, 2 * size, 0),
        (6, 0, size, size, half), (6, size, size, 3 * size, half),
        (7, 0, 2 * size, 6 * size, 0), (7, 2 * size, size, 5 * size, half),
        (7, 3 * size, size, 7 * size, half),
    )
    return place((*state, third), spots, 8 * size)


def place_kernel(spots, *refs):
    pieces, (out, sems) = refs[:-2], refs[-2:]
    copies = []
    for at, (piece, start, size, row, col) in enumerate(spots):
        source = pieces[piece]
        copies.append(
            pltpu.make_async_copy(
                source.at[pl.ds(start, size), :],
                out.at[pl.ds(row, size), pl.ds(col, source.shape[1])],
                sems.at[at],
            )
        )
    for copy in copies:
        copy.start()
    for copy in copies:
        copy.wait()


def place(pieces, spots, count):
    return pl.pallas_call(
        functools.partial(place_kernel, spots),
        out_shape=jax.ShapeDtypeStruct((count, pieces[0].shape[1]), BF16),
        in_specs=[pl.BlockSpec(memory_space=pltpu.VMEM)] * len(pieces),
        out_specs=pl.BlockSpec(memory_space=pltpu.HBM),
        scratch_shapes=[pltpu.SemaphoreType.DMA((len(spots),))],
        compiler_params=pltpu.CompilerParams(vmem_limit_bytes=60 * 2**20),
        cost_estimate=FREE,
        name="place",
    )(*pieces)


def product_kernel(terms, keep, *refs):
    count = len(terms)
    step = pl.program_id(0)
    flipped = sum(term[0] == 0 for term in terms)
    scratch = refs[len(refs) - flipped :]
    total, used = None, 0
    for at, (left_dim, right_dim, cut) in enumerate(terms):
        left, right = refs[2 * at], refs[2 * at + 1]
        if left_dim == 0:
            store = scratch[used]
            used += 1

            @pl.when(step == 0)
            def _(left=left, store=store):
                store[...] = upright(left[...])

            left = store
        block = right[...] if cut is None else right[:, cut[0] : cut[1]]
        one = dot(left[...], block, 1, right_dim)
        total = one if total is None else total + one
    if not keep:
        refs[2 * count][...] = total.astype(BF16)
        return
    came, left_out, right_out, x_out, y_out = refs[2 * count : 2 * count + 5]
    total = total + came[...].astype(F32)
    blocks = total.reshape(2, 2, total.shape[0] // 4, total.shape[1])
    half = pl.num_programs(0) // 2

    @pl.when(step < half)
    def _():
        left_out[...] = blocks[:, 0]
        x_out[...] = blocks[:, 1].astype(BF16)

    @pl.when(step >= half)
    def _():
        right_out[...] = blocks[0]
        y_out[...] = blocks[1].astype(BF16)


def product(terms, part, came=None):
    tile = 512
    args, specs, kinds, scratch = [], [], [], []
    for left, right, left_dim, right_dim, cut, *block in terms:
        rows = left.shape[1 - left_dim] // 2
        depth = left.shape[left_dim]
        if left_dim == 1:
            specs.append(pl.BlockSpec((rows, depth), lambda n: (part, 0)))
        else:
            specs.append(pl.BlockSpec((depth, rows), lambda n: (0, part)))
            scratch.append(pltpu.VMEM((rows, depth), BF16))
        if right_dim == 1:
            width = right.shape[0]
            if block:
                specs.append(pl.BlockSpec((tile, depth), lambda n, at=block[0]: (n, at)))
            else:
                specs.append(pl.BlockSpec((tile, right.shape[1]), lambda n: (n, 0)))
        else:
            width = right.shape[1]
            specs.append(pl.BlockSpec((right.shape[0], tile), lambda n: (0, n)))
        args += [left, right]
        kinds.append((left_dim, right_dim, cut))
    if came is None:
        out_shape = jax.ShapeDtypeStruct((rows, width), BF16)
        out_specs = pl.BlockSpec((rows, tile), lambda n: (0, n))
    else:
        args.append(came)
        specs.append(pl.BlockSpec((rows, tile), lambda n: (0, n)))
        half = width // tile // 2
        shape = (2, rows // 4, width // 2)
        out_shape = [jax.ShapeDtypeStruct(shape, d) for d in (F32, F32, BF16, BF16)]
        first = pl.BlockSpec((2, rows // 4, tile), lambda n: (0, 0, jnp.minimum(n, half - 1)))
        last = pl.BlockSpec((2, rows // 4, tile), lambda n: (0, 0, jnp.maximum(n - half, 0)))
        out_specs = [first, last, first, last]
    return pl.pallas_call(
        functools.partial(product_kernel, kinds, came is not None),
        out_shape=out_shape,
        grid=(width // tile,),
        in_specs=specs,
        out_specs=out_specs,
        scratch_shapes=scratch,
        compiler_params=pltpu.CompilerParams(vmem_limit_bytes=56 * 2**20),
        cost_estimate=pl.CostEstimate(
            flops=2 * sum(t[0].size for t in terms) // 2 * width,
            bytes_accessed=2 * sum(t[0].size for t in terms) + 2 * rows * width,
            transcendentals=0,
        ),
        name="product",
    )(*args)


def spread_one(terms, came=None):
    came = swap(product(terms, 1), "c") if came is None else came
    left, right, send_x, send_y = product(terms, 0, came)
    return left, right, swap(send_x, "x"), swap(send_y, "y"), (send_x, send_y)


def spread_two(state):
    left, right, left_x, right_y = state[:4]
    left = left + left_x.astype(F32)
    right = right + right_y.astype(F32)
    send_y, send_x = left[1].astype(BF16), right[1].astype(BF16)
    return left[0], right[0], swap(send_y, "y"), swap(send_x, "x"), (send_x, send_y)


def spread_three(state):
    left, right, left_y, right_x = state[:4]
    return jnp.concatenate((left + left_y.astype(F32), right + right_x.astype(F32)), axis=1)


def over_z(x, combine):
    peers, step = lax.axis_size("z"), 1
    assert peers & (peers - 1) == 0
    while step < peers:
        x = combine(x, along(x, step))
        step *= 2
    return x


def place_of(block, rank):
    j = jnp.bitwise_xor(block, rank)
    return jnp.bitwise_or(jnp.left_shift(jnp.bitwise_and(j, 1), 2), jnp.right_shift(j, 1))


def lanes_of(block, rank):
    return pl.ds(pl.multiple_of(place_of(block, rank) * BLOCK, BLOCK), BLOCK)


def rope_kernel(info, qkv, cos, sin, out):
    rank = info[0]

    @pl.loop(0, SLOT_LEN // BLOCK)
    def _(block):
        source = lanes_of(block, rank)
        target = pl.ds(pl.multiple_of(block * BLOCK, BLOCK), BLOCK)
        c, s = cos[:, target], sin[:, target]
        for head in range(HEADS + 1):
            first = qkv[pl.ds(head * HD, HALF), source]
            second = qkv[pl.ds(head * HD + HALF, HALF), source]
            scale = MULTIPLIER if head < HEADS else 1.0
            out[pl.ds(head * HD, HALF), target] = ((first * c - second * s).astype(BF16) * scale).astype(BF16)
            out[pl.ds(head * HD + HALF, HALF), target] = ((second * c + first * s).astype(BF16) * scale).astype(BF16)
        rest = (HEADS + 1) * HD
        out[pl.ds(rest, HD), target] = qkv[pl.ds(rest, HD), source].astype(BF16)


KEYS = SLOT_LEN + LEAD
K_AT = HEADS * HD
V_AT = K_AT + HD


def upright(x):
    return x.astype(F32).T.astype(BF16)


def causal():
    keys = lax.broadcasted_iota(jnp.int32, (CHUNK, CHUNK), 0)
    queries = lax.broadcasted_iota(jnp.int32, (CHUNK, CHUNK), 1)
    return keys <= queries


def key_range(step):
    last = step == SLOT_LEN // CHUNK - 1
    low = jnp.where(last, KEYS // CHUNK - 1, 0)
    high = jnp.where(last, KEYS // CHUNK, step + 2)
    return low, high


def chunk_of(i):
    return pl.ds(pl.multiple_of(i * CHUNK, CHUNK), CHUNK)


def head_rows(h):
    return pl.ds(pl.multiple_of(h * HD, HD), HD)


def attend_kernel(info, qkv, halo, heads_out, lse_out, peak_out, k_up, v_flat, scores):
    rank = info[0]
    k_up[pl.ds(0, LEAD), :] = upright(halo[pl.ds(0, HD), :])
    v_flat[:, pl.ds(0, LEAD)] = halo[pl.ds(HD, HD), :]
    v_flat[:, pl.ds(LEAD, SLOT_LEN)] = qkv[pl.ds(V_AT, HD), :]

    @pl.loop(0, SLOT_LEN // CHUNK)
    def _(i):
        k_up[pl.ds(pl.multiple_of(LEAD + i * CHUNK, CHUNK), CHUNK), :] = upright(
            qkv[pl.ds(K_AT, HD), chunk_of(i)]
        )

    peak_out[...] = jnp.full(peak_out.shape, NEGATIVE, F32)
    lse_out[...] = jnp.zeros(lse_out.shape, F32)

    @pl.loop(0, HEADS)
    def _(h):
        @pl.loop(0, SLOT_LEN // CHUNK)
        def _(step):
            low, high = key_range(step)
            query = qkv[head_rows(h), chunk_of(step)]

            def raw(kc):
                return jnp.dot(k_up[chunk_of(kc), :], query, preferred_element_type=F32)

            def first(kc, top):
                s = raw(kc)
                scores[chunk_of(kc - low), :] = s
                return jnp.maximum(top, jnp.max(s, axis=0, keepdims=True))

            s = jnp.where(causal(), raw(high - 1), NEGATIVE)
            scores[chunk_of(high - 1 - low), :] = s
            top = lax.fori_loop(low, high - 1, first, jnp.max(s, axis=0, keepdims=True))

            def second(kc, total):
                e = jnp.exp(scores[chunk_of(kc), :] - top)
                scores[chunk_of(kc), :] = e
                return total + jnp.sum(e, axis=0, keepdims=True)

            total = lax.fori_loop(0, high - low, second, jnp.zeros((1, CHUNK), F32))
            inverse = 1.0 / total

            def third(kc, mixed):
                probs = (scores[chunk_of(kc), :] * inverse).astype(BF16)
                return mixed + jnp.dot(
                    v_flat[:, chunk_of(kc + low)], probs, preferred_element_type=F32
                )

            mixed = lax.fori_loop(0, high - low, third, jnp.zeros((HD, CHUNK), F32))
            mixed = mixed.astype(BF16)
            for part in range(CHUNK // BLOCK):
                heads_out[head_rows(h), lanes_of(step * (CHUNK // BLOCK) + part, rank)] = mixed[
                    :, part * BLOCK : (part + 1) * BLOCK
                ]
            lse_out[pl.ds(h, 1), chunk_of(step)] = top + jnp.log(total)
            last = step == SLOT_LEN // CHUNK - 1
            start = jnp.where(last, 0, LEAD + step * CHUNK)
            alive = jnp.where(last, info[2], info[1])
            spots = lax.broadcasted_iota(jnp.int32, (1, CHUNK), 1) + start
            best = jnp.max(jnp.where(spots < alive, top, NEGATIVE), axis=1, keepdims=True)
            peak_out[pl.ds(h, 1), :] = jnp.maximum(peak_out[pl.ds(h, 1), :], best)


def attend_back_kernel(
    info, qkv, halo, upstream, lse, cos, sin, dq_out, dkv_out, halo_out,
    k_up, v_up, k_flat, probs_s, grads_s, dk_s, dv_s, up_abs,
):
    rank = info[0]
    k_up[pl.ds(0, LEAD), :] = upright(halo[pl.ds(0, HD), :])
    v_up[pl.ds(0, LEAD), :] = upright(halo[pl.ds(HD, HD), :])
    k_flat[:, pl.ds(0, LEAD)] = halo[pl.ds(0, HD), :]
    k_flat[:, pl.ds(LEAD, SLOT_LEN)] = qkv[pl.ds(K_AT, HD), :]

    @pl.loop(0, SLOT_LEN // CHUNK)
    def _(i):
        rows = pl.ds(pl.multiple_of(LEAD + i * CHUNK, CHUNK), CHUNK)
        k_up[rows, :] = upright(qkv[pl.ds(K_AT, HD), chunk_of(i)])
        v_up[rows, :] = upright(qkv[pl.ds(V_AT, HD), chunk_of(i)])

    @pl.loop(0, SLOT_LEN // BLOCK)
    def _(block):
        target = pl.ds(pl.multiple_of(block * BLOCK, BLOCK), BLOCK)
        up_abs[:, target] = upstream[:, lanes_of(block, rank)]

    dk_s[...] = jnp.zeros(dk_s.shape, F32)
    dv_s[...] = jnp.zeros(dv_s.shape, F32)

    @pl.loop(0, HEADS)
    def _(h):
        @pl.loop(0, SLOT_LEN // CHUNK)
        def _(step):
            low, high = key_range(step)
            here = chunk_of(step)
            query = qkv[head_rows(h), here]
            grad = up_abs[head_rows(h), here]
            query_up, grad_up = upright(query), upright(grad)
            logs = lse[pl.ds(h, 1), here]

            def one(kc, masked):
                s = jnp.dot(k_up[chunk_of(kc), :], query, preferred_element_type=F32)
                p = jnp.exp(s - logs)
                if masked:
                    p = jnp.where(causal(), p, 0.0)
                g = jnp.dot(v_up[chunk_of(kc), :], grad, preferred_element_type=F32)
                probs_s[chunk_of(kc - low), :] = p
                grads_s[chunk_of(kc - low), :] = g
                dv_s[chunk_of(kc), :] += jnp.dot(
                    p.astype(BF16), grad_up, preferred_element_type=F32
                )
                return jnp.sum(p * g, axis=0, keepdims=True)

            delta = one(high - 1, True)
            delta = lax.fori_loop(low, high - 1, lambda kc, d: d + one(kc, False), delta)

            def two(kc, dq):
                p, g = probs_s[chunk_of(kc - low), :], grads_s[chunk_of(kc - low), :]
                ds = (p * (g - delta)).astype(BF16)
                dk_s[chunk_of(kc), :] += jnp.dot(ds, query_up, preferred_element_type=F32)
                return dq + jnp.dot(k_flat[:, chunk_of(kc)], ds, preferred_element_type=F32)

            dq = lax.fori_loop(low, high, two, jnp.zeros((HD, CHUNK), F32)) * MULTIPLIER
            c, s = cos[:, here], sin[:, here]
            u1, u2 = dq[:HALF], dq[HALF:]
            t1, t2 = (u1 * c + u2 * s).astype(BF16), (u2 * c - u1 * s).astype(BF16)
            for part in range(CHUNK // BLOCK):
                there = lanes_of(step * (CHUNK // BLOCK) + part, rank)
                cut = slice(part * BLOCK, (part + 1) * BLOCK)
                dq_out[pl.ds(pl.multiple_of(h * HD, HD), HALF), there] = t1[:, cut]
                dq_out[pl.ds(pl.multiple_of(h * HD + HALF, HALF), HALF), there] = t2[:, cut]

    halo_out[pl.ds(0, HD), :] = dk_s[pl.ds(0, LEAD), :].T.astype(BF16)
    halo_out[pl.ds(HD, HD), :] = dv_s[pl.ds(0, LEAD), :].T.astype(BF16)

    @pl.loop(0, SLOT_LEN // CHUNK)
    def _(i):
        rows = pl.ds(pl.multiple_of(LEAD + i * CHUNK, CHUNK), CHUNK)
        dkv_out[pl.ds(0, HD), chunk_of(i)] = dk_s[rows, :].T
        dkv_out[pl.ds(HD, HD), chunk_of(i)] = dv_s[rows, :].T


def finish_kernel(info, dkv, halo, cos, sin, out):
    rank = info[0]
    owned = (SLOT_LEN - LEAD) // BLOCK
    for block in range(SLOT_LEN // BLOCK):
        source = pl.ds(block * BLOCK, BLOCK)
        target = lanes_of(block, rank)
        c, s = cos[:, source], sin[:, source]
        u1, u2 = dkv[pl.ds(0, HALF), source], dkv[pl.ds(HALF, HALF), source]
        rest = dkv[pl.ds(HD, HD), source]
        if block >= owned:
            part = pl.ds((block - owned) * BLOCK, BLOCK)
            u1 = u1 + halo[pl.ds(0, HALF), part].astype(F32)
            u2 = u2 + halo[pl.ds(HALF, HALF), part].astype(F32)
            rest = rest + halo[pl.ds(HD, HD), part].astype(F32)
        out[pl.ds(0, HALF), target] = (u1 * c + u2 * s).astype(BF16)
        out[pl.ds(HALF, HALF), target] = (u2 * c - u1 * s).astype(BF16)
        out[pl.ds(HD, HD), target] = rest.astype(BF16)


def call(kernel, info, args, outs, scratch, name):
    spec = pl.BlockSpec(memory_space=pltpu.VMEM)
    return pl.pallas_call(
        kernel,
        out_shape=[jax.ShapeDtypeStruct(s, d) for s, d in outs],
        in_specs=[pl.BlockSpec(memory_space=pltpu.SMEM)] + [spec] * len(args),
        out_specs=[spec] * len(outs),
        scratch_shapes=[pltpu.VMEM(s, d) for s, d in scratch],
        compiler_params=pltpu.CompilerParams(vmem_limit_bytes=40 * 2**20),
        cost_estimate=FREE,
        name=name,
    )(info, *args)


def hidden_kernel(rows, gate_w, up_w, gate_out, up_out, hidden_out):
    gate, up = dot(rows[...], gate_w[...], 1, 0), dot(rows[...], up_w[...], 1, 0)
    gate_out[...], up_out[...] = gate, up
    hidden_out[...] = (gate * jax.nn.sigmoid(gate) * up).astype(BF16)


def hidden_back_kernel(rows, weights, gates, ups, gate_out, up_out):
    grad = dot(rows[...], weights[...], 1, 1)
    gate = gates[...]
    sig = jax.nn.sigmoid(gate)
    gate_out[...] = (grad * ups[...] * sig * (1.0 + gate * (1.0 - sig))).astype(BF16)
    up_out[...] = (grad * gate * sig).astype(BF16)


def ffn_call(kernel, rows, weights, width, kinds, held, name):
    high, wide = min(512, rows.shape[0]), min(512, width)
    depth, steps = rows.shape[1], width // wide
    tile = pl.BlockSpec((high, wide), lambda n, m: (m, n))
    if held:
        specs = [pl.BlockSpec((wide, depth), lambda n, m: (n, 0))]
    else:
        specs = [pl.BlockSpec((depth, wide), lambda n, m: (0, n)),
                 pl.BlockSpec((depth, wide), lambda n, m: (0, n + steps))]
    return pl.pallas_call(
        kernel,
        out_shape=[jax.ShapeDtypeStruct((rows.shape[0], width), kind) for kind in kinds],
        grid=(steps, rows.shape[0] // high),
        in_specs=[pl.BlockSpec((high, depth), lambda n, m: (m, 0))] + specs + [tile] * len(held),
        out_specs=[tile] * len(kinds),
        compiler_params=pltpu.CompilerParams(vmem_limit_bytes=56 * 2**20),
        cost_estimate=FREE,
        name=name,
    )(rows, *([weights] * len(specs)), *held)


def outer_kernel(right_dim, left, right, out):
    out[...] = dot(left[...], right[...], 0, right_dim).astype(BF16)


def outer_gain_kernel(right_dim, cut, left, right, weights, out, gain):
    total = dot(left[...], right[...], 0, right_dim)
    out[...] = total.astype(BF16)
    scaled = total * weights[:, cut[0] : cut[1]].astype(F32)
    gain[...] = jnp.broadcast_to(jnp.sum(scaled, axis=1, keepdims=True), gain.shape)


def outer(left, right, right_dim, weights=None, cut=None):
    depth, high = left.shape
    wide = right.shape[1 - right_dim]
    rows, cols = min(512, high), min(1024, wide)
    right_block = (depth, cols) if right_dim == 0 else (cols, depth)
    right_map = (lambda n, m: (0, n)) if right_dim == 0 else (lambda n, m: (n, 0))
    specs = [pl.BlockSpec((depth, rows), lambda n, m: (0, m)), pl.BlockSpec(right_block, right_map)]
    outs = [jax.ShapeDtypeStruct((high, wide), BF16)]
    out_specs = [pl.BlockSpec((rows, cols), lambda n, m: (m, n))]
    args, kernel = (left, right), functools.partial(outer_kernel, right_dim)
    if weights is not None:
        args, kernel = (left, right, weights), functools.partial(outer_gain_kernel, right_dim, cut)
        specs.append(pl.BlockSpec((rows, weights.shape[1]), lambda n, m: (m, 0)))
        outs.append(jax.ShapeDtypeStruct((high, 128), F32))
        out_specs.append(pl.BlockSpec((rows, 128), lambda n, m: (m, 0)))
    return pl.pallas_call(
        kernel,
        out_shape=outs,
        grid=(wide // cols, high // rows),
        in_specs=specs,
        out_specs=out_specs,
        compiler_params=pltpu.CompilerParams(vmem_limit_bytes=56 * 2**20),
        cost_estimate=pl.CostEstimate(
            flops=2 * depth * high * wide,
            bytes_accessed=2 * (depth * (high + wide) + high * wide),
            transcendentals=0,
        ),
        name="outer",
    )(*args)


def norm_back(values, scale, upstream):
    mean_term = jnp.mean(values * upstream, axis=1, keepdims=True)
    return scale * upstream - values * (scale * scale * scale) * mean_term


def shards(
    layer_in, lengths, clip_level, attn_gain, w_query, w_key, w_value, w_out,
    mlp_gain, w_gate, w_up, w_down, cotangent,
):
    tok_rows, width = layer_in.shape
    z_rank, y_rank = lax.axis_index("z"), lax.axis_index("y")
    rank = (y_rank * 2 + lax.axis_index("x")) * 2 + lax.axis_index("c")
    slots = lengths.shape[0]
    next_slot = (z_rank + 1) % slots
    info = jnp.stack(
        (rank, lax.dynamic_index_in_dim(lengths, z_rank, keepdims=False),
         lax.dynamic_index_in_dim(lengths, next_slot, keepdims=False))
    ).astype(jnp.int32)
    inner = rank * tok_rows + jnp.arange(tok_rows, dtype=jnp.int32) + LEAD
    own_mask = jnp.where(inner < SLOT_LEN, inner < info[1], inner - SLOT_LEN < info[2])
    own_mask = own_mask.astype(F32)[:, None]
    spots = ((jnp.arange(SLOT_LEN, dtype=jnp.int32) + LEAD) % SLOT_LEN).astype(F32)
    freq = THETA ** (-(jnp.arange(HALF, dtype=F32) * 2.0 / HD))
    angles = spots[None, :] * freq[:, None]
    cos, sin = jnp.cos(angles), jnp.sin(angles)
    def heads_part(which):
        return jnp.concatenate(
            (half_of(w_out, which, 0).T, half_of(w_query, which, 1), half_of(w_key, which, 1),
             half_of(w_value, which, 1)), 1
        )

    def ffn_part(which):
        return jnp.concatenate((half_of(w_gate, which, 1), half_of(w_up, which, 1)), 1)

    other_y = 1 - y_rank
    heads_w = ordered(heads_part(y_rank), swap(heads_part(other_y), "y"), y_rank, 0)
    full_heads = lax.all_gather(heads_w, "z", axis=0, tiled=True)
    out_cols = HEADS * HD
    heads_cut = (out_cols, full_heads.shape[1])

    ffn_other = swap(after(ffn_part(other_y), heads_w), "y")
    ffn_w = ordered(ffn_part(y_rank), ffn_other, y_rank, 0)
    layer_f = layer_in.astype(F32)
    scale_one = lax.rsqrt(jnp.mean(layer_f * layer_f, axis=1, keepdims=True) + EPSILON)
    normal_one = rounded(layer_f * scale_one)
    gain_one = attn_gain.astype(F32)
    acts = gather_one(after((normal_one * gain_one[None, :]).astype(BF16), heads_w))
    acts = gather_two(acts)
    full_heads, ffn_w, *acts = tie(full_heads, ffn_w, *acts)
    full_out, full_qkv = full_heads[:, :out_cols], full_heads[:, out_cols:]
    acts_one = gather_three(acts)
    full_ffn = lax.all_gather(ffn_w, "z", axis=0, tiled=True)

    grad_out = cotangent.astype(F32)
    down_in = (RESIDUAL * own_mask * grad_out).astype(BF16)
    back_rows = gather_one(after(down_in, ffn_other))
    rows = acts_one.shape[0]
    flat = dot(full_qkv, acts_one, 0, 1)
    (qkv,) = call(
        rope_kernel, info, (flat, cos, sin), [((flat.shape[0], rows), BF16)], [], "rope"
    )
    halo = along(qkv[K_AT:, SLOT_LEN - LEAD :], 1)
    qkv, halo, *back_rows = tie(qkv, halo, *back_rows)
    down_other = swap(after(half_of(w_down, other_y, 0), back_rows[2], back_rows[3]), "y")
    back_rows = gather_two(back_rows)
    heads, lse, peak = call(
        attend_kernel, info, (qkv, halo),
        [((HEADS * HD, rows), BF16), ((8, rows), F32), ((8, 128), F32)],
        [((KEYS, HD), BF16), ((HD, KEYS), BF16), ((SLOT_LEN, CHUNK), F32)],
        "attend",
    )
    heads, down_other, *back_rows = tie(heads, down_other, *back_rows)
    down_w = ordered(half_of(w_down, y_rank, 0), down_other, y_rank, 1)

    terms = [(heads, full_heads, 0, 1, (0, out_cols))]
    own_peak = peak[:HEADS]
    came, other_peak = tie(swap(product(terms, 1), "c"), swap(own_peak, "y"))
    branch = spread_one(terms, came)
    head_peak = after(ordered(own_peak, other_peak, y_rank, 0), *branch[4])
    head_peak = over_z(head_peak, jnp.maximum)
    down_rows = gather_three((*back_rows[:5], *after(back_rows[5:], *branch[4])))
    *got, down_rows, down_w, head_peak = tie(*branch[2:4], down_rows, down_w, head_peak)
    head_peak = head_peak[:, 0]
    branch = spread_two((*branch[:2], *got))
    full_down = lax.all_gather(down_w, "z", axis=1, tiled=True)
    branch_one = spread_three(branch)
    resid = layer_f + RESIDUAL * own_mask * branch_one
    scale_two = lax.rsqrt(jnp.mean(resid * resid, axis=1, keepdims=True) + EPSILON)
    normal_two = rounded(resid * scale_two)
    gain_two = mlp_gain.astype(F32)
    acts = gather_one((normal_two * gain_two[None, :]).astype(BF16))
    full_ffn, *acts = tie(full_ffn, *acts)
    acts = gather_two(acts)
    acts_two = gather_three(acts)

    width = full_ffn.shape[1] // 2
    gate_proj, up_proj, hidden = ffn_call(
        hidden_kernel, acts_two, full_ffn, width, (F32, F32, BF16), (), "hidden"
    )

    def reduced(grad, axis):
        return lax.psum_scatter(grad, "z", scatter_dimension=axis, tiled=True)

    def traded(total, axis, *behind):
        total = after(total, *behind)
        return half_of(total, y_rank, axis), swap(half_of(total, other_y, axis), "y")

    (down_part,) = outer(hidden, down_rows, 0)
    down_sum = reduced(down_part, 1)
    down_rows = after(down_rows, down_part)
    gate_grad, up_grad = ffn_call(
        hidden_back_kernel, down_rows, full_down, width, (BF16, BF16), (gate_proj, up_proj),
        "hidden_back",
    )
    norm_two = spread_one(
        [(gate_grad, full_ffn, 1, 1, None, 0), (up_grad, full_ffn, 1, 1, None, 1)]
    )
    held = after(acts_two, swap(norm_two[4][0][0, :8, :128], "c"))
    ffn_parts = [outer(held, grad, 0)[0] for grad in (gate_grad, up_grad)]
    one_sum, two_sum = [reduced(part, 0) for part in ffn_parts]
    got = tie(*norm_two[2:4], *ffn_parts)[:2]
    norm_two = spread_two((*norm_two[:2], *got))
    held = after(hidden, *norm_two[4])
    high_part = product([(held, full_down, 1, 0, None)], 1)
    got = tie(*norm_two[2:4], high_part)[:2]
    norm_two_grad = spread_three((*norm_two[:2], *got))
    grad_resid = grad_out + norm_back(resid, scale_two, gain_two[None, :] * norm_two_grad)
    mixed = gather_one((RESIDUAL * own_mask * grad_resid).astype(BF16))
    low_part = product([(after(hidden, mixed[0]), full_down, 1, 0, None)], 0, swap(high_part, "c"))
    gain_two_part = jnp.sum(normal_two * norm_two_grad, axis=0)
    *got, gain_two_part = tie(*mixed[2:4], gain_two_part, *low_part)[:3]
    mixed = gather_two((*mixed[:2], *got))
    send_x, send_y = after(low_part[2:], *mixed[1:])
    second = (*low_part[:2], swap(send_x, "x"), swap(send_y, "y"))
    mixed_rows = gather_three(mixed)
    mixed_rows, down_sum = tie(mixed_rows, down_sum)
    down_own, down_other = traded(down_sum, 1)

    heads_grad = dot(full_out, mixed_rows, 0, 1).astype(BF16)
    dq, dkv, back = call(
        attend_back_kernel, info, (qkv, halo, heads_grad, lse, cos, sin),
        [((HEADS * HD, rows), BF16), ((2 * HD, rows), F32), ((2 * HD, LEAD), BF16)],
        [((KEYS, HD), BF16), ((KEYS, HD), BF16), ((HD, KEYS), BF16),
         ((SLOT_LEN, CHUNK), F32), ((SLOT_LEN, CHUNK), F32),
         ((KEYS, HD), F32), ((KEYS, HD), F32), ((HEADS * HD, SLOT_LEN), BF16)],
        "attend_back",
    )
    back, down_other, *got = tie(back, down_other, *second[2:4])
    back_sent = along(back, -1)
    second = spread_two((*second[:2], *got))
    (out_part,) = outer(after(mixed_rows, back), heads, 1)
    out_sum = reduced(out_part, 0)
    dkv, back_sent, out_part, one_sum = tie(dkv, back_sent, out_part, one_sum)
    one_own, one_other = traded(one_sum, 0)
    (dkv_done,) = call(
        finish_kernel, info, (dkv, back_sent, cos, sin), [((2 * HD, rows), BF16)], [], "finish"
    )
    dqkv = jnp.concatenate((dq, dkv_done))
    terms = [(dqkv, full_heads, 0, 1, heads_cut)]
    came = swap(product(terms, 1), "c")
    came, out_sum, two_sum, one_other, *got = tie(came, out_sum, two_sum, one_other, *second[2:4])
    branch_two = spread_three((*second[:2], *got))
    result = resid + RESIDUAL * own_mask * branch_two

    norm_one = spread_one(terms, came)
    qkv_part, sums = outer(after(acts_one, *norm_one[4]), dqkv, 1, full_heads, heads_cut)
    gain_one_part = sums[:, 0] / gain_one
    qkv_sum = reduced(qkv_part, 0)
    *got, gain_one_part = tie(*norm_one[2:4], gain_one_part, qkv_part)[:3]
    norm_one = spread_two((*norm_one[:2], *got))
    two_own, two_other = traded(two_sum, 0, *norm_one[4])
    norm_one_grad = spread_three(norm_one)
    norm_one_grad, qkv_sum = tie(norm_one_grad, qkv_sum)
    grad_input = grad_resid + norm_back(layer_f, scale_one, gain_one[None, :] * norm_one_grad)
    gain_one_part = after(gain_one_part, norm_one_grad)
    out_own, out_other = traded(out_sum, 0, norm_one_grad)
    own, other = traded(qkv_sum, 0, norm_one_grad)

    gains = jnp.stack((gain_one_part, gain_two_part))
    gains = gains.reshape(2, lax.axis_size("z"), 2, 2, 2, -1)
    for dim, axis in ((4, "c"), (3, "x"), (2, "y")):
        at = lax.axis_index(axis)
        other_at = lax.dynamic_index_in_dim(gains, 1 - at, dim, keepdims=False)
        gains = lax.dynamic_index_in_dim(gains, at, dim, keepdims=False) + swap(other_at, axis)
    gains = lax.dynamic_index_in_dim(over_z(gains, jnp.add), z_rank, 1, keepdims=False)

    down_grad = ordered(down_own, down_other, y_rank, 0).astype(F32)
    gate_w_grad = ordered(one_own, one_other, y_rank, 1).astype(F32)
    up_w_grad = ordered(two_own, two_other, y_rank, 1).astype(F32)
    out_grad = ordered(out_own.T, out_other.T, y_rank, 0).astype(F32)

    def columns(start, stop):
        return ordered(own[:, start:stop], other[:, start:stop], y_rank, 1).astype(F32)

    query_grad = columns(0, K_AT)
    key_grad = columns(K_AT, V_AT)
    value_grad = columns(V_AT, V_AT + HD)

    level = clip_level[0].astype(F32) * LEVEL_UNIT
    factor = level / jnp.maximum(level, head_peak)
    query_clipped = w_query.astype(F32) * jnp.repeat(jnp.sqrt(factor), HD)[None, :]
    kv_factor = jnp.min(factor.reshape(-1, HEADS), axis=1)
    key_clipped = w_key.astype(F32) * jnp.repeat(jnp.sqrt(kv_factor), HD)[None, :]
    return (
        result.astype(BF16),
        grad_input.astype(BF16),
        gains[0],
        query_grad,
        key_grad,
        value_grad,
        out_grad,
        gains[1],
        gate_w_grad,
        up_w_grad,
        down_grad,
        query_clipped,
        key_clipped,
    )


def solution(mesh):
    fsdp, tp = mesh.shape["fsdp"], mesh.shape["tp"]
    fine = Mesh(mesh.devices.reshape(fsdp // 2, 2, tp // 2, 2), EVERY)
    rows, cols = ("z", "y"), ("x", "c")
    tokens, down, across = P(EVERY, None), P(rows, cols), P(cols, rows)
    in_specs = (
        tokens, P(), P(), P(), down, down, down, across, P(), down, down, across, tokens,
    )
    out_specs = (
        tokens, tokens, P(EVERY), down, down, down, across, P(EVERY), down, down, across,
        down, down,
    )
    return jax.shard_map(shards, mesh=fine, in_specs=in_specs, out_specs=out_specs, check_vma=False)
```

```python
import functools

import jax
import jax.numpy as jnp
from jax import lax
from jax.experimental import pallas as pl
from jax.experimental.pallas import tpu as pltpu
from jax.sharding import Mesh
from jax.sharding import PartitionSpec as P

HD = 64
HALF = HD // 2
SLOT_LEN = 2048
LEAD = 512
CHUNK = 512
BLOCK = 256
HEADS = 4

EPSILON = 1e-05
THETA = 10000000.0
MULTIPLIER = 0.015625
RESIDUAL = 0.22
LEVEL_UNIT = 0.125
NEGATIVE = -1e30
GROUP = ("y", "x", "c")
EVERY = ("z", "y", "x", "c")
F32 = jnp.float32
BF16 = jnp.bfloat16
FREE = pl.CostEstimate(flops=0, bytes_accessed=0, transcendentals=0)


def rounded(x):
    return lax.reduce_precision(x, exponent_bits=8, mantissa_bits=7)


def swap(x, axis):
    return lax.ppermute(x, axis, [(0, 1), (1, 0)])


def along(x, by):
    peers = lax.axis_size("z")
    return lax.ppermute(x, "z", [(i, (i + by) % peers) for i in range(peers)])


def dot(left, right, left_dim, right_dim):
    return lax.dot_general(
        left, right, (((left_dim,), (right_dim,)), ((), ())), preferred_element_type=F32
    )


def half_of(x, which, axis):
    size = x.shape[axis] // 2
    return lax.dynamic_slice_in_dim(x, which * size, size, axis)


def ordered(own, other, rank, axis):
    return jnp.where(
        rank == 0,
        jnp.concatenate((own, other), axis=axis),
        jnp.concatenate((other, own), axis=axis),
    )


def after(x, *others):
    return lax.optimization_barrier((x, *others))[0]


def tie(*xs):
    return lax.optimization_barrier(xs)


def gather_one(v, halves=None):
    half = v.shape[1] // 2
    halves = (v[:, :half], v[:, half:]) if halves is None else halves
    return v, swap(v, "c"), swap(halves[0], "x"), swap(halves[1], "y")


def gather_two(state):
    v, near, a01, b10 = state
    half = v.shape[1] // 2
    a1 = swap(jnp.concatenate((v[:, :half], a01)), "y")
    b1 = swap(jnp.concatenate((v[:, half:], b10)), "x")
    second = swap(jnp.concatenate((a01, b10)), "c")
    return v, near, a01, b10, second, a1, b1


def gather_three(state):
    size, half = state[0].shape[0], state[0].shape[1] // 2
    state = (state[0], *tie(*state[1:]))
    third = swap(jnp.concatenate(state[5:]), "c")
    spots = (
        (0, 0, size, 0, 0), (1, 0, size, 4 * size, 0), (2, 0, size, size, 0),
        (3, 0, size, 2 * size, half), (4, 0, size, 5 * size, 0),
        (4, size, size, 6 * size, half), (5, 0, 2 * size, 2 * size, 0),
        (6, 0, size, size, half), (6, size, size, 3 * size, half),
        (7, 0, 2 * size, 6 * size, 0), (7, 2 * size, size, 5 * size, half),
        (7, 3 * size, size, 7 * size, half),
    )
    return place((*state, third), spots, 8 * size)


def place_kernel(spots, *refs):
    pieces, (out, sems) = refs[:-2], refs[-2:]
    copies = []
    for at, (piece, start, size, row, col) in enumerate(spots):
        source = pieces[piece]
        copies.append(
            pltpu.make_async_copy(
                source.at[pl.ds(start, size), :],
                out.at[pl.ds(row, size), pl.ds(col, source.shape[1])],
                sems.at[at],
            )
        )
    for copy in copies:
        copy.start()
    for copy in copies:
        copy.wait()


def place(pieces, spots, count):
    return pl.pallas_call(
        functools.partial(place_kernel, spots),
        out_shape=jax.ShapeDtypeStruct((count, pieces[0].shape[1]), BF16),
        in_specs=[pl.BlockSpec(memory_space=pltpu.VMEM)] * len(pieces),
        out_specs=pl.BlockSpec(memory_space=pltpu.HBM),
        scratch_shapes=[pltpu.SemaphoreType.DMA((len(spots),))],
        compiler_params=pltpu.CompilerParams(vmem_limit_bytes=60 * 2**20),
        cost_estimate=FREE,
        name="place",
    )(*pieces)


def product_kernel(terms, keep, *refs):
    count = len(terms)
    step = pl.program_id(0)
    flipped = sum(term[0] == 0 for term in terms)
    scratch = refs[len(refs) - flipped :]
    total, used = None, 0
    for at, (left_dim, right_dim, cut) in enumerate(terms):
        left, right = refs[2 * at], refs[2 * at + 1]
        if left_dim == 0:
            store = scratch[used]
            used += 1

            @pl.when(step == 0)
            def _(left=left, store=store):
                store[...] = upright(left[...])

            left = store
        block = right[...] if cut is None else right[:, cut[0] : cut[1]]
        one = dot(left[...], block, 1, right_dim)
        total = one if total is None else total + one
    if not keep:
        refs[2 * count][...] = total.astype(BF16)
        return
    came, left_out, right_out, x_out, y_out = refs[2 * count : 2 * count + 5]
    total = total + came[...].astype(F32)
    blocks = total.reshape(2, 2, total.shape[0] // 4, total.shape[1])
    half = pl.num_programs(0) // 2

    @pl.when(step < half)
    def _():
        left_out[...] = blocks[:, 0]
        x_out[...] = blocks[:, 1].astype(BF16)

    @pl.when(step >= half)
    def _():
        right_out[...] = blocks[0]
        y_out[...] = blocks[1].astype(BF16)


def product(terms, part, came=None):
    tile = 512
    args, specs, kinds, scratch = [], [], [], []
    for left, right, left_dim, right_dim, cut, *block in terms:
        rows = left.shape[1 - left_dim] // 2
        depth = left.shape[left_dim]
        if left_dim == 1:
            specs.append(pl.BlockSpec((rows, depth), lambda n: (part, 0)))
        else:
            specs.append(pl.BlockSpec((depth, rows), lambda n: (0, part)))
            scratch.append(pltpu.VMEM((rows, depth), BF16))
        if right_dim == 1:
            width = right.shape[0]
            if block:
                specs.append(pl.BlockSpec((tile, depth), lambda n, at=block[0]: (n, at)))
            else:
                specs.append(pl.BlockSpec((tile, right.shape[1]), lambda n: (n, 0)))
        else:
            width = right.shape[1]
            specs.append(pl.BlockSpec((right.shape[0], tile), lambda n: (0, n)))
        args += [left, right]
        kinds.append((left_dim, right_dim, cut))
    if came is None:
        out_shape = jax.ShapeDtypeStruct((rows, width), BF16)
        out_specs = pl.BlockSpec((rows, tile), lambda n: (0, n))
    else:
        args.append(came)
        specs.append(pl.BlockSpec((rows, tile), lambda n: (0, n)))
        half = width // tile // 2
        shape = (2, rows // 4, width // 2)
        out_shape = [jax.ShapeDtypeStruct(shape, d) for d in (F32, F32, BF16, BF16)]
        first = pl.BlockSpec((2, rows // 4, tile), lambda n: (0, 0, jnp.minimum(n, half - 1)))
        last = pl.BlockSpec((2, rows // 4, tile), lambda n: (0, 0, jnp.maximum(n - half, 0)))
        out_specs = [first, last, first, last]
    return pl.pallas_call(
        functools.partial(product_kernel, kinds, came is not None),
        out_shape=out_shape,
        grid=(width // tile,),
        in_specs=specs,
        out_specs=out_specs,
        scratch_shapes=scratch,
        compiler_params=pltpu.CompilerParams(vmem_limit_bytes=56 * 2**20),
        cost_estimate=FREE,
        name="product",
    )(*args)


def spread_one(terms, came=None, *later):
    came = swap(product(terms, 1), "c") if came is None else came
    left, right, send_x, send_y = product(terms, 0, came)
    if later:
        send_x, send_y, *later = tie(send_x, send_y, *later)
    return left, right, swap(send_x, "x"), swap(send_y, "y"), *later


def fold_kernel(left, right, left_x, right_y, left_out, right_out, y_out, x_out):
    total = left[...] + left_x[...].astype(F32)
    left_out[...], y_out[...] = total[0], total[1].astype(BF16)
    total = right[...] + right_y[...].astype(F32)
    right_out[...], x_out[...] = total[0], total[1].astype(BF16)


def fold(*parts):
    rows, cols = parts[0].shape[1:]
    size = rows // 4
    return pl.pallas_call(
        fold_kernel,
        out_shape=[jax.ShapeDtypeStruct((rows, cols), d) for d in (F32, F32, BF16, BF16)],
        grid=(4,),
        in_specs=[pl.BlockSpec((2, size, cols), lambda i: (0, i, 0))] * 4,
        out_specs=[pl.BlockSpec((size, cols), lambda i: (i, 0))] * 4,
        cost_estimate=FREE,
        name="fold",
    )(*parts)


def spread_two(state, *extra):
    left, right, send_y, send_x = fold(*state[:4])
    if extra:
        send_y, send_x, *extra = tie(send_y, send_x, *extra)
    return left, right, swap(send_y, "y"), swap(send_x, "x"), *extra


def spread_three(state):
    left, right, left_y, right_x = state[:4]
    return jnp.concatenate((left + left_y.astype(F32), right + right_x.astype(F32)), axis=1)


def joined(left, right, left_y, right_x):
    return jnp.concatenate(
        (left[...] + left_y[...].astype(F32), right[...] + right_x[...].astype(F32)), axis=1
    )


def store_halves(value, out, left_out, right_out):
    half = value.shape[1] // 2
    out[...], left_out[...], right_out[...] = value, value[:, :half], value[:, half:]


def residual_kernel(*refs):
    values, mask, gain = (ref[...] for ref in refs[4:7])
    resid_out, scale_out = refs[7:9]
    resid = values.astype(F32) + RESIDUAL * mask * joined(*refs[:4])
    scale = lax.rsqrt(jnp.mean(resid * resid, axis=1, keepdims=True) + EPSILON)
    resid_out[...], scale_out[...] = resid, scale
    normal = (resid * scale).astype(BF16).astype(F32)
    store_halves((normal * gain).astype(BF16), *refs[9:12])


def residual_back_kernel(*refs):
    base, values, scale, gain, mask = (ref[...] for ref in refs[4:9])
    sums, grad_out = refs[9:11]
    upstream = joined(*refs[:4])
    normal = (values * scale).astype(BF16).astype(F32)

    @pl.when(pl.program_id(0) == 0)
    def _():
        sums[...] = jnp.zeros(sums.shape, F32)

    share = normal * upstream
    sums[...] += jnp.sum(share.reshape(-1, 8, share.shape[1]), axis=0)
    grad = base.astype(F32) + norm_back(values, scale, gain * upstream)
    grad_out[...] = grad
    store_halves((RESIDUAL * mask * grad).astype(BF16), *refs[11:14])


def input_back_kernel(*refs):
    base, values, scale, gain = (ref[...] for ref in refs[4:8])
    grad = base + norm_back(values.astype(F32), scale, gain * joined(*refs[:4]))
    refs[8][...] = grad.astype(BF16)


def row_call(kernel, args, outs, name):
    rows = args[0].shape[0]
    size = rows // 4

    def spec(shape):
        if shape[0] == rows:
            return pl.BlockSpec((size, shape[1]), lambda i: (i, 0))
        return pl.BlockSpec(shape, lambda i: (0, 0))

    return pl.pallas_call(
        kernel,
        out_shape=[jax.ShapeDtypeStruct(shape, kind) for shape, kind in outs],
        grid=(4,),
        in_specs=[spec(arg.shape) for arg in args],
        out_specs=[spec(shape) for shape, _ in outs],
        cost_estimate=FREE,
        name=name,
    )(*args)


def over_z(x, combine):
    peers, step = lax.axis_size("z"), 1
    assert peers & (peers - 1) == 0
    while step < peers:
        x = combine(x, along(x, step))
        step *= 2
    return x


def place_of(block, rank):
    j = jnp.bitwise_xor(block, rank)
    return jnp.bitwise_or(jnp.left_shift(jnp.bitwise_and(j, 1), 2), jnp.right_shift(j, 1))


def lanes_of(block, rank):
    return pl.ds(pl.multiple_of(place_of(block, rank) * BLOCK, BLOCK), BLOCK)


def rope_kernel(info, qkv, cos, sin, out):
    rank = info[0]

    @pl.loop(0, SLOT_LEN // BLOCK)
    def _(block):
        source = lanes_of(block, rank)
        target = pl.ds(pl.multiple_of(block * BLOCK, BLOCK), BLOCK)
        c, s = cos[:, target], sin[:, target]
        for head in range(HEADS + 1):
            first = qkv[pl.ds(head * HD, HALF), source]
            second = qkv[pl.ds(head * HD + HALF, HALF), source]
            scale = MULTIPLIER if head < HEADS else 1.0
            out[pl.ds(head * HD, HALF), target] = ((first * c - second * s).astype(BF16) * scale).astype(BF16)
            out[pl.ds(head * HD + HALF, HALF), target] = ((second * c + first * s).astype(BF16) * scale).astype(BF16)
        rest = (HEADS + 1) * HD
        out[pl.ds(rest, HD), target] = qkv[pl.ds(rest, HD), source].astype(BF16)


KEYS = SLOT_LEN + LEAD
K_AT = HEADS * HD
V_AT = K_AT + HD


def upright(x):
    return x.astype(F32).T.astype(BF16)


def causal():
    keys = lax.broadcasted_iota(jnp.int32, (CHUNK, CHUNK), 0)
    queries = lax.broadcasted_iota(jnp.int32, (CHUNK, CHUNK), 1)
    return keys <= queries


def key_range(step):
    last = step == SLOT_LEN // CHUNK - 1
    low = jnp.where(last, KEYS // CHUNK - 1, 0)
    high = jnp.where(last, KEYS // CHUNK, step + 2)
    return low, high


def chunk_of(i):
    return pl.ds(pl.multiple_of(i * CHUNK, CHUNK), CHUNK)


def head_rows(h):
    return pl.ds(pl.multiple_of(h * HD, HD), HD)


def attend_kernel(info, qkv, halo, heads_out, lse_out, peak_out, k_up, v_flat, scores):
    rank = info[0]
    k_up[pl.ds(0, LEAD), :] = upright(halo[pl.ds(0, HD), :])
    v_flat[:, pl.ds(0, LEAD)] = halo[pl.ds(HD, HD), :]
    v_flat[:, pl.ds(LEAD, SLOT_LEN)] = qkv[pl.ds(V_AT, HD), :]

    @pl.loop(0, SLOT_LEN // CHUNK)
    def _(i):
        k_up[pl.ds(pl.multiple_of(LEAD + i * CHUNK, CHUNK), CHUNK), :] = upright(
            qkv[pl.ds(K_AT, HD), chunk_of(i)]
        )

    peak_out[...] = jnp.full(peak_out.shape, NEGATIVE, F32)
    lse_out[...] = jnp.zeros(lse_out.shape, F32)

    @pl.loop(0, HEADS)
    def _(h):
        @pl.loop(0, SLOT_LEN // CHUNK)
        def _(step):
            low, high = key_range(step)
            query = qkv[head_rows(h), chunk_of(step)]

            def raw(kc):
                return jnp.dot(k_up[chunk_of(kc), :], query, preferred_element_type=F32)

            def first(kc, top):
                s = raw(kc)
                scores[chunk_of(kc - low), :] = s
                return jnp.maximum(top, jnp.max(s, axis=0, keepdims=True))

            s = jnp.where(causal(), raw(high - 1), NEGATIVE)
            scores[chunk_of(high - 1 - low), :] = s
            top = lax.fori_loop(low, high - 1, first, jnp.max(s, axis=0, keepdims=True))

            def second(kc, total):
                e = jnp.exp(scores[chunk_of(kc), :] - top)
                scores[chunk_of(kc), :] = e
                return total + jnp.sum(e, axis=0, keepdims=True)

            total = lax.fori_loop(0, high - low, second, jnp.zeros((1, CHUNK), F32))
            inverse = 1.0 / total

            def third(kc, mixed):
                probs = (scores[chunk_of(kc), :] * inverse).astype(BF16)
                return mixed + jnp.dot(
                    v_flat[:, chunk_of(kc + low)], probs, preferred_element_type=F32
                )

            mixed = lax.fori_loop(0, high - low, third, jnp.zeros((HD, CHUNK), F32))
            mixed = mixed.astype(BF16)
            for part in range(CHUNK // BLOCK):
                heads_out[head_rows(h), lanes_of(step * (CHUNK // BLOCK) + part, rank)] = mixed[
                    :, part * BLOCK : (part + 1) * BLOCK
                ]
            lse_out[pl.ds(h, 1), chunk_of(step)] = top + jnp.log(total)
            last = step == SLOT_LEN // CHUNK - 1
            start = jnp.where(last, 0, LEAD + step * CHUNK)
            alive = jnp.where(last, info[2], info[1])
            spots = lax.broadcasted_iota(jnp.int32, (1, CHUNK), 1) + start
            best = jnp.max(jnp.where(spots < alive, top, NEGATIVE), axis=1, keepdims=True)
            peak_out[pl.ds(h, 1), :] = jnp.maximum(peak_out[pl.ds(h, 1), :], best)


def attend_back_kernel(
    info, qkv, halo, upstream, lse, cos, sin, dq_out, dkv_out, halo_out,
    k_up, v_up, k_flat, probs_s, grads_s, dk_s, dv_s, up_abs,
):
    rank = info[0]
    k_up[pl.ds(0, LEAD), :] = upright(halo[pl.ds(0, HD), :])
    v_up[pl.ds(0, LEAD), :] = upright(halo[pl.ds(HD, HD), :])
    k_flat[:, pl.ds(0, LEAD)] = halo[pl.ds(0, HD), :]
    k_flat[:, pl.ds(LEAD, SLOT_LEN)] = qkv[pl.ds(K_AT, HD), :]

    @pl.loop(0, SLOT_LEN // CHUNK)
    def _(i):
        rows = pl.ds(pl.multiple_of(LEAD + i * CHUNK, CHUNK), CHUNK)
        k_up[rows, :] = upright(qkv[pl.ds(K_AT, HD), chunk_of(i)])
        v_up[rows, :] = upright(qkv[pl.ds(V_AT, HD), chunk_of(i)])

    @pl.loop(0, SLOT_LEN // BLOCK)
    def _(block):
        target = pl.ds(pl.multiple_of(block * BLOCK, BLOCK), BLOCK)
        up_abs[:, target] = upstream[:, lanes_of(block, rank)]

    dk_s[...] = jnp.zeros(dk_s.shape, F32)
    dv_s[...] = jnp.zeros(dv_s.shape, F32)

    @pl.loop(0, HEADS)
    def _(h):
        @pl.loop(0, SLOT_LEN // CHUNK)
        def _(step):
            low, high = key_range(step)
            here = chunk_of(step)
            query = qkv[head_rows(h), here]
            grad = up_abs[head_rows(h), here]
            query_up, grad_up = upright(query), upright(grad)
            logs = lse[pl.ds(h, 1), here]

            def one(kc, masked):
                s = jnp.dot(k_up[chunk_of(kc), :], query, preferred_element_type=F32)
                p = jnp.exp(s - logs)
                if masked:
                    p = jnp.where(causal(), p, 0.0)
                g = jnp.dot(v_up[chunk_of(kc), :], grad, preferred_element_type=F32)
                probs_s[chunk_of(kc - low), :] = p
                grads_s[chunk_of(kc - low), :] = g
                dv_s[chunk_of(kc), :] += jnp.dot(
                    p.astype(BF16), grad_up, preferred_element_type=F32
                )
                return jnp.sum(p * g, axis=0, keepdims=True)

            delta = one(high - 1, True)
            delta = lax.fori_loop(low, high - 1, lambda kc, d: d + one(kc, False), delta)

            def two(kc, dq):
                p, g = probs_s[chunk_of(kc - low), :], grads_s[chunk_of(kc - low), :]
                ds = (p * (g - delta)).astype(BF16)
                dk_s[chunk_of(kc), :] += jnp.dot(ds, query_up, preferred_element_type=F32)
                return dq + jnp.dot(k_flat[:, chunk_of(kc)], ds, preferred_element_type=F32)

            dq = lax.fori_loop(low, high, two, jnp.zeros((HD, CHUNK), F32)) * MULTIPLIER
            c, s = cos[:, here], sin[:, here]
            u1, u2 = dq[:HALF], dq[HALF:]
            t1, t2 = (u1 * c + u2 * s).astype(BF16), (u2 * c - u1 * s).astype(BF16)
            for part in range(CHUNK // BLOCK):
                there = lanes_of(step * (CHUNK // BLOCK) + part, rank)
                cut = slice(part * BLOCK, (part + 1) * BLOCK)
                dq_out[pl.ds(pl.multiple_of(h * HD, HD), HALF), there] = t1[:, cut]
                dq_out[pl.ds(pl.multiple_of(h * HD + HALF, HALF), HALF), there] = t2[:, cut]

    halo_out[pl.ds(0, HD), :] = dk_s[pl.ds(0, LEAD), :].T.astype(BF16)
    halo_out[pl.ds(HD, HD), :] = dv_s[pl.ds(0, LEAD), :].T.astype(BF16)

    @pl.loop(0, SLOT_LEN // CHUNK)
    def _(i):
        rows = pl.ds(pl.multiple_of(LEAD + i * CHUNK, CHUNK), CHUNK)
        dkv_out[pl.ds(0, HD), chunk_of(i)] = dk_s[rows, :].T
        dkv_out[pl.ds(HD, HD), chunk_of(i)] = dv_s[rows, :].T


def finish_kernel(info, dkv, halo, cos, sin, out):
    rank = info[0]
    owned = (SLOT_LEN - LEAD) // BLOCK
    for block in range(SLOT_LEN // BLOCK):
        source = pl.ds(block * BLOCK, BLOCK)
        target = lanes_of(block, rank)
        c, s = cos[:, source], sin[:, source]
        u1, u2 = dkv[pl.ds(0, HALF), source], dkv[pl.ds(HALF, HALF), source]
        rest = dkv[pl.ds(HD, HD), source]
        if block >= owned:
            part = pl.ds((block - owned) * BLOCK, BLOCK)
            u1 = u1 + halo[pl.ds(0, HALF), part].astype(F32)
            u2 = u2 + halo[pl.ds(HALF, HALF), part].astype(F32)
            rest = rest + halo[pl.ds(HD, HD), part].astype(F32)
        out[pl.ds(0, HALF), target] = (u1 * c + u2 * s).astype(BF16)
        out[pl.ds(HALF, HALF), target] = (u2 * c - u1 * s).astype(BF16)
        out[pl.ds(HD, HD), target] = rest.astype(BF16)


def call(kernel, info, args, outs, scratch, name):
    spec = pl.BlockSpec(memory_space=pltpu.VMEM)
    return pl.pallas_call(
        kernel,
        out_shape=[jax.ShapeDtypeStruct(s, d) for s, d in outs],
        in_specs=[pl.BlockSpec(memory_space=pltpu.SMEM)] + [spec] * len(args),
        out_specs=[spec] * len(outs),
        scratch_shapes=[pltpu.VMEM(s, d) for s, d in scratch],
        compiler_params=pltpu.CompilerParams(vmem_limit_bytes=40 * 2**20),
        cost_estimate=FREE,
        name=name,
    )(info, *args)


def hidden_kernel(rows, gate_w, up_w, gate_out, up_out, hidden_out):
    gate, up = dot(rows[...], gate_w[...], 1, 0), dot(rows[...], up_w[...], 1, 0)
    gate_out[...], up_out[...] = gate, up
    hidden_out[...] = (gate * jax.nn.sigmoid(gate) * up).astype(BF16)


def hidden_back_kernel(rows, weights, gates, ups, gate_out, up_out):
    grad = dot(rows[...], weights[...], 1, 1)
    gate = gates[...]
    sig = jax.nn.sigmoid(gate)
    gate_out[...] = (grad * ups[...] * sig * (1.0 + gate * (1.0 - sig))).astype(BF16)
    up_out[...] = (grad * gate * sig).astype(BF16)


def ffn_call(kernel, rows, weights, width, kinds, held, name):
    high, wide = min(512, rows.shape[0]), min(512, width)
    depth, steps = rows.shape[1], width // wide
    tile = pl.BlockSpec((high, wide), lambda n, m: (m, n))
    if held:
        specs = [pl.BlockSpec((wide, depth), lambda n, m: (n, 0))]
    else:
        specs = [pl.BlockSpec((depth, wide), lambda n, m: (0, n)),
                 pl.BlockSpec((depth, wide), lambda n, m: (0, n + steps))]
    return pl.pallas_call(
        kernel,
        out_shape=[jax.ShapeDtypeStruct((rows.shape[0], width), kind) for kind in kinds],
        grid=(steps, rows.shape[0] // high),
        in_specs=[pl.BlockSpec((high, depth), lambda n, m: (m, 0))] + specs + [tile] * len(held),
        out_specs=[tile] * len(kinds),
        compiler_params=pltpu.CompilerParams(vmem_limit_bytes=56 * 2**20),
        cost_estimate=FREE,
        name=name,
    )(rows, *([weights] * len(specs)), *held)


def outer_kernel(right_dim, left, right, out):
    out[...] = dot(left[...], right[...], 0, right_dim).astype(BF16)


def outer_gain_kernel(right_dim, cut, left, right, weights, out, gain):
    total = dot(left[...], right[...], 0, right_dim)
    out[...] = total.astype(BF16)
    scaled = total * weights[:, cut[0] : cut[1]].astype(F32)
    gain[...] = jnp.broadcast_to(jnp.sum(scaled, axis=1, keepdims=True), gain.shape)


def outer(left, right, right_dim, weights=None, cut=None):
    depth, high = left.shape
    wide = right.shape[1 - right_dim]
    rows, cols = min(512, high), min(1024, wide)
    right_block = (depth, cols) if right_dim == 0 else (cols, depth)
    right_map = (lambda n, m: (0, n)) if right_dim == 0 else (lambda n, m: (n, 0))
    specs = [pl.BlockSpec((depth, rows), lambda n, m: (0, m)), pl.BlockSpec(right_block, right_map)]
    outs = [jax.ShapeDtypeStruct((high, wide), BF16)]
    out_specs = [pl.BlockSpec((rows, cols), lambda n, m: (m, n))]
    args, kernel = (left, right), functools.partial(outer_kernel, right_dim)
    if weights is not None:
        args, kernel = (left, right, weights), functools.partial(outer_gain_kernel, right_dim, cut)
        specs.append(pl.BlockSpec((rows, weights.shape[1]), lambda n, m: (m, 0)))
        outs.append(jax.ShapeDtypeStruct((high, 128), F32))
        out_specs.append(pl.BlockSpec((rows, 128), lambda n, m: (m, 0)))
    return pl.pallas_call(
        kernel,
        out_shape=outs,
        grid=(wide // cols, high // rows),
        in_specs=specs,
        out_specs=out_specs,
        compiler_params=pltpu.CompilerParams(vmem_limit_bytes=56 * 2**20),
        cost_estimate=FREE,
        name="outer",
    )(*args)


def norm_back(values, scale, upstream):
    mean_term = jnp.mean(values * upstream, axis=1, keepdims=True)
    return scale * upstream - values * (scale * scale * scale) * mean_term


def shards(
    layer_in, lengths, clip_level, attn_gain, w_query, w_key, w_value, w_out,
    mlp_gain, w_gate, w_up, w_down, cotangent,
):
    tok_rows, width = layer_in.shape
    z_rank, y_rank = lax.axis_index("z"), lax.axis_index("y")
    rank = (y_rank * 2 + lax.axis_index("x")) * 2 + lax.axis_index("c")
    slots = lengths.shape[0]
    next_slot = (z_rank + 1) % slots
    info = jnp.stack(
        (rank, lax.dynamic_index_in_dim(lengths, z_rank, keepdims=False),
         lax.dynamic_index_in_dim(lengths, next_slot, keepdims=False))
    ).astype(jnp.int32)
    inner = rank * tok_rows + jnp.arange(tok_rows, dtype=jnp.int32) + LEAD
    own_mask = jnp.where(inner < SLOT_LEN, inner < info[1], inner - SLOT_LEN < info[2])
    own_mask = own_mask.astype(F32)[:, None]
    spots = ((jnp.arange(SLOT_LEN, dtype=jnp.int32) + LEAD) % SLOT_LEN).astype(F32)
    freq = THETA ** (-(jnp.arange(HALF, dtype=F32) * 2.0 / HD))
    angles = spots[None, :] * freq[:, None]
    cos, sin = jnp.cos(angles), jnp.sin(angles)
    def heads_part(which):
        return jnp.concatenate(
            (half_of(w_out, which, 0).T, half_of(w_query, which, 1), half_of(w_key, which, 1),
             half_of(w_value, which, 1)), 1
        )

    def ffn_part(which):
        return jnp.concatenate((half_of(w_gate, which, 1), half_of(w_up, which, 1)), 1)

    other_y = 1 - y_rank
    heads_w = ordered(heads_part(y_rank), swap(heads_part(other_y), "y"), y_rank, 0)
    full_heads = lax.all_gather(heads_w, "z", axis=0, tiled=True)
    out_cols = HEADS * HD
    heads_cut = (out_cols, full_heads.shape[1])

    ffn_own, ffn_sent = tie(ffn_part(y_rank), ffn_part(other_y))
    ffn_w = ordered(ffn_own, swap(ffn_sent, "y"), y_rank, 0)
    layer_f = layer_in.astype(F32)
    scale_one = lax.rsqrt(jnp.mean(layer_f * layer_f, axis=1, keepdims=True) + EPSILON)
    normal_one = rounded(layer_f * scale_one)
    gain_one = attn_gain.astype(F32)
    acts = gather_one(after((normal_one * gain_one[None, :]).astype(BF16), heads_w))
    acts = gather_two(acts)
    full_heads, ffn_w, *acts = tie(full_heads, ffn_w, *acts)
    full_out, full_qkv = full_heads[:, :out_cols], full_heads[:, out_cols:]
    acts_one = gather_three(acts)
    full_ffn = lax.all_gather(ffn_w, "z", axis=0, tiled=True)

    grad_out = cotangent.astype(F32)
    down_in = (RESIDUAL * own_mask * grad_out).astype(BF16)
    back_rows = gather_one(down_in)
    rows = acts_one.shape[0]
    flat = dot(full_qkv, acts_one, 0, 1)
    (qkv,) = call(
        rope_kernel, info, (flat, cos, sin), [((flat.shape[0], rows), BF16)], [], "rope"
    )
    halo = along(qkv[K_AT:, SLOT_LEN - LEAD :], 1)
    qkv, halo, *back_rows = tie(qkv, halo, *back_rows)
    down_other = swap(after(half_of(w_down, other_y, 0), back_rows[2], back_rows[3]), "y")
    back_rows = gather_two(back_rows)
    heads, lse, peak = call(
        attend_kernel, info, (qkv, halo),
        [((HEADS * HD, rows), BF16), ((8, rows), F32), ((8, 128), F32)],
        [((KEYS, HD), BF16), ((HD, KEYS), BF16), ((SLOT_LEN, CHUNK), F32)],
        "attend",
    )
    heads, down_other, *back_rows = tie(heads, down_other, *back_rows)
    down_w = ordered(half_of(w_down, y_rank, 0), down_other, y_rank, 1)

    terms = [(heads, full_heads, 0, 1, (0, out_cols))]
    own_peak = peak[:HEADS]
    came, other_peak = tie(swap(product(terms, 1), "c"), swap(own_peak, "y"))
    branch = spread_one(terms, came)
    head_peak = over_z(ordered(own_peak, other_peak, y_rank, 0), jnp.maximum)
    down_rows = gather_three(back_rows)
    *got, down_rows, down_w, head_peak = tie(*branch[2:4], down_rows, down_w, head_peak)
    head_peak = head_peak[:, 0]
    branch = spread_two((*branch[:2], *got))
    full_down = lax.all_gather(down_w, "z", axis=1, tiled=True)
    gain_two = mlp_gain.astype(F32)
    narrow = (tok_rows, width // 2)
    resid, scale_two, *acts = row_call(
        residual_kernel, (*branch[:4], layer_in, own_mask, gain_two[None, :]),
        [((tok_rows, width), F32), ((tok_rows, 1), F32), ((tok_rows, width), BF16),
         (narrow, BF16), (narrow, BF16)], "residual",
    )
    acts = gather_one(acts[0], acts[1:])
    full_ffn, *acts = tie(full_ffn, *acts)
    acts = gather_two(acts)
    acts_two = gather_three(acts)

    hid = full_ffn.shape[1] // 2
    gate_proj, up_proj, hidden = ffn_call(
        hidden_kernel, acts_two, full_ffn, hid, (F32, F32, BF16), (), "hidden"
    )

    def reduced(grad, axis):
        return lax.psum_scatter(grad, "z", scatter_dimension=axis, tiled=True)

    def traded(total, axis, *behind):
        total = after(total, *behind)
        return half_of(total, y_rank, axis), swap(half_of(total, other_y, axis), "y")

    (down_part,) = outer(hidden, down_rows, 0)
    down_sum = reduced(down_part, 1)
    down_rows = after(down_rows, down_part)
    gate_grad, up_grad = ffn_call(
        hidden_back_kernel, down_rows, full_down, hid, (BF16, BF16), (gate_proj, up_proj),
        "hidden_back",
    )
    terms = [(gate_grad, full_ffn, 1, 1, None, 0), (up_grad, full_ffn, 1, 1, None, 1)]
    *norm_two, acts_two = spread_one(terms, None, acts_two)
    ffn_parts = [outer(acts_two, grad, 0)[0] for grad in (gate_grad, up_grad)]
    *got, ffn_parts[0], ffn_parts[1] = tie(*norm_two[2:4], *ffn_parts)
    one_sum, two_sum = [reduced(part, 0) for part in ffn_parts]
    norm_two = spread_two((*norm_two[:2], *got))
    gain_two_part, grad_resid, *mixed = row_call(
        residual_back_kernel,
        (*norm_two[:4], cotangent, resid, scale_two, gain_two[None, :], own_mask),
        [((8, width), F32), ((tok_rows, width), F32), ((tok_rows, width), BF16), (narrow, BF16),
         (narrow, BF16)], "residual_back",
    )
    mixed_in, hidden = tie(mixed[0], hidden)
    mixed = gather_one(mixed_in, mixed[1:])
    terms = [(hidden, full_down, 1, 0, None)]
    *got, high_part = tie(*mixed[2:4], product(terms, 1))
    mixed = gather_two((*mixed[:2], *got))
    low_part = product(terms, 0, swap(high_part, "c"))
    a1, b1, *low_part = tie(*mixed[5:], *low_part)
    mixed = (*mixed[:5], a1, b1)
    second = (*low_part[:2], swap(low_part[2], "x"), swap(low_part[3], "y"))
    mixed_rows = gather_three(mixed)
    mixed_rows, down_sum, one_sum = tie(mixed_rows, down_sum, one_sum)
    down_own, down_other = traded(down_sum, 1)
    one_own, one_other = traded(one_sum, 0)

    heads_grad = dot(full_out, mixed_rows, 0, 1).astype(BF16)
    dq, dkv, back = call(
        attend_back_kernel, info, (qkv, halo, heads_grad, lse, cos, sin),
        [((HEADS * HD, rows), BF16), ((2 * HD, rows), F32), ((2 * HD, LEAD), BF16)],
        [((KEYS, HD), BF16), ((KEYS, HD), BF16), ((HD, KEYS), BF16),
         ((SLOT_LEN, CHUNK), F32), ((SLOT_LEN, CHUNK), F32),
         ((KEYS, HD), F32), ((KEYS, HD), F32), ((HEADS * HD, SLOT_LEN), BF16)],
        "attend_back",
    )
    back, down_other, one_other, *got = tie(back, down_other, one_other, *second[2:4])
    back_sent = along(back, -1)
    left, right, *sent = fold(*second[:2], *got)
    (out_part,) = outer(mixed_rows, heads, 1)
    dkv, back_sent, out_part, *sent = tie(dkv, back_sent, out_part, *sent)
    out_sum = reduced(out_part, 0)
    second = left, right, swap(sent[0], "y"), swap(sent[1], "x")
    (dkv_done,) = call(
        finish_kernel, info, (dkv, back_sent, cos, sin), [((2 * HD, rows), BF16)], [], "finish"
    )
    dqkv = jnp.concatenate((dq, dkv_done))
    terms = [(dqkv, full_heads, 0, 1, heads_cut)]
    high_part, acts_one, two_sum = tie(product(terms, 1), acts_one, two_sum)
    two_own, two_sent = half_of(two_sum, y_rank, 0), half_of(two_sum, other_y, 0)
    qkv_part, sums = outer(acts_one, dqkv, 1, full_heads, heads_cut)
    came, qkv_part, sums, *got = tie(swap(high_part, "c"), qkv_part, sums, *second[2:4])
    branch_two = spread_three((*second[:2], *got))
    result = resid + RESIDUAL * own_mask * branch_two
    norm_one = spread_one(terms, came)
    qkv_sum = reduced(qkv_part, 0)
    gains = jnp.stack((sums[:, 0] / gain_one, jnp.sum(gain_two_part, axis=0)))
    gains = over_z(gains, jnp.add).reshape(2, lax.axis_size("z"), 2, 2, 2, -1)

    def halved(gains, dim, axis):
        at = lax.axis_index(axis)
        return (lax.dynamic_index_in_dim(gains, at, dim, keepdims=False),
                lax.dynamic_index_in_dim(gains, 1 - at, dim, keepdims=False))

    kept, sent = halved(gains, 4, "c")
    kept, sent = halved(kept + swap(sent, "c"), 3, "x")
    *got, out_sum = tie(*norm_one[2:4], out_sum)
    out_own, out_sent = half_of(out_sum, y_rank, 0), half_of(out_sum, other_y, 0)
    norm_one = spread_two((*norm_one[:2], *got), sent, out_sent, two_sent)
    sent, out_sent, two_sent = norm_one[4:]
    kept, sent = halved(kept + swap(sent, "x"), 2, "y")
    gains = kept + swap(sent, "y")
    two_other, out_other = swap(two_sent, "y"), swap(out_sent, "y")
    *norm_one, qkv_sum = tie(*norm_one[:4], qkv_sum)
    own, other = traded(qkv_sum, 0)
    (grad_input,) = row_call(
        input_back_kernel, (*norm_one, grad_resid, layer_in, scale_one, gain_one[None, :]),
        [((tok_rows, width), BF16)], "input_back",
    )
    gains = lax.dynamic_index_in_dim(gains, z_rank, 1, keepdims=False)

    down_grad = ordered(down_own, down_other, y_rank, 0).astype(F32)
    gate_w_grad = ordered(one_own, one_other, y_rank, 1).astype(F32)
    up_w_grad = ordered(two_own, two_other, y_rank, 1).astype(F32)
    out_grad = ordered(out_own.T, out_other.T, y_rank, 0).astype(F32)

    def columns(start, stop):
        return ordered(own[:, start:stop], other[:, start:stop], y_rank, 1).astype(F32)

    query_grad = columns(0, K_AT)
    key_grad = columns(K_AT, V_AT)
    value_grad = columns(V_AT, V_AT + HD)

    level = clip_level[0].astype(F32) * LEVEL_UNIT
    factor = level / jnp.maximum(level, head_peak)
    query_clipped = w_query.astype(F32) * jnp.repeat(jnp.sqrt(factor), HD)[None, :]
    kv_factor = jnp.min(factor.reshape(-1, HEADS), axis=1)
    key_clipped = w_key.astype(F32) * jnp.repeat(jnp.sqrt(kv_factor), HD)[None, :]
    return (
        result.astype(BF16),
        grad_input,
        gains[0],
        query_grad,
        key_grad,
        value_grad,
        out_grad,
        gains[1],
        gate_w_grad,
        up_w_grad,
        down_grad,
        query_clipped,
        key_clipped,
    )


def solution(mesh):
    fsdp, tp = mesh.shape["fsdp"], mesh.shape["tp"]
    fine = Mesh(mesh.devices.reshape(fsdp // 2, 2, tp // 2, 2), EVERY)
    rows, cols = ("z", "y"), ("x", "c")
    tokens, down, across = P(EVERY, None), P(rows, cols), P(cols, rows)
    in_specs = (
        tokens, P(), P(), P(), down, down, down, across, P(), down, down, across, tokens,
    )
    out_specs = (
        tokens, tokens, P(EVERY), down, down, down, across, P(EVERY), down, down, across,
        down, down,
    )
    return jax.shard_map(shards, mesh=fine, in_specs=in_specs, out_specs=out_specs, check_vma=False)
```

```python
import functools

import jax
import jax.numpy as jnp
from jax import lax
from jax.experimental import pallas as pl
from jax.experimental.pallas import tpu as pltpu
from jax.sharding import Mesh
from jax.sharding import PartitionSpec as P

HD = 64
HALF = HD // 2
SLOT_LEN = 2048
LEAD = 512
CHUNK = 512
BLOCK = 256
HEADS = 4

EPSILON = 1e-05
THETA = 10000000.0
MULTIPLIER = 0.015625
RESIDUAL = 0.22
LEVEL_UNIT = 0.125
NEGATIVE = -1e30
GROUP = ("y", "x", "c")
EVERY = ("z", "y", "x", "c")
F32 = jnp.float32
BF16 = jnp.bfloat16
FREE = pl.CostEstimate(flops=0, bytes_accessed=0, transcendentals=0)


def rounded(x):
    return lax.reduce_precision(x, exponent_bits=8, mantissa_bits=7)


def swap(x, axis):
    return lax.ppermute(x, axis, [(0, 1), (1, 0)])


def along(x, by):
    peers = lax.axis_size("z")
    return lax.ppermute(x, "z", [(i, (i + by) % peers) for i in range(peers)])


def dot(left, right, left_dim, right_dim):
    return lax.dot_general(
        left, right, (((left_dim,), (right_dim,)), ((), ())), preferred_element_type=F32
    )


def half_of(x, which, axis):
    size = x.shape[axis] // 2
    return lax.dynamic_slice_in_dim(x, which * size, size, axis)


def ordered(own, other, rank, axis):
    return jnp.where(
        rank == 0,
        jnp.concatenate((own, other), axis=axis),
        jnp.concatenate((other, own), axis=axis),
    )


def after(x, *others):
    return lax.optimization_barrier((x, *others))[0]


def tie(*xs):
    return lax.optimization_barrier(xs)


def gather_one(v, halves=None):
    half = v.shape[1] // 2
    halves = (v[:, :half], v[:, half:]) if halves is None else halves
    return v, swap(v, "c"), swap(halves[0], "x"), swap(halves[1], "y")


def gather_two(state):
    v, near, a01, b10 = state
    half = v.shape[1] // 2
    a1 = swap(jnp.concatenate((v[:, :half], a01)), "y")
    b1 = swap(jnp.concatenate((v[:, half:], b10)), "x")
    second = swap(jnp.concatenate((a01, b10)), "c")
    return v, near, a01, b10, second, a1, b1


def gather_three(state):
    size, half = state[0].shape[0], state[0].shape[1] // 2
    state = (state[0], *tie(*state[1:]))
    third = swap(jnp.concatenate(state[5:]), "c")
    spots = (
        (0, 0, size, 0, 0), (1, 0, size, 4 * size, 0), (2, 0, size, size, 0),
        (3, 0, size, 2 * size, half), (4, 0, size, 5 * size, 0),
        (4, size, size, 6 * size, half), (5, 0, 2 * size, 2 * size, 0),
        (6, 0, size, size, half), (6, size, size, 3 * size, half),
        (7, 0, 2 * size, 6 * size, 0), (7, 2 * size, size, 5 * size, half),
        (7, 3 * size, size, 7 * size, half),
    )
    return place((*state, third), spots, 8 * size)


def place_kernel(spots, count, *refs):
    pieces, out, held = refs[:count], refs[count], refs[count + 1 : 2 * count + 1]
    load_sems, sems = refs[-2:]
    loads = [
        pltpu.make_async_copy(piece, here, load_sems.at[i])
        for i, (piece, here) in enumerate(zip(pieces, held, strict=True))
    ]
    for load in loads:
        load.start()
    copies = []
    for i, load in enumerate(loads):
        load.wait()
        for at, (piece, start, size, row, col) in enumerate(spots):
            if piece == i:
                source = held[piece]
                copy = pltpu.make_async_copy(
                    source.at[pl.ds(start, size), :],
                    out.at[pl.ds(row, size), pl.ds(col, source.shape[1])],
                    sems.at[at],
                )
                copy.start()
                copies.append(copy)
    for copy in copies:
        copy.wait()


def place(pieces, spots, count):
    number = len(pieces)
    return pl.pallas_call(
        functools.partial(place_kernel, spots, number),
        out_shape=jax.ShapeDtypeStruct((count, pieces[0].shape[1]), BF16),
        in_specs=[pl.BlockSpec(memory_space=pl.ANY)] * number,
        out_specs=pl.BlockSpec(memory_space=pltpu.HBM),
        scratch_shapes=[pltpu.VMEM(piece.shape, BF16) for piece in pieces]
        + [pltpu.SemaphoreType.DMA((number,)), pltpu.SemaphoreType.DMA((len(spots),))],
        compiler_params=pltpu.CompilerParams(vmem_limit_bytes=60 * 2**20),
        cost_estimate=FREE,
        name="place",
    )(*pieces)


def product_kernel(terms, keep, *refs):
    count = len(terms)
    step = pl.program_id(0)
    flipped = sum(term[0] == 0 for term in terms)
    scratch = refs[len(refs) - flipped :]
    total, used = None, 0
    for at, (left_dim, right_dim, cut) in enumerate(terms):
        left, right = refs[2 * at], refs[2 * at + 1]
        if left_dim == 0:
            store = scratch[used]
            used += 1

            @pl.when(step == 0)
            def _(left=left, store=store):
                store[...] = upright(left[...])

            left = store
        block = right[...] if cut is None else right[:, cut[0] : cut[1]]
        one = dot(left[...], block, 1, right_dim)
        total = one if total is None else total + one
    if not keep:
        refs[2 * count][...] = total.astype(BF16)
        return
    came, left_out, right_out, x_out, y_out = refs[2 * count : 2 * count + 5]
    total = total + came[...].astype(F32)
    blocks = total.reshape(2, 2, total.shape[0] // 4, total.shape[1])
    half = pl.num_programs(0) // 2

    @pl.when(step < half)
    def _():
        left_out[...] = blocks[:, 0]
        x_out[...] = blocks[:, 1].astype(BF16)

    @pl.when(step >= half)
    def _():
        right_out[...] = blocks[0]
        y_out[...] = blocks[1].astype(BF16)


def product(terms, part, came=None):
    tile = 512
    args, specs, kinds, scratch = [], [], [], []
    for left, right, left_dim, right_dim, cut, *block in terms:
        rows = left.shape[1 - left_dim] // 2
        depth = left.shape[left_dim]
        if left_dim == 1:
            specs.append(pl.BlockSpec((rows, depth), lambda n: (part, 0)))
        else:
            specs.append(pl.BlockSpec((depth, rows), lambda n: (0, part)))
            scratch.append(pltpu.VMEM((rows, depth), BF16))
        if right_dim == 1:
            width = right.shape[0]
            if block:
                specs.append(pl.BlockSpec((tile, depth), lambda n, at=block[0]: (n, at)))
            else:
                specs.append(pl.BlockSpec((tile, right.shape[1]), lambda n: (n, 0)))
        else:
            width = right.shape[1]
            specs.append(pl.BlockSpec((right.shape[0], tile), lambda n: (0, n)))
        args += [left, right]
        kinds.append((left_dim, right_dim, cut))
    if came is None:
        out_shape = jax.ShapeDtypeStruct((rows, width), BF16)
        out_specs = pl.BlockSpec((rows, tile), lambda n: (0, n))
    else:
        args.append(came)
        specs.append(pl.BlockSpec((rows, tile), lambda n: (0, n)))
        half = width // tile // 2
        shape = (2, rows // 4, width // 2)
        out_shape = [jax.ShapeDtypeStruct(shape, d) for d in (F32, F32, BF16, BF16)]
        first = pl.BlockSpec((2, rows // 4, tile), lambda n: (0, 0, jnp.minimum(n, half - 1)))
        last = pl.BlockSpec((2, rows // 4, tile), lambda n: (0, 0, jnp.maximum(n - half, 0)))
        out_specs = [first, last, first, last]
    return pl.pallas_call(
        functools.partial(product_kernel, kinds, came is not None),
        out_shape=out_shape,
        grid=(width // tile,),
        in_specs=specs,
        out_specs=out_specs,
        scratch_shapes=scratch,
        compiler_params=pltpu.CompilerParams(vmem_limit_bytes=56 * 2**20),
        cost_estimate=FREE,
        name="product",
    )(*args)


def spread_one(terms, came=None, *later):
    came = swap(product(terms, 1), "c") if came is None else came
    left, right, send_x, send_y = product(terms, 0, came)
    if later:
        send_x, send_y, *later = tie(send_x, send_y, *later)
    return left, right, swap(send_x, "x"), swap(send_y, "y"), *later


def fold_kernel(left, right, left_x, right_y, left_out, right_out, y_out, x_out):
    total = left[...] + left_x[...].astype(F32)
    left_out[...], y_out[...] = total[0], total[1].astype(BF16)
    total = right[...] + right_y[...].astype(F32)
    right_out[...], x_out[...] = total[0], total[1].astype(BF16)


def fold(*parts):
    rows, cols = parts[0].shape[1:]
    size = rows // 2
    return pl.pallas_call(
        fold_kernel,
        out_shape=[jax.ShapeDtypeStruct((rows, cols), d) for d in (F32, F32, BF16, BF16)],
        grid=(2,),
        in_specs=[pl.BlockSpec((2, size, cols), lambda i: (0, i, 0))] * 4,
        out_specs=[pl.BlockSpec((size, cols), lambda i: (i, 0))] * 4,
        cost_estimate=FREE,
        name="fold",
    )(*parts)


def spread_two(state, *extra):
    left, right, send_y, send_x = fold(*state[:4])
    if extra:
        send_y, send_x, *extra = tie(send_y, send_x, *extra)
    return left, right, swap(send_y, "y"), swap(send_x, "x"), *extra


def spread_three(state):
    left, right, left_y, right_x = state[:4]
    return jnp.concatenate((left + left_y.astype(F32), right + right_x.astype(F32)), axis=1)


def joined(left, right, left_y, right_x):
    return jnp.concatenate(
        (left[...] + left_y[...].astype(F32), right[...] + right_x[...].astype(F32)), axis=1
    )


def store_halves(value, out, left_out, right_out):
    half = value.shape[1] // 2
    out[...], left_out[...], right_out[...] = value, value[:, :half], value[:, half:]


def residual_kernel(*refs):
    values, mask, gain = (ref[...] for ref in refs[4:7])
    resid_out, scale_out = refs[7:9]
    resid = values.astype(F32) + RESIDUAL * mask * joined(*refs[:4])
    scale = lax.rsqrt(jnp.mean(resid * resid, axis=1, keepdims=True) + EPSILON)
    resid_out[...], scale_out[...] = resid, scale
    normal = (resid * scale).astype(BF16).astype(F32)
    store_halves((normal * gain).astype(BF16), *refs[9:12])


def residual_back_kernel(*refs):
    base, values, scale, gain, mask = (ref[...] for ref in refs[4:9])
    sums, grad_out = refs[9:11]
    upstream = joined(*refs[:4])
    normal = (values * scale).astype(BF16).astype(F32)

    @pl.when(pl.program_id(0) == 0)
    def _():
        sums[...] = jnp.zeros(sums.shape, F32)

    share = normal * upstream
    sums[...] += jnp.sum(share.reshape(-1, 8, share.shape[1]), axis=0)
    grad = base.astype(F32) + norm_back(values, scale, gain * upstream)
    grad_out[...] = grad
    store_halves((RESIDUAL * mask * grad).astype(BF16), *refs[11:14])


def input_back_kernel(*refs):
    base, values, scale, gain = (ref[...] for ref in refs[4:8])
    grad = base + norm_back(values.astype(F32), scale, gain * joined(*refs[:4]))
    refs[8][...] = grad.astype(BF16)


def row_call(kernel, args, outs, name):
    rows = args[0].shape[0]
    size = rows // 4

    def spec(shape):
        if shape[0] == rows:
            return pl.BlockSpec((size, shape[1]), lambda i: (i, 0))
        return pl.BlockSpec(shape, lambda i: (0, 0))

    return pl.pallas_call(
        kernel,
        out_shape=[jax.ShapeDtypeStruct(shape, kind) for shape, kind in outs],
        grid=(4,),
        in_specs=[spec(arg.shape) for arg in args],
        out_specs=[spec(shape) for shape, _ in outs],
        cost_estimate=FREE,
        name=name,
    )(*args)


def over_z(x, combine):
    peers, step = lax.axis_size("z"), 1
    assert peers & (peers - 1) == 0
    while step < peers:
        x = combine(x, along(x, step))
        step *= 2
    return x


def place_of(block, rank):
    j = jnp.bitwise_xor(block, rank)
    return jnp.bitwise_or(jnp.left_shift(jnp.bitwise_and(j, 1), 2), jnp.right_shift(j, 1))


def lanes_of(block, rank):
    return pl.ds(pl.multiple_of(place_of(block, rank) * BLOCK, BLOCK), BLOCK)


def rope_kernel(info, qkv, cos, sin, out):
    rank = info[0]

    @pl.loop(0, SLOT_LEN // BLOCK)
    def _(block):
        source = lanes_of(block, rank)
        target = pl.ds(pl.multiple_of(block * BLOCK, BLOCK), BLOCK)
        c, s = cos[:, target], sin[:, target]
        for head in range(HEADS + 1):
            first = qkv[pl.ds(head * HD, HALF), source]
            second = qkv[pl.ds(head * HD + HALF, HALF), source]
            scale = MULTIPLIER if head < HEADS else 1.0
            out[pl.ds(head * HD, HALF), target] = ((first * c - second * s).astype(BF16) * scale).astype(BF16)
            out[pl.ds(head * HD + HALF, HALF), target] = ((second * c + first * s).astype(BF16) * scale).astype(BF16)
        rest = (HEADS + 1) * HD
        out[pl.ds(rest, HD), target] = qkv[pl.ds(rest, HD), source].astype(BF16)


TOGETHER = 4
KEYS = SLOT_LEN + LEAD
K_AT = HEADS * HD
V_AT = K_AT + HD


def upright(x):
    return x.astype(F32).T.astype(BF16)


def causal():
    keys = lax.broadcasted_iota(jnp.int32, (CHUNK, CHUNK), 0)
    queries = lax.broadcasted_iota(jnp.int32, (CHUNK, CHUNK), 1)
    return keys <= queries


def key_range(step):
    last = step == SLOT_LEN // CHUNK - 1
    low = jnp.where(last, KEYS // CHUNK - 1, 0)
    high = jnp.where(last, KEYS // CHUNK, step + 2)
    return low, high


def chunk_of(i):
    return pl.ds(pl.multiple_of(i * CHUNK, CHUNK), CHUNK)


def head_rows(h):
    return pl.ds(pl.multiple_of(h * HD, HD), HD)


def attend_kernel(info, qkv, halo, heads_out, lse_out, peak_out, k_up, v_flat, scores):
    rank = info[0]
    k_up[pl.ds(0, LEAD), :] = upright(halo[pl.ds(0, HD), :])
    v_flat[:, pl.ds(0, LEAD)] = halo[pl.ds(HD, HD), :]
    v_flat[:, pl.ds(LEAD, SLOT_LEN)] = qkv[pl.ds(V_AT, HD), :]

    @pl.loop(0, SLOT_LEN // CHUNK)
    def _(i):
        k_up[pl.ds(pl.multiple_of(LEAD + i * CHUNK, CHUNK), CHUNK), :] = upright(
            qkv[pl.ds(K_AT, HD), chunk_of(i)]
        )

    peak_out[...] = jnp.full(peak_out.shape, NEGATIVE, F32)
    lse_out[...] = jnp.zeros(lse_out.shape, F32)

    @pl.loop(0, HEADS // TOGETHER)
    def _(group):
        @pl.loop(0, SLOT_LEN // CHUNK)
        def _(step):
            low, high = key_range(step)
            heads = [group * TOGETHER + i for i in range(TOGETHER)]
            query = [qkv[head_rows(h), chunk_of(step)] for h in heads]

            def raw(kc, i):
                return jnp.dot(k_up[chunk_of(kc), :], query[i], preferred_element_type=F32)

            def first(kc, tops):
                outs = []
                for i in range(TOGETHER):
                    s = raw(kc, i)
                    scores[i, chunk_of(kc - low)] = s
                    outs.append(jnp.maximum(tops[i], jnp.max(s, axis=0, keepdims=True)))
                return tuple(outs)

            tops = []
            for i in range(TOGETHER):
                s = jnp.where(causal(), raw(high - 1, i), NEGATIVE)
                scores[i, chunk_of(high - 1 - low)] = s
                tops.append(jnp.max(s, axis=0, keepdims=True))
            tops = lax.fori_loop(low, high - 1, first, tuple(tops))

            def second(kc, totals):
                outs = []
                for i in range(TOGETHER):
                    e = jnp.exp(scores[i, chunk_of(kc)] - tops[i])
                    scores[i, chunk_of(kc)] = e
                    outs.append(totals[i] + jnp.sum(e, axis=0, keepdims=True))
                return tuple(outs)

            totals = lax.fori_loop(0, high - low, second, (jnp.zeros((1, CHUNK), F32),) * TOGETHER)
            inverses = [1.0 / total for total in totals]

            def third(kc, mixed):
                outs = []
                for i in range(TOGETHER):
                    probs = (scores[i, chunk_of(kc)] * inverses[i]).astype(BF16)
                    more = jnp.dot(
                        v_flat[:, chunk_of(kc + low)], probs, preferred_element_type=F32
                    )
                    outs.append(mixed[i] + more)
                return tuple(outs)

            mixed_all = lax.fori_loop(
                0, high - low, third, (jnp.zeros((HD, CHUNK), F32),) * TOGETHER
            )
            last = step == SLOT_LEN // CHUNK - 1
            start = jnp.where(last, 0, LEAD + step * CHUNK)
            alive = jnp.where(last, info[2], info[1])
            spots = lax.broadcasted_iota(jnp.int32, (1, CHUNK), 1) + start
            for i, h in enumerate(heads):
                mixed = mixed_all[i].astype(BF16)
                for part in range(CHUNK // BLOCK):
                    there = lanes_of(step * (CHUNK // BLOCK) + part, rank)
                    heads_out[head_rows(h), there] = mixed[:, part * BLOCK : (part + 1) * BLOCK]
                lse_out[pl.ds(h, 1), chunk_of(step)] = tops[i] + jnp.log(totals[i])
                best = jnp.where(spots < alive, tops[i], NEGATIVE)
                best = jnp.max(best, axis=1, keepdims=True)
                peak_out[pl.ds(h, 1), :] = jnp.maximum(peak_out[pl.ds(h, 1), :], best)


def attend_back_kernel(
    info, qkv, halo, upstream, lse, cos, sin, dq_out, dkv_out, halo_out,
    k_up, v_up, k_flat, probs_s, grads_s, dk_s, dv_s, up_abs,
):
    rank = info[0]
    k_up[pl.ds(0, LEAD), :] = upright(halo[pl.ds(0, HD), :])
    v_up[pl.ds(0, LEAD), :] = upright(halo[pl.ds(HD, HD), :])
    k_flat[:, pl.ds(0, LEAD)] = halo[pl.ds(0, HD), :]
    k_flat[:, pl.ds(LEAD, SLOT_LEN)] = qkv[pl.ds(K_AT, HD), :]

    @pl.loop(0, SLOT_LEN // CHUNK)
    def _(i):
        rows = pl.ds(pl.multiple_of(LEAD + i * CHUNK, CHUNK), CHUNK)
        k_up[rows, :] = upright(qkv[pl.ds(K_AT, HD), chunk_of(i)])
        v_up[rows, :] = upright(qkv[pl.ds(V_AT, HD), chunk_of(i)])

    @pl.loop(0, SLOT_LEN // BLOCK)
    def _(block):
        target = pl.ds(pl.multiple_of(block * BLOCK, BLOCK), BLOCK)
        up_abs[:, target] = upstream[:, lanes_of(block, rank)]

    dk_s[...] = jnp.zeros(dk_s.shape, F32)
    dv_s[...] = jnp.zeros(dv_s.shape, F32)

    @pl.loop(0, HEADS // TOGETHER)
    def _(group):
        @pl.loop(0, SLOT_LEN // CHUNK)
        def _(step):
            low, high = key_range(step)
            here = chunk_of(step)
            heads = [group * TOGETHER + i for i in range(TOGETHER)]
            query = [qkv[head_rows(h), here] for h in heads]
            grad = [up_abs[head_rows(h), here] for h in heads]
            query_up, grad_up = [upright(x) for x in query], [upright(x) for x in grad]
            logs = [lse[pl.ds(h, 1), here] for h in heads]

            def spot(i, kc):
                return i, chunk_of(kc - low)

            def one(kc, masked):
                deltas, added = [], None
                for i in range(TOGETHER):
                    s = jnp.dot(k_up[chunk_of(kc), :], query[i], preferred_element_type=F32)
                    p = jnp.exp(s - logs[i])
                    if masked:
                        p = jnp.where(causal(), p, 0.0)
                    g = jnp.dot(v_up[chunk_of(kc), :], grad[i], preferred_element_type=F32)
                    probs_s[spot(i, kc)] = p
                    grads_s[spot(i, kc)] = g
                    more = jnp.dot(p.astype(BF16), grad_up[i], preferred_element_type=F32)
                    added = more if added is None else added + more
                    deltas.append(jnp.sum(p * g, axis=0, keepdims=True))
                dv_s[chunk_of(kc), :] += added
                return tuple(deltas)

            def both(kc, deltas):
                return tuple(d + e for d, e in zip(deltas, one(kc, False), strict=True))

            deltas = lax.fori_loop(low, high - 1, both, one(high - 1, True))

            def two(kc, dqs):
                outs, added = [], None
                for i in range(TOGETHER):
                    p, g = probs_s[spot(i, kc)], grads_s[spot(i, kc)]
                    ds = (p * (g - deltas[i])).astype(BF16)
                    more = jnp.dot(ds, query_up[i], preferred_element_type=F32)
                    added = more if added is None else added + more
                    outs.append(
                        dqs[i] + jnp.dot(k_flat[:, chunk_of(kc)], ds, preferred_element_type=F32)
                    )
                dk_s[chunk_of(kc), :] += added
                return tuple(outs)

            zero = jnp.zeros((HD, CHUNK), F32)
            dqs = lax.fori_loop(low, high, two, (zero,) * TOGETHER)
            c, s = cos[:, here], sin[:, here]
            for i in range(TOGETHER):
                dq = dqs[i] * MULTIPLIER
                u1, u2 = dq[:HALF], dq[HALF:]
                t1, t2 = (u1 * c + u2 * s).astype(BF16), (u2 * c - u1 * s).astype(BF16)
                at = heads[i] * HD
                for part in range(CHUNK // BLOCK):
                    there = lanes_of(step * (CHUNK // BLOCK) + part, rank)
                    cut = slice(part * BLOCK, (part + 1) * BLOCK)
                    dq_out[pl.ds(pl.multiple_of(at, HD), HALF), there] = t1[:, cut]
                    dq_out[pl.ds(pl.multiple_of(at + HALF, HALF), HALF), there] = t2[:, cut]

    halo_out[pl.ds(0, HD), :] = dk_s[pl.ds(0, LEAD), :].T.astype(BF16)
    halo_out[pl.ds(HD, HD), :] = dv_s[pl.ds(0, LEAD), :].T.astype(BF16)

    @pl.loop(0, SLOT_LEN // CHUNK)
    def _(i):
        rows = pl.ds(pl.multiple_of(LEAD + i * CHUNK, CHUNK), CHUNK)
        dkv_out[pl.ds(0, HD), chunk_of(i)] = dk_s[rows, :].T
        dkv_out[pl.ds(HD, HD), chunk_of(i)] = dv_s[rows, :].T


def finish_kernel(info, dkv, halo, cos, sin, out):
    rank = info[0]
    owned = (SLOT_LEN - LEAD) // BLOCK
    for block in range(SLOT_LEN // BLOCK):
        source = pl.ds(block * BLOCK, BLOCK)
        target = lanes_of(block, rank)
        c, s = cos[:, source], sin[:, source]
        u1, u2 = dkv[pl.ds(0, HALF), source], dkv[pl.ds(HALF, HALF), source]
        rest = dkv[pl.ds(HD, HD), source]
        if block >= owned:
            part = pl.ds((block - owned) * BLOCK, BLOCK)
            u1 = u1 + halo[pl.ds(0, HALF), part].astype(F32)
            u2 = u2 + halo[pl.ds(HALF, HALF), part].astype(F32)
            rest = rest + halo[pl.ds(HD, HD), part].astype(F32)
        out[pl.ds(0, HALF), target] = (u1 * c + u2 * s).astype(BF16)
        out[pl.ds(HALF, HALF), target] = (u2 * c - u1 * s).astype(BF16)
        out[pl.ds(HD, HD), target] = rest.astype(BF16)


def call(kernel, info, args, outs, scratch, name, limit=40):
    spec = pl.BlockSpec(memory_space=pltpu.VMEM)
    return pl.pallas_call(
        kernel,
        out_shape=[jax.ShapeDtypeStruct(s, d) for s, d in outs],
        in_specs=[pl.BlockSpec(memory_space=pltpu.SMEM)] + [spec] * len(args),
        out_specs=[spec] * len(outs),
        scratch_shapes=[pltpu.VMEM(s, d) for s, d in scratch],
        compiler_params=pltpu.CompilerParams(vmem_limit_bytes=limit * 2**20),
        cost_estimate=FREE,
        name=name,
    )(info, *args)


def hidden_kernel(rows, gate_w, up_w, gate_out, up_out, hidden_out):
    gate, up = dot(rows[...], gate_w[...], 1, 0), dot(rows[...], up_w[...], 1, 0)
    gate_out[...], up_out[...] = gate, up
    hidden_out[...] = (gate * jax.nn.sigmoid(gate) * up).astype(BF16)


def hidden_back_kernel(rows, weights, gates, ups, gate_out, up_out):
    grad = dot(rows[...], weights[...], 1, 1)
    gate = gates[...]
    sig = jax.nn.sigmoid(gate)
    gate_out[...] = (grad * ups[...] * sig * (1.0 + gate * (1.0 - sig))).astype(BF16)
    up_out[...] = (grad * gate * sig).astype(BF16)


def ffn_call(kernel, rows, weights, width, kinds, held, name):
    high, wide = min(256 if held else 512, rows.shape[0]), min(1024, width)
    depth, steps = rows.shape[1], width // wide
    tile = pl.BlockSpec((high, wide), lambda n, m: (m, n))
    if held:
        specs = [pl.BlockSpec((wide, depth), lambda n, m: (n, 0))]
    else:
        specs = [pl.BlockSpec((depth, wide), lambda n, m: (0, n)),
                 pl.BlockSpec((depth, wide), lambda n, m: (0, n + steps))]
    return pl.pallas_call(
        kernel,
        out_shape=[jax.ShapeDtypeStruct((rows.shape[0], width), kind) for kind in kinds],
        grid=(steps, rows.shape[0] // high),
        in_specs=[pl.BlockSpec((high, depth), lambda n, m: (m, 0))] + specs + [tile] * len(held),
        out_specs=[tile] * len(kinds),
        compiler_params=pltpu.CompilerParams(vmem_limit_bytes=56 * 2**20),
        cost_estimate=FREE,
        name=name,
    )(rows, *([weights] * len(specs)), *held)


def outer_kernel(right_dim, left, right, out):
    out[...] = dot(left[...], right[...], 0, right_dim).astype(BF16)


def outer_gain_kernel(right_dim, cut, left, right, weights, out, gain):
    total = dot(left[...], right[...], 0, right_dim)
    out[...] = total.astype(BF16)
    scaled = total * weights[:, cut[0] : cut[1]].astype(F32)
    gain[...] = jnp.broadcast_to(jnp.sum(scaled, axis=1, keepdims=True), gain.shape)


def outer(left, right, right_dim, weights=None, cut=None):
    depth, high = left.shape
    wide = right.shape[1 - right_dim]
    rows, cols = min(512, high), min(1024, wide)
    right_block = (depth, cols) if right_dim == 0 else (cols, depth)
    right_map = (lambda n, m: (0, n)) if right_dim == 0 else (lambda n, m: (n, 0))
    specs = [pl.BlockSpec((depth, rows), lambda n, m: (0, m)), pl.BlockSpec(right_block, right_map)]
    outs = [jax.ShapeDtypeStruct((high, wide), BF16)]
    out_specs = [pl.BlockSpec((rows, cols), lambda n, m: (m, n))]
    args, kernel = (left, right), functools.partial(outer_kernel, right_dim)
    if weights is not None:
        args, kernel = (left, right, weights), functools.partial(outer_gain_kernel, right_dim, cut)
        specs.append(pl.BlockSpec((rows, weights.shape[1]), lambda n, m: (m, 0)))
        outs.append(jax.ShapeDtypeStruct((high, 128), F32))
        out_specs.append(pl.BlockSpec((rows, 128), lambda n, m: (m, 0)))
    return pl.pallas_call(
        kernel,
        out_shape=outs,
        grid=(wide // cols, high // rows),
        in_specs=specs,
        out_specs=out_specs,
        compiler_params=pltpu.CompilerParams(vmem_limit_bytes=56 * 2**20),
        cost_estimate=FREE,
        name="outer",
    )(*args)


def norm_back(values, scale, upstream):
    mean_term = jnp.mean(values * upstream, axis=1, keepdims=True)
    return scale * upstream - values * (scale * scale * scale) * mean_term


def shards(
    layer_in, lengths, clip_level, attn_gain, w_query, w_key, w_value, w_out,
    mlp_gain, w_gate, w_up, w_down, cotangent,
):
    tok_rows, width = layer_in.shape
    z_rank, y_rank = lax.axis_index("z"), lax.axis_index("y")
    rank = (y_rank * 2 + lax.axis_index("x")) * 2 + lax.axis_index("c")
    slots = lengths.shape[0]
    next_slot = (z_rank + 1) % slots
    info = jnp.stack(
        (rank, lax.dynamic_index_in_dim(lengths, z_rank, keepdims=False),
         lax.dynamic_index_in_dim(lengths, next_slot, keepdims=False))
    ).astype(jnp.int32)
    inner = rank * tok_rows + jnp.arange(tok_rows, dtype=jnp.int32) + LEAD
    own_mask = jnp.where(inner < SLOT_LEN, inner < info[1], inner - SLOT_LEN < info[2])
    own_mask = own_mask.astype(F32)[:, None]
    spots = ((jnp.arange(SLOT_LEN, dtype=jnp.int32) + LEAD) % SLOT_LEN).astype(F32)
    freq = THETA ** (-(jnp.arange(HALF, dtype=F32) * 2.0 / HD))
    angles = spots[None, :] * freq[:, None]
    cos, sin = jnp.cos(angles), jnp.sin(angles)
    def heads_part(which):
        return jnp.concatenate(
            (half_of(w_out, which, 0).T, half_of(w_query, which, 1), half_of(w_key, which, 1),
             half_of(w_value, which, 1)), 1
        )

    def ffn_part(which):
        return jnp.concatenate((half_of(w_gate, which, 1), half_of(w_up, which, 1)), 1)

    other_y = 1 - y_rank
    heads_w = ordered(heads_part(y_rank), swap(heads_part(other_y), "y"), y_rank, 0)
    full_heads = lax.all_gather(heads_w, "z", axis=0, tiled=True)
    out_cols = HEADS * HD
    heads_cut = (out_cols, full_heads.shape[1])

    ffn_own, ffn_sent = tie(ffn_part(y_rank), ffn_part(other_y))
    ffn_w = ordered(ffn_own, swap(ffn_sent, "y"), y_rank, 0)
    layer_f = layer_in.astype(F32)
    scale_one = lax.rsqrt(jnp.mean(layer_f * layer_f, axis=1, keepdims=True) + EPSILON)
    normal_one = rounded(layer_f * scale_one)
    gain_one = attn_gain.astype(F32)
    acts = gather_one(after((normal_one * gain_one[None, :]).astype(BF16), heads_w))
    acts = gather_two(acts)
    full_heads, ffn_w, *acts = tie(full_heads, ffn_w, *acts)
    full_out, full_qkv = full_heads[:, :out_cols], full_heads[:, out_cols:]
    acts_one = gather_three(acts)
    full_ffn = lax.all_gather(ffn_w, "z", axis=0, tiled=True)

    grad_out = cotangent.astype(F32)
    down_in = (RESIDUAL * own_mask * grad_out).astype(BF16)
    back_rows = gather_one(down_in)
    rows = acts_one.shape[0]
    flat = dot(full_qkv, acts_one, 0, 1)
    (qkv,) = call(
        rope_kernel, info, (flat, cos, sin), [((flat.shape[0], rows), BF16)], [], "rope"
    )
    halo = along(qkv[K_AT:, SLOT_LEN - LEAD :], 1)
    qkv, halo, *back_rows = tie(qkv, halo, *back_rows)
    down_other = swap(after(half_of(w_down, other_y, 0), back_rows[2], back_rows[3]), "y")
    back_rows = gather_two(back_rows)
    heads, lse, peak = call(
        attend_kernel, info, (qkv, halo),
        [((HEADS * HD, rows), BF16), ((8, rows), F32), ((8, 128), F32)],
        [((KEYS, HD), BF16), ((HD, KEYS), BF16), ((TOGETHER, SLOT_LEN, CHUNK), F32)],
        "attend",
    )
    heads, *back_rows = tie(heads, *back_rows)

    terms = [(heads, full_heads, 0, 1, (0, out_cols))]
    high_part, own_peak, down_other = tie(product(terms, 1), peak[:HEADS], down_other)
    came, other_peak = tie(swap(high_part, "c"), swap(own_peak, "y"))
    down_w = ordered(half_of(w_down, y_rank, 0), down_other, y_rank, 1)
    branch = spread_one(terms, came)
    head_peak = over_z(ordered(own_peak, other_peak, y_rank, 0), jnp.maximum)
    down_rows = gather_three(back_rows)
    *got, down_rows, down_w, head_peak = tie(*branch[2:4], down_rows, down_w, head_peak)
    head_peak = head_peak[:, 0]
    branch = spread_two((*branch[:2], *got))
    full_down = lax.all_gather(down_w, "z", axis=1, tiled=True)
    gain_two = mlp_gain.astype(F32)
    narrow = (tok_rows, width // 2)
    resid, scale_two, *acts = row_call(
        residual_kernel, (*branch[:4], layer_in, own_mask, gain_two[None, :]),
        [((tok_rows, width), F32), ((tok_rows, 1), F32), ((tok_rows, width), BF16),
         (narrow, BF16), (narrow, BF16)], "residual",
    )
    acts = gather_one(acts[0], acts[1:])
    full_ffn, *acts = tie(full_ffn, *acts)
    acts = gather_two(acts)
    acts_two = gather_three(acts)

    hid = full_ffn.shape[1] // 2
    gate_proj, up_proj, hidden = ffn_call(
        hidden_kernel, acts_two, full_ffn, hid, (F32, F32, BF16), (), "hidden"
    )

    def reduced(grad, axis):
        return lax.psum_scatter(grad, "z", scatter_dimension=axis, tiled=True)

    def traded(total, axis, *behind):
        total = after(total, *behind)
        return half_of(total, y_rank, axis), swap(half_of(total, other_y, axis), "y")

    (down_part,) = outer(hidden, down_rows, 0)
    down_sum = reduced(down_part, 1)
    down_rows = after(down_rows, down_part)
    gate_grad, up_grad = ffn_call(
        hidden_back_kernel, down_rows, full_down, hid, (BF16, BF16), (gate_proj, up_proj),
        "hidden_back",
    )
    terms = [(gate_grad, full_ffn, 1, 1, None, 0), (up_grad, full_ffn, 1, 1, None, 1)]
    *norm_two, acts_two = spread_one(terms, None, acts_two)
    ffn_parts = [outer(acts_two, grad, 0)[0] for grad in (gate_grad, up_grad)]
    *got, ffn_parts[0], ffn_parts[1] = tie(*norm_two[2:4], *ffn_parts)
    one_sum, two_sum = [reduced(part, 0) for part in ffn_parts]
    norm_two = spread_two((*norm_two[:2], *got))
    gain_two_part, grad_resid, *mixed = row_call(
        residual_back_kernel,
        (*norm_two[:4], cotangent, resid, scale_two, gain_two[None, :], own_mask),
        [((8, width), F32), ((tok_rows, width), F32), ((tok_rows, width), BF16), (narrow, BF16),
         (narrow, BF16)], "residual_back",
    )
    mixed_in, hidden = tie(mixed[0], hidden)
    mixed = gather_one(mixed_in, mixed[1:])
    terms = [(hidden, full_down, 1, 0, None)]
    *got, high_part = tie(*mixed[2:4], product(terms, 1))
    mixed = gather_two((*mixed[:2], *got))
    low_part = product(terms, 0, swap(high_part, "c"))
    a1, b1, *low_part = tie(*mixed[5:], *low_part)
    mixed = (*mixed[:5], a1, b1)
    second = (*low_part[:2], swap(low_part[2], "x"), swap(low_part[3], "y"))
    mixed_rows = gather_three(mixed)
    mixed_rows, down_sum, one_sum = tie(mixed_rows, down_sum, one_sum)
    down_own, down_other = traded(down_sum, 1)
    one_own, one_other = traded(one_sum, 0)

    heads_grad = dot(full_out, mixed_rows, 0, 1).astype(BF16)
    dq, dkv, back = call(
        attend_back_kernel, info, (qkv, halo, heads_grad, lse, cos, sin),
        [((HEADS * HD, rows), BF16), ((2 * HD, rows), F32), ((2 * HD, LEAD), BF16)],
        [((KEYS, HD), BF16), ((KEYS, HD), BF16), ((HD, KEYS), BF16),
         ((TOGETHER, SLOT_LEN, CHUNK), F32), ((TOGETHER, SLOT_LEN, CHUNK), F32),
         ((KEYS, HD), F32), ((KEYS, HD), F32), ((HEADS * HD, SLOT_LEN), BF16)],
        "attend_back", 60,
    )
    back, down_other, one_other, *got = tie(back, down_other, one_other, *second[2:4])
    back_sent = along(back, -1)
    left, right, *sent = fold(*second[:2], *got)
    (out_part,) = outer(mixed_rows, heads, 1)
    dkv, back_sent, out_part, *sent = tie(dkv, back_sent, out_part, *sent)
    out_sum = reduced(out_part, 0)
    second = left, right, swap(sent[0], "y"), swap(sent[1], "x")
    (dkv_done,) = call(
        finish_kernel, info, (dkv, back_sent, cos, sin), [((2 * HD, rows), BF16)], [], "finish"
    )
    dqkv = jnp.concatenate((dq, dkv_done))
    terms = [(dqkv, full_heads, 0, 1, heads_cut)]
    high_part, acts_one = tie(product(terms, 1), acts_one)
    qkv_part, sums = outer(acts_one, dqkv, 1, full_heads, heads_cut)
    came, qkv_part, sums, two_sum, *got = tie(
        swap(high_part, "c"), qkv_part, sums, two_sum, *second[2:4]
    )
    two_own = half_of(two_sum, y_rank, 0)
    came, two_sent = tie(came, half_of(two_sum, other_y, 0))
    qkv_sum = reduced(qkv_part, 0)
    branch_two = spread_three((*second[:2], *got))
    result = resid + RESIDUAL * own_mask * branch_two
    *norm_one, sums, two_other = spread_one(terms, came, sums, swap(two_sent, "y"))
    gains = jnp.stack((sums[:, 0] / gain_one, jnp.sum(gain_two_part, axis=0)))
    gains = over_z(gains, jnp.add)
    *got, gains, out_sum = tie(*norm_one[2:4], gains, out_sum)
    gains = gains.reshape(2, lax.axis_size("z"), 2, 2, 2, -1)

    def halved(gains, dim, axis):
        at = lax.axis_index(axis)
        return (lax.dynamic_index_in_dim(gains, at, dim, keepdims=False),
                lax.dynamic_index_in_dim(gains, 1 - at, dim, keepdims=False))

    norm_one = spread_two((*norm_one[:2], *got), gains)
    gains = norm_one[4]
    out_own, out_sent = half_of(out_sum, y_rank, 0), half_of(out_sum, other_y, 0)
    own, qkv_sent = half_of(qkv_sum, y_rank, 0), half_of(qkv_sum, other_y, 0)
    kept, sent = halved(gains, 4, "c")
    kept, sent = halved(kept + swap(sent, "c"), 3, "x")
    *norm_one, qkv_sent, kept, sent, out_sent = tie(*norm_one[:4], qkv_sent, kept, sent, out_sent)
    other, out_other = swap(qkv_sent, "y"), swap(out_sent, "y")
    (grad_input,) = row_call(
        input_back_kernel, (*norm_one, grad_resid, layer_in, scale_one, gain_one[None, :]),
        [((tok_rows, width), BF16)], "input_back",
    )
    kept, sent = halved(kept + swap(sent, "x"), 2, "y")
    gains = lax.dynamic_index_in_dim(kept + swap(sent, "y"), z_rank, 1, keepdims=False)

    down_grad = ordered(down_own, down_other, y_rank, 0).astype(F32)
    gate_w_grad = ordered(one_own, one_other, y_rank, 1).astype(F32)
    up_w_grad = ordered(two_own, two_other, y_rank, 1).astype(F32)
    out_grad = ordered(out_own.T, out_other.T, y_rank, 0).astype(F32)

    def columns(start, stop):
        return ordered(own[:, start:stop], other[:, start:stop], y_rank, 1).astype(F32)

    query_grad = columns(0, K_AT)
    key_grad = columns(K_AT, V_AT)
    value_grad = columns(V_AT, V_AT + HD)

    level = clip_level[0].astype(F32) * LEVEL_UNIT
    factor = level / jnp.maximum(level, head_peak)
    query_clipped = w_query.astype(F32) * jnp.repeat(jnp.sqrt(factor), HD)[None, :]
    kv_factor = jnp.min(factor.reshape(-1, HEADS), axis=1)
    key_clipped = w_key.astype(F32) * jnp.repeat(jnp.sqrt(kv_factor), HD)[None, :]
    return (
        result.astype(BF16),
        grad_input,
        gains[0],
        query_grad,
        key_grad,
        value_grad,
        out_grad,
        gains[1],
        gate_w_grad,
        up_w_grad,
        down_grad,
        query_clipped,
        key_clipped,
    )


def solution(mesh):
    fsdp, tp = mesh.shape["fsdp"], mesh.shape["tp"]
    fine = Mesh(mesh.devices.reshape(fsdp // 2, 2, tp // 2, 2), EVERY)
    rows, cols = ("z", "y"), ("x", "c")
    tokens, down, across = P(EVERY, None), P(rows, cols), P(cols, rows)
    in_specs = (
        tokens, P(), P(), P(), down, down, down, across, P(), down, down, across, tokens,
    )
    out_specs = (
        tokens, tokens, P(EVERY), down, down, down, across, P(EVERY), down, down, across,
        down, down,
    )
    return jax.shard_map(shards, mesh=fine, in_specs=in_specs, out_specs=out_specs, check_vma=False)
```

```python
import functools

import jax
import jax.numpy as jnp
from jax import lax
from jax.experimental import pallas as pl
from jax.experimental.pallas import tpu as pltpu
from jax.sharding import Mesh
from jax.sharding import PartitionSpec as P

HD = 64
HALF = HD // 2
SLOT_LEN = 2048
LEAD = 512
CHUNK = 512
BLOCK = 256
HEADS = 4

EPSILON = 1e-05
THETA = 10000000.0
MULTIPLIER = 0.015625
RESIDUAL = 0.22
LEVEL_UNIT = 0.125
NEGATIVE = -1e30
GROUP = ("y", "x", "c")
EVERY = ("z", "y", "x", "c")
F32 = jnp.float32
BF16 = jnp.bfloat16
FREE = pl.CostEstimate(flops=0, bytes_accessed=0, transcendentals=0)


def rounded(x):
    return lax.reduce_precision(x, exponent_bits=8, mantissa_bits=7)


def swap(x, axis):
    return lax.ppermute(x, axis, [(0, 1), (1, 0)])


def along(x, by):
    peers = lax.axis_size("z")
    return lax.ppermute(x, "z", [(i, (i + by) % peers) for i in range(peers)])


def dot(left, right, left_dim, right_dim):
    return lax.dot_general(
        left, right, (((left_dim,), (right_dim,)), ((), ())), preferred_element_type=F32
    )


def half_of(x, which, axis):
    size = x.shape[axis] // 2
    return lax.dynamic_slice_in_dim(x, which * size, size, axis)


def ordered(own, other, rank, axis):
    return jnp.where(
        rank == 0,
        jnp.concatenate((own, other), axis=axis),
        jnp.concatenate((other, own), axis=axis),
    )


def after(x, *others):
    return lax.optimization_barrier((x, *others))[0]


def tie(*xs):
    return lax.optimization_barrier(xs)


def gather_one(v, halves=None):
    half = v.shape[1] // 2
    halves = (v[:, :half], v[:, half:]) if halves is None else halves
    return v, swap(v, "c"), swap(halves[0], "x"), swap(halves[1], "y")


def gather_two(state):
    v, near, a01, b10 = state
    half = v.shape[1] // 2
    a1 = swap(jnp.concatenate((v[:, :half], a01)), "y")
    b1 = swap(jnp.concatenate((v[:, half:], b10)), "x")
    second = swap(jnp.concatenate((a01, b10)), "c")
    return v, near, a01, b10, second, a1, b1


def gather_three(state):
    size, half = state[0].shape[0], state[0].shape[1] // 2
    state = (state[0], *tie(*state[1:]))
    third = swap(jnp.concatenate(state[5:]), "c")
    spots = (
        (0, 0, size, 0, 0), (1, 0, size, 4 * size, 0), (2, 0, size, size, 0),
        (3, 0, size, 2 * size, half), (4, 0, size, 5 * size, 0),
        (4, size, size, 6 * size, half), (5, 0, 2 * size, 2 * size, 0),
        (6, 0, size, size, half), (6, size, size, 3 * size, half),
        (7, 0, 2 * size, 6 * size, 0), (7, 2 * size, size, 5 * size, half),
        (7, 3 * size, size, 7 * size, half),
    )
    return place((*state, third), spots, 8 * size)


def place_kernel(spots, count, *refs):
    pieces, out, held = refs[:count], refs[count], refs[count + 1 : 2 * count + 1]
    load_sems, sems = refs[-2:]
    loads = [
        pltpu.make_async_copy(piece, here, load_sems.at[i])
        for i, (piece, here) in enumerate(zip(pieces, held, strict=True))
    ]
    for load in loads:
        load.start()
    copies = []
    for i, load in enumerate(loads):
        load.wait()
        for at, (piece, start, size, row, col) in enumerate(spots):
            if piece == i:
                source = held[piece]
                copy = pltpu.make_async_copy(
                    source.at[pl.ds(start, size), :],
                    out.at[pl.ds(row, size), pl.ds(col, source.shape[1])],
                    sems.at[at],
                )
                copy.start()
                copies.append(copy)
    for copy in copies:
        copy.wait()


def place(pieces, spots, count):
    number = len(pieces)
    return pl.pallas_call(
        functools.partial(place_kernel, spots, number),
        out_shape=jax.ShapeDtypeStruct((count, pieces[0].shape[1]), BF16),
        in_specs=[pl.BlockSpec(memory_space=pl.ANY)] * number,
        out_specs=pl.BlockSpec(memory_space=pltpu.HBM),
        scratch_shapes=[pltpu.VMEM(piece.shape, BF16) for piece in pieces]
        + [pltpu.SemaphoreType.DMA((number,)), pltpu.SemaphoreType.DMA((len(spots),))],
        compiler_params=pltpu.CompilerParams(vmem_limit_bytes=60 * 2**20),
        cost_estimate=FREE,
        name="place",
    )(*pieces)


def product_kernel(terms, keep, *refs):
    count = len(terms)
    step = pl.program_id(0)
    flipped = sum(term[0] == 0 for term in terms)
    scratch = refs[len(refs) - flipped :]
    total, used = None, 0
    for at, (left_dim, right_dim, cut) in enumerate(terms):
        left, right = refs[2 * at], refs[2 * at + 1]
        if left_dim == 0:
            store = scratch[used]
            used += 1

            @pl.when(step == 0)
            def _(left=left, store=store):
                store[...] = upright(left[...])

            left = store
        block = right[...] if cut is None else right[:, cut[0] : cut[1]]
        one = dot(left[...], block, 1, right_dim)
        total = one if total is None else total + one
    if not keep:
        refs[2 * count][...] = total.astype(BF16)
        return
    came, left_out, right_out, x_out, y_out = refs[2 * count : 2 * count + 5]
    total = total + came[...].astype(F32)
    blocks = total.reshape(2, 2, total.shape[0] // 4, total.shape[1])
    half = pl.num_programs(0) // 2

    @pl.when(step < half)
    def _():
        left_out[...] = blocks[:, 0]
        x_out[...] = blocks[:, 1].astype(BF16)

    @pl.when(step >= half)
    def _():
        right_out[...] = blocks[0]
        y_out[...] = blocks[1].astype(BF16)


def product(terms, part, came=None):
    tile = 512
    args, specs, kinds, scratch = [], [], [], []
    for left, right, left_dim, right_dim, cut, *block in terms:
        whole = not isinstance(left, tuple)
        at = part if whole else 0
        left = left if whole else left[part]
        rows = left.shape[1 - left_dim] // (2 if whole else 1)
        depth = left.shape[left_dim]
        if left_dim == 1:
            specs.append(pl.BlockSpec((rows, depth), lambda n, at=at: (at, 0)))
        else:
            specs.append(pl.BlockSpec((depth, rows), lambda n: (0, part)))
            scratch.append(pltpu.VMEM((rows, depth), BF16))
        if right_dim == 1:
            width = right.shape[0]
            if block:
                specs.append(pl.BlockSpec((tile, depth), lambda n, to=block[0]: (n, to)))
            else:
                specs.append(pl.BlockSpec((tile, right.shape[1]), lambda n: (n, 0)))
        else:
            width = right.shape[1]
            specs.append(pl.BlockSpec((right.shape[0], tile), lambda n: (0, n)))
        args += [left, right]
        kinds.append((left_dim, right_dim, cut))
    if came is None:
        out_shape = jax.ShapeDtypeStruct((rows, width), BF16)
        out_specs = pl.BlockSpec((rows, tile), lambda n: (0, n))
    else:
        args.append(came)
        specs.append(pl.BlockSpec((rows, tile), lambda n: (0, n)))
        half = width // tile // 2
        shape = (2, rows // 4, width // 2)
        out_shape = [jax.ShapeDtypeStruct(shape, d) for d in (F32, F32, BF16, BF16)]
        first = pl.BlockSpec((2, rows // 4, tile), lambda n: (0, 0, jnp.minimum(n, half - 1)))
        last = pl.BlockSpec((2, rows // 4, tile), lambda n: (0, 0, jnp.maximum(n - half, 0)))
        out_specs = [first, last, first, last]
    return pl.pallas_call(
        functools.partial(product_kernel, kinds, came is not None),
        out_shape=out_shape,
        grid=(width // tile,),
        in_specs=specs,
        out_specs=out_specs,
        scratch_shapes=scratch,
        compiler_params=pltpu.CompilerParams(vmem_limit_bytes=56 * 2**20),
        cost_estimate=FREE,
        name="product",
    )(*args)


def spread_one(terms, came=None, *later):
    came = swap(product(terms, 1), "c") if came is None else came
    left, right, send_x, send_y = product(terms, 0, came)
    if later:
        send_x, send_y, *later = tie(send_x, send_y, *later)
    return left, right, swap(send_x, "x"), swap(send_y, "y"), *later


ROWS = 64


def fold_kernel(left, right, left_x, right_y, left_out, right_out, y_out, x_out):
    total = left[...] + left_x[...].astype(F32)
    left_out[...], y_out[...] = total[0], total[1].astype(BF16)
    total = right[...] + right_y[...].astype(F32)
    right_out[...], x_out[...] = total[0], total[1].astype(BF16)


def fold(*parts):
    rows, cols = parts[0].shape[1:]
    size = rows // 2
    return pl.pallas_call(
        fold_kernel,
        out_shape=[jax.ShapeDtypeStruct((rows, cols), d) for d in (F32, F32, BF16, BF16)],
        grid=(2,),
        in_specs=[pl.BlockSpec((2, size, cols), lambda i: (0, i, 0))] * 4,
        out_specs=[pl.BlockSpec((size, cols), lambda i: (i, 0))] * 4,
        cost_estimate=FREE,
        name="fold",
    )(*parts)


def resident(kernel, args, outs, name):
    spec = pl.BlockSpec(memory_space=pltpu.VMEM)
    return pl.pallas_call(
        kernel,
        out_shape=[jax.ShapeDtypeStruct(shape, kind) for shape, kind in outs],
        in_specs=[spec] * len(args),
        out_specs=[spec] * len(outs),
        compiler_params=pltpu.CompilerParams(vmem_limit_bytes=24 * 2**20),
        cost_estimate=FREE,
        name=name,
    )(*args)


def fold_loop_kernel(left, right, left_x, right_y, left_out, right_out, y_out, x_out):
    @pl.loop(0, left.shape[1] // ROWS)
    def _(i):
        here = pl.ds(pl.multiple_of(i * ROWS, ROWS), ROWS)
        total = left[:, here, :] + left_x[:, here, :].astype(F32)
        left_out[here, :], y_out[here, :] = total[0], total[1].astype(BF16)
        total = right[:, here, :] + right_y[:, here, :].astype(F32)
        right_out[here, :], x_out[here, :] = total[0], total[1].astype(BF16)


def fold_resident(*parts):
    shape = parts[0].shape[1:]
    return resident(fold_loop_kernel, parts, [(shape, d) for d in (F32, F32, BF16, BF16)], "fold")


def spread_two(state, *extra, folding=fold_resident):
    left, right, send_y, send_x = folding(*state[:4])
    if extra:
        send_y, send_x, *extra = tie(send_y, send_x, *extra)
    return left, right, swap(send_y, "y"), swap(send_x, "x"), *extra


def spread_three(state):
    left, right, left_y, right_x = state[:4]
    return jnp.concatenate((left + left_y.astype(F32), right + right_x.astype(F32)), axis=1)


def joined(left, right, left_y, right_x):
    return jnp.concatenate(
        (left[...] + left_y[...].astype(F32), right[...] + right_x[...].astype(F32)), axis=1
    )


def store_halves(value, out, left_out, right_out):
    half = value.shape[1] // 2
    out[...], left_out[...], right_out[...] = value, value[:, :half], value[:, half:]


def residual_kernel(*refs):
    values, mask, gain = (ref[...] for ref in refs[4:7])
    resid_out, scale_out = refs[7:9]
    resid = values.astype(F32) + RESIDUAL * mask * joined(*refs[:4])
    scale = lax.rsqrt(jnp.mean(resid * resid, axis=1, keepdims=True) + EPSILON)
    resid_out[...], scale_out[...] = resid, scale
    normal = (resid * scale).astype(BF16).astype(F32)
    store_halves((normal * gain).astype(BF16), *refs[9:12])


def residual_back_kernel(*refs):
    base, values, scale, gain, mask = (ref[...] for ref in refs[4:9])
    sums, grad_out = refs[9:11]
    upstream = joined(*refs[:4])
    normal = (values * scale).astype(BF16).astype(F32)
    share = normal * upstream
    sums[...] += jnp.sum(share.reshape(-1, 8, share.shape[1]), axis=0)
    grad = base.astype(F32) + norm_back(values, scale, gain * upstream)
    grad_out[...] = grad
    store_halves((RESIDUAL * mask * grad).astype(BF16), *refs[11:14])


def input_back_kernel(*refs):
    base, values, scale, gain = (ref[...] for ref in refs[4:8])
    grad = base + norm_back(values.astype(F32), scale, gain * joined(*refs[:4]))
    refs[8][...] = grad.astype(BF16)


def input_back(*args):
    rows, width = args[4].shape

    def spec(shape):
        if shape[0] == rows:
            return pl.BlockSpec((ROWS, shape[1]), lambda i: (i, 0))
        return pl.BlockSpec(shape, lambda i: (0, 0))

    return pl.pallas_call(
        input_back_kernel,
        out_shape=jax.ShapeDtypeStruct((rows, width), BF16),
        grid=(rows // ROWS,),
        in_specs=[spec(arg.shape) for arg in args],
        out_specs=spec((rows, width)),
        cost_estimate=FREE,
        name="input_back",
    )(*args)


def row_call(kernel, args, outs, name):
    rows = args[0].shape[0]

    def looped(*refs):
        for ref in refs[len(args) :]:
            if ref.shape[0] == 8:
                ref[...] = jnp.zeros(ref.shape, F32)

        @pl.loop(0, rows // ROWS)
        def _(i):
            here = pl.ds(pl.multiple_of(i * ROWS, ROWS), ROWS)
            kernel(*(ref.at[here, :] if ref.shape[0] == rows else ref for ref in refs))

    return resident(looped, args, outs, name)


def over_z(x, combine):
    peers, step = lax.axis_size("z"), 1
    assert peers & (peers - 1) == 0
    while step < peers:
        x = combine(x, along(x, step))
        step *= 2
    return x


def place_of(block, rank):
    j = jnp.bitwise_xor(block, rank)
    return jnp.bitwise_or(jnp.left_shift(jnp.bitwise_and(j, 1), 2), jnp.right_shift(j, 1))


def lanes_of(block, rank):
    return pl.ds(pl.multiple_of(place_of(block, rank) * BLOCK, BLOCK), BLOCK)


def rope_kernel(info, qkv, cos, sin, out):
    rank = info[0]

    @pl.loop(0, SLOT_LEN // BLOCK)
    def _(block):
        source = lanes_of(block, rank)
        target = pl.ds(pl.multiple_of(block * BLOCK, BLOCK), BLOCK)
        c, s = cos[:, target], sin[:, target]
        for head in range(HEADS + 1):
            first = qkv[pl.ds(head * HD, HALF), source]
            second = qkv[pl.ds(head * HD + HALF, HALF), source]
            scale = MULTIPLIER if head < HEADS else 1.0
            out[pl.ds(head * HD, HALF), target] = ((first * c - second * s).astype(BF16) * scale).astype(BF16)
            out[pl.ds(head * HD + HALF, HALF), target] = ((second * c + first * s).astype(BF16) * scale).astype(BF16)
        rest = (HEADS + 1) * HD
        out[pl.ds(rest, HD), target] = qkv[pl.ds(rest, HD), source].astype(BF16)


TOGETHER = 4
KEYS = SLOT_LEN + LEAD
K_AT = HEADS * HD
V_AT = K_AT + HD


def upright(x):
    return x.astype(F32).T.astype(BF16)


def causal():
    keys = lax.broadcasted_iota(jnp.int32, (CHUNK, CHUNK), 0)
    queries = lax.broadcasted_iota(jnp.int32, (CHUNK, CHUNK), 1)
    return keys <= queries


def key_range(step):
    last = step == SLOT_LEN // CHUNK - 1
    low = jnp.where(last, KEYS // CHUNK - 1, 0)
    high = jnp.where(last, KEYS // CHUNK, step + 2)
    return low, high


def chunk_of(i):
    return pl.ds(pl.multiple_of(i * CHUNK, CHUNK), CHUNK)


def head_rows(h):
    return pl.ds(pl.multiple_of(h * HD, HD), HD)


def attend_kernel(info, qkv, halo, heads_out, lse_out, peak_out, k_up, v_flat, scores):
    rank = info[0]
    k_up[pl.ds(0, LEAD), :] = upright(halo[pl.ds(0, HD), :])
    v_flat[:, pl.ds(0, LEAD)] = halo[pl.ds(HD, HD), :]
    v_flat[:, pl.ds(LEAD, SLOT_LEN)] = qkv[pl.ds(V_AT, HD), :]

    @pl.loop(0, SLOT_LEN // CHUNK)
    def _(i):
        k_up[pl.ds(pl.multiple_of(LEAD + i * CHUNK, CHUNK), CHUNK), :] = upright(
            qkv[pl.ds(K_AT, HD), chunk_of(i)]
        )

    peak_out[...] = jnp.full(peak_out.shape, NEGATIVE, F32)
    lse_out[...] = jnp.zeros(lse_out.shape, F32)

    @pl.loop(0, HEADS // TOGETHER)
    def _(group):
        @pl.loop(0, SLOT_LEN // CHUNK)
        def _(step):
            low, high = key_range(step)
            heads = [group * TOGETHER + i for i in range(TOGETHER)]
            query = [qkv[head_rows(h), chunk_of(step)] for h in heads]

            def raw(kc, i):
                return jnp.dot(k_up[chunk_of(kc), :], query[i], preferred_element_type=F32)

            def first(kc, tops):
                outs = []
                for i in range(TOGETHER):
                    s = raw(kc, i)
                    scores[i, chunk_of(kc - low)] = s
                    outs.append(jnp.maximum(tops[i], jnp.max(s, axis=0, keepdims=True)))
                return tuple(outs)

            tops = []
            for i in range(TOGETHER):
                s = jnp.where(causal(), raw(high - 1, i), NEGATIVE)
                scores[i, chunk_of(high - 1 - low)] = s
                tops.append(jnp.max(s, axis=0, keepdims=True))
            tops = lax.fori_loop(low, high - 1, first, tuple(tops))

            def second(kc, totals):
                outs = []
                for i in range(TOGETHER):
                    e = jnp.exp(scores[i, chunk_of(kc)] - tops[i])
                    scores[i, chunk_of(kc)] = e
                    outs.append(totals[i] + jnp.sum(e, axis=0, keepdims=True))
                return tuple(outs)

            totals = lax.fori_loop(0, high - low, second, (jnp.zeros((1, CHUNK), F32),) * TOGETHER)
            inverses = [1.0 / total for total in totals]

            def third(kc, mixed):
                outs = []
                for i in range(TOGETHER):
                    probs = (scores[i, chunk_of(kc)] * inverses[i]).astype(BF16)
                    more = jnp.dot(
                        v_flat[:, chunk_of(kc + low)], probs, preferred_element_type=F32
                    )
                    outs.append(mixed[i] + more)
                return tuple(outs)

            mixed_all = lax.fori_loop(
                0, high - low, third, (jnp.zeros((HD, CHUNK), F32),) * TOGETHER
            )
            last = step == SLOT_LEN // CHUNK - 1
            start = jnp.where(last, 0, LEAD + step * CHUNK)
            alive = jnp.where(last, info[2], info[1])
            spots = lax.broadcasted_iota(jnp.int32, (1, CHUNK), 1) + start
            for i, h in enumerate(heads):
                mixed = mixed_all[i].astype(BF16)
                for part in range(CHUNK // BLOCK):
                    there = lanes_of(step * (CHUNK // BLOCK) + part, rank)
                    heads_out[head_rows(h), there] = mixed[:, part * BLOCK : (part + 1) * BLOCK]
                lse_out[pl.ds(h, 1), chunk_of(step)] = tops[i] + jnp.log(totals[i])
                best = jnp.where(spots < alive, tops[i], NEGATIVE)
                best = jnp.max(best, axis=1, keepdims=True)
                peak_out[pl.ds(h, 1), :] = jnp.maximum(peak_out[pl.ds(h, 1), :], best)


def attend_back_kernel(
    info, qkv, halo, upstream, lse, cos, sin, dq_out, dkv_out, halo_out,
    k_up, v_up, k_flat, probs_s, grads_s, dk_s, dv_s, up_abs,
):
    rank = info[0]
    k_up[pl.ds(0, LEAD), :] = upright(halo[pl.ds(0, HD), :])
    v_up[pl.ds(0, LEAD), :] = upright(halo[pl.ds(HD, HD), :])
    k_flat[:, pl.ds(0, LEAD)] = halo[pl.ds(0, HD), :]
    k_flat[:, pl.ds(LEAD, SLOT_LEN)] = qkv[pl.ds(K_AT, HD), :]

    @pl.loop(0, SLOT_LEN // CHUNK)
    def _(i):
        rows = pl.ds(pl.multiple_of(LEAD + i * CHUNK, CHUNK), CHUNK)
        k_up[rows, :] = upright(qkv[pl.ds(K_AT, HD), chunk_of(i)])
        v_up[rows, :] = upright(qkv[pl.ds(V_AT, HD), chunk_of(i)])

    @pl.loop(0, SLOT_LEN // BLOCK)
    def _(block):
        target = pl.ds(pl.multiple_of(block * BLOCK, BLOCK), BLOCK)
        up_abs[:, target] = upstream[:, lanes_of(block, rank)]

    dk_s[...] = jnp.zeros(dk_s.shape, F32)
    dv_s[...] = jnp.zeros(dv_s.shape, F32)

    @pl.loop(0, HEADS // TOGETHER)
    def _(group):
        @pl.loop(0, SLOT_LEN // CHUNK)
        def _(step):
            low, high = key_range(step)
            here = chunk_of(step)
            heads = [group * TOGETHER + i for i in range(TOGETHER)]
            query = [qkv[head_rows(h), here] for h in heads]
            grad = [up_abs[head_rows(h), here] for h in heads]
            query_up, grad_up = [upright(x) for x in query], [upright(x) for x in grad]
            logs = [lse[pl.ds(h, 1), here] for h in heads]

            def spot(i, kc):
                return i, chunk_of(kc - low)

            def one(kc, masked):
                deltas, added = [], None
                for i in range(TOGETHER):
                    s = jnp.dot(k_up[chunk_of(kc), :], query[i], preferred_element_type=F32)
                    p = jnp.exp(s - logs[i])
                    if masked:
                        p = jnp.where(causal(), p, 0.0)
                    g = jnp.dot(v_up[chunk_of(kc), :], grad[i], preferred_element_type=F32)
                    probs_s[spot(i, kc)] = p
                    grads_s[spot(i, kc)] = g
                    more = jnp.dot(p.astype(BF16), grad_up[i], preferred_element_type=F32)
                    added = more if added is None else added + more
                    deltas.append(jnp.sum(p * g, axis=0, keepdims=True))
                dv_s[chunk_of(kc), :] += added
                return tuple(deltas)

            def both(kc, deltas):
                return tuple(d + e for d, e in zip(deltas, one(kc, False), strict=True))

            deltas = lax.fori_loop(low, high - 1, both, one(high - 1, True))

            def two(kc, dqs):
                outs, added = [], None
                for i in range(TOGETHER):
                    p, g = probs_s[spot(i, kc)], grads_s[spot(i, kc)]
                    ds = (p * (g - deltas[i])).astype(BF16)
                    more = jnp.dot(ds, query_up[i], preferred_element_type=F32)
                    added = more if added is None else added + more
                    outs.append(
                        dqs[i] + jnp.dot(k_flat[:, chunk_of(kc)], ds, preferred_element_type=F32)
                    )
                dk_s[chunk_of(kc), :] += added
                return tuple(outs)

            zero = jnp.zeros((HD, CHUNK), F32)
            dqs = lax.fori_loop(low, high, two, (zero,) * TOGETHER)
            c, s = cos[:, here], sin[:, here]
            for i in range(TOGETHER):
                dq = dqs[i] * MULTIPLIER
                u1, u2 = dq[:HALF], dq[HALF:]
                t1, t2 = (u1 * c + u2 * s).astype(BF16), (u2 * c - u1 * s).astype(BF16)
                at = heads[i] * HD
                for part in range(CHUNK // BLOCK):
                    there = lanes_of(step * (CHUNK // BLOCK) + part, rank)
                    cut = slice(part * BLOCK, (part + 1) * BLOCK)
                    dq_out[pl.ds(pl.multiple_of(at, HD), HALF), there] = t1[:, cut]
                    dq_out[pl.ds(pl.multiple_of(at + HALF, HALF), HALF), there] = t2[:, cut]

    halo_out[pl.ds(0, HD), :] = dk_s[pl.ds(0, LEAD), :].T.astype(BF16)
    halo_out[pl.ds(HD, HD), :] = dv_s[pl.ds(0, LEAD), :].T.astype(BF16)

    @pl.loop(0, SLOT_LEN // CHUNK)
    def _(i):
        rows = pl.ds(pl.multiple_of(LEAD + i * CHUNK, CHUNK), CHUNK)
        dkv_out[pl.ds(0, HD), chunk_of(i)] = dk_s[rows, :].T
        dkv_out[pl.ds(HD, HD), chunk_of(i)] = dv_s[rows, :].T


def finish_kernel(info, dkv, halo, cos, sin, out):
    rank = info[0]
    owned = (SLOT_LEN - LEAD) // BLOCK
    for block in range(SLOT_LEN // BLOCK):
        source = pl.ds(block * BLOCK, BLOCK)
        target = lanes_of(block, rank)
        c, s = cos[:, source], sin[:, source]
        u1, u2 = dkv[pl.ds(0, HALF), source], dkv[pl.ds(HALF, HALF), source]
        rest = dkv[pl.ds(HD, HD), source]
        if block >= owned:
            part = pl.ds((block - owned) * BLOCK, BLOCK)
            u1 = u1 + halo[pl.ds(0, HALF), part].astype(F32)
            u2 = u2 + halo[pl.ds(HALF, HALF), part].astype(F32)
            rest = rest + halo[pl.ds(HD, HD), part].astype(F32)
        out[pl.ds(0, HALF), target] = (u1 * c + u2 * s).astype(BF16)
        out[pl.ds(HALF, HALF), target] = (u2 * c - u1 * s).astype(BF16)
        out[pl.ds(HD, HD), target] = rest.astype(BF16)


def call(kernel, info, args, outs, scratch, name, limit=40):
    spec = pl.BlockSpec(memory_space=pltpu.VMEM)
    return pl.pallas_call(
        kernel,
        out_shape=[jax.ShapeDtypeStruct(s, d) for s, d in outs],
        in_specs=[pl.BlockSpec(memory_space=pltpu.SMEM)] + [spec] * len(args),
        out_specs=[spec] * len(outs),
        scratch_shapes=[pltpu.VMEM(s, d) for s, d in scratch],
        compiler_params=pltpu.CompilerParams(vmem_limit_bytes=limit * 2**20),
        cost_estimate=FREE,
        name=name,
    )(info, *args)


def hidden_kernel(rows, gate_w, up_w, gate_out, up_out, hidden_out):
    gate, up = dot(rows[...], gate_w[...], 1, 0), dot(rows[...], up_w[...], 1, 0)
    gate_out[...], up_out[...] = gate, up
    hidden_out[...] = (gate * jax.nn.sigmoid(gate) * up).astype(BF16)


def hidden_back_kernel(rows, weights, gates, ups, gate_out, up_out):
    grad = dot(rows[...], weights[...], 1, 1)
    gate = gates[...]
    sig = jax.nn.sigmoid(gate)
    gate_out[...] = (grad * ups[...] * sig * (1.0 + gate * (1.0 - sig))).astype(BF16)
    up_out[...] = (grad * gate * sig).astype(BF16)


def ffn_call(kernel, rows, weights, width, kinds, held, name, part=0, parts=1):
    high, wide = min(256 if held else 512, rows.shape[0]), min(1024, width)
    depth, steps = rows.shape[1], width // wide
    count = rows.shape[0] // parts
    skip = part * (count // high)
    tile = pl.BlockSpec((high, wide), lambda n, m: (m, n))
    held_tile = pl.BlockSpec((high, wide), lambda n, m: (m + skip, n))
    if held:
        specs = [pl.BlockSpec((wide, depth), lambda n, m: (n, 0))]
    else:
        specs = [pl.BlockSpec((depth, wide), lambda n, m: (0, n)),
                 pl.BlockSpec((depth, wide), lambda n, m: (0, n + steps))]
    return pl.pallas_call(
        kernel,
        out_shape=[jax.ShapeDtypeStruct((count, width), kind) for kind in kinds],
        grid=(steps, count // high),
        in_specs=[pl.BlockSpec((high, depth), lambda n, m: (m + skip, 0))]
        + specs
        + [held_tile] * len(held),
        out_specs=[tile] * len(kinds),
        compiler_params=pltpu.CompilerParams(vmem_limit_bytes=56 * 2**20),
        cost_estimate=FREE,
        name=name,
    )(rows, *([weights] * len(specs)), *held)


def outer_halves_kernel(left, low, high, out):
    rows = low.shape[0]
    total = dot(left[:rows], low[...], 0, 0) + dot(left[rows:], high[...], 0, 0)
    out[...] = total.astype(BF16)


def outer_halves(left, low, high):
    (depth, tall), wide = left.shape, low.shape[1]
    rows, cols = min(512, tall), min(1024, wide)
    half = pl.BlockSpec((depth // 2, cols), lambda n, m: (0, n))
    return pl.pallas_call(
        outer_halves_kernel,
        out_shape=jax.ShapeDtypeStruct((tall, wide), BF16),
        grid=(wide // cols, tall // rows),
        in_specs=[pl.BlockSpec((depth, rows), lambda n, m: (0, m)), half, half],
        out_specs=pl.BlockSpec((rows, cols), lambda n, m: (m, n)),
        compiler_params=pltpu.CompilerParams(vmem_limit_bytes=56 * 2**20),
        cost_estimate=FREE,
        name="outer_halves",
    )(left, low, high)


def outer_kernel(right_dim, left, right, out):
    out[...] = dot(left[...], right[...], 0, right_dim).astype(BF16)


def outer_gain_kernel(right_dim, cut, left, right, weights, out, gain):
    total = dot(left[...], right[...], 0, right_dim)
    out[...] = total.astype(BF16)
    scaled = total * weights[:, cut[0] : cut[1]].astype(F32)
    gain[...] = jnp.broadcast_to(jnp.sum(scaled, axis=1, keepdims=True), gain.shape)


def outer(left, right, right_dim, weights=None, cut=None):
    depth, high = left.shape
    wide = right.shape[1 - right_dim]
    rows, cols = min(512, high), min(1024, wide)
    right_block = (depth, cols) if right_dim == 0 else (cols, depth)
    right_map = (lambda n, m: (0, n)) if right_dim == 0 else (lambda n, m: (n, 0))
    specs = [pl.BlockSpec((depth, rows), lambda n, m: (0, m)), pl.BlockSpec(right_block, right_map)]
    outs = [jax.ShapeDtypeStruct((high, wide), BF16)]
    out_specs = [pl.BlockSpec((rows, cols), lambda n, m: (m, n))]
    args, kernel = (left, right), functools.partial(outer_kernel, right_dim)
    if weights is not None:
        args, kernel = (left, right, weights), functools.partial(outer_gain_kernel, right_dim, cut)
        specs.append(pl.BlockSpec((rows, weights.shape[1]), lambda n, m: (m, 0)))
        outs.append(jax.ShapeDtypeStruct((high, 128), F32))
        out_specs.append(pl.BlockSpec((rows, 128), lambda n, m: (m, 0)))
    return pl.pallas_call(
        kernel,
        out_shape=outs,
        grid=(wide // cols, high // rows),
        in_specs=specs,
        out_specs=out_specs,
        compiler_params=pltpu.CompilerParams(vmem_limit_bytes=56 * 2**20),
        cost_estimate=FREE,
        name="outer",
    )(*args)


def norm_back(values, scale, upstream):
    mean_term = jnp.mean(values * upstream, axis=1, keepdims=True)
    return scale * upstream - values * (scale * scale * scale) * mean_term


def shards(
    layer_in, lengths, clip_level, attn_gain, w_query, w_key, w_value, w_out,
    mlp_gain, w_gate, w_up, w_down, cotangent,
):
    tok_rows, width = layer_in.shape
    z_rank, y_rank = lax.axis_index("z"), lax.axis_index("y")
    rank = (y_rank * 2 + lax.axis_index("x")) * 2 + lax.axis_index("c")
    slots = lengths.shape[0]
    next_slot = (z_rank + 1) % slots
    info = jnp.stack(
        (rank, lax.dynamic_index_in_dim(lengths, z_rank, keepdims=False),
         lax.dynamic_index_in_dim(lengths, next_slot, keepdims=False))
    ).astype(jnp.int32)
    inner = rank * tok_rows + jnp.arange(tok_rows, dtype=jnp.int32) + LEAD
    own_mask = jnp.where(inner < SLOT_LEN, inner < info[1], inner - SLOT_LEN < info[2])
    own_mask = own_mask.astype(F32)[:, None]
    spots = ((jnp.arange(SLOT_LEN, dtype=jnp.int32) + LEAD) % SLOT_LEN).astype(F32)
    freq = THETA ** (-(jnp.arange(HALF, dtype=F32) * 2.0 / HD))
    angles = spots[None, :] * freq[:, None]
    cos, sin = jnp.cos(angles), jnp.sin(angles)
    def heads_part(which):
        return jnp.concatenate(
            (half_of(w_out, which, 0).T, half_of(w_query, which, 1), half_of(w_key, which, 1),
             half_of(w_value, which, 1)), 1
        )

    def ffn_part(which):
        return jnp.concatenate((half_of(w_gate, which, 1), half_of(w_up, which, 1)), 1)

    other_y = 1 - y_rank
    heads_w = ordered(heads_part(y_rank), swap(heads_part(other_y), "y"), y_rank, 0)
    full_heads = lax.all_gather(heads_w, "z", axis=0, tiled=True)
    out_cols = HEADS * HD
    heads_cut = (out_cols, full_heads.shape[1])

    ffn_own, ffn_sent = tie(ffn_part(y_rank), ffn_part(other_y))
    ffn_w = ordered(ffn_own, swap(ffn_sent, "y"), y_rank, 0)
    layer_f = layer_in.astype(F32)
    scale_one = lax.rsqrt(jnp.mean(layer_f * layer_f, axis=1, keepdims=True) + EPSILON)
    normal_one = rounded(layer_f * scale_one)
    gain_one = attn_gain.astype(F32)
    acts = gather_one(after((normal_one * gain_one[None, :]).astype(BF16), heads_w))
    acts = gather_two(acts)
    full_heads, ffn_w, *acts = tie(full_heads, ffn_w, *acts)
    full_out, full_qkv = full_heads[:, :out_cols], full_heads[:, out_cols:]
    acts_one = gather_three(acts)
    full_ffn = lax.all_gather(ffn_w, "z", axis=0, tiled=True)

    grad_out = cotangent.astype(F32)
    down_in = (RESIDUAL * own_mask * grad_out).astype(BF16)
    back_rows = gather_one(down_in)
    rows = acts_one.shape[0]
    flat = dot(full_qkv, acts_one, 0, 1)
    (qkv,) = call(
        rope_kernel, info, (flat, cos, sin), [((flat.shape[0], rows), BF16)], [], "rope"
    )
    halo = along(qkv[K_AT:, SLOT_LEN - LEAD :], 1)
    qkv, halo, *back_rows = tie(qkv, halo, *back_rows)
    down_other = swap(after(half_of(w_down, other_y, 0), back_rows[2], back_rows[3]), "y")
    back_rows = gather_two(back_rows)
    heads, lse, peak = call(
        attend_kernel, info, (qkv, halo),
        [((HEADS * HD, rows), BF16), ((8, rows), F32), ((8, 128), F32)],
        [((KEYS, HD), BF16), ((HD, KEYS), BF16), ((TOGETHER, SLOT_LEN, CHUNK), F32)],
        "attend",
    )
    heads, *back_rows = tie(heads, *back_rows)

    terms = [(heads, full_heads, 0, 1, (0, out_cols))]
    high_part, own_peak, down_other = tie(product(terms, 1), peak[:HEADS], down_other)
    came, other_peak = tie(swap(high_part, "c"), swap(own_peak, "y"))
    down_w = ordered(half_of(w_down, y_rank, 0), down_other, y_rank, 1)
    branch = spread_one(terms, came)
    head_peak = over_z(ordered(own_peak, other_peak, y_rank, 0), jnp.maximum)
    down_rows = gather_three(back_rows)
    *got, down_rows, down_w, head_peak = tie(*branch[2:4], down_rows, down_w, head_peak)
    head_peak = head_peak[:, 0]
    branch = spread_two((*branch[:2], *got))
    full_down = lax.all_gather(down_w, "z", axis=1, tiled=True)
    gain_two = mlp_gain.astype(F32)
    narrow = (tok_rows, width // 2)
    resid, scale_two, *acts = row_call(
        residual_kernel, (*branch[:4], layer_in, own_mask, gain_two[None, :]),
        [((tok_rows, width), F32), ((tok_rows, 1), F32), ((tok_rows, width), BF16),
         (narrow, BF16), (narrow, BF16)], "residual",
    )
    acts = gather_one(acts[0], acts[1:])
    full_ffn, *acts = tie(full_ffn, *acts)
    acts = gather_two(acts)
    acts_two = gather_three(acts)

    hid = full_ffn.shape[1] // 2
    gate_proj, up_proj, hidden = ffn_call(
        hidden_kernel, acts_two, full_ffn, hid, (F32, F32, BF16), (), "hidden"
    )

    def reduced(grad, axis):
        return lax.psum_scatter(grad, "z", scatter_dimension=axis, tiled=True)

    def traded(total, axis, *behind):
        total = after(total, *behind)
        return half_of(total, y_rank, axis), swap(half_of(total, other_y, axis), "y")

    (down_part,) = outer(hidden, down_rows, 0)
    down_sum = reduced(down_part, 1)
    down_rows = after(down_rows, down_part)
    def grads(part, rows):
        return ffn_call(
            hidden_back_kernel, rows, full_down, hid, (BF16, BF16), (gate_proj, up_proj),
            "hidden_back", part, 2,
        )

    def back_terms(gate_grad, up_grad):
        return [(gate_grad, full_ffn, 1, 1, None, 0), (up_grad, full_ffn, 1, 1, None, 1)]

    high_grads = grads(1, down_rows)
    high_part = product(back_terms(*((None, grad) for grad in high_grads)), 1)
    high_part, down_rows = tie(high_part, down_rows)
    low_grads = grads(0, down_rows)
    came, *low_grads = tie(swap(high_part, "c"), *low_grads)
    pairs = list(zip(low_grads, high_grads, strict=True))
    *norm_two, acts_two = spread_one(back_terms(*pairs), came, acts_two)
    ffn_parts = [outer_halves(acts_two, *pair) for pair in pairs]
    *got, ffn_parts[0], ffn_parts[1] = tie(*norm_two[2:4], *ffn_parts)
    one_sum, two_sum = [reduced(part, 0) for part in ffn_parts]
    norm_two = spread_two((*norm_two[:2], *got))
    gain_two_part, grad_resid, *mixed = row_call(
        residual_back_kernel,
        (*norm_two[:4], cotangent, resid, scale_two, gain_two[None, :], own_mask),
        [((8, width), F32), ((tok_rows, width), F32), ((tok_rows, width), BF16), (narrow, BF16),
         (narrow, BF16)], "residual_back",
    )
    mixed_in, hidden = tie(mixed[0], hidden)
    mixed = gather_one(mixed_in, mixed[1:])
    terms = [(hidden, full_down, 1, 0, None)]
    *got, high_part = tie(*mixed[2:4], product(terms, 1))
    mixed = gather_two((*mixed[:2], *got))
    low_part = product(terms, 0, swap(high_part, "c"))
    a1, b1, *low_part = tie(*mixed[5:], *low_part)
    mixed = (*mixed[:5], a1, b1)
    second = (*low_part[:2], swap(low_part[2], "x"), swap(low_part[3], "y"))
    mixed_rows = gather_three(mixed)
    mixed_rows, down_sum, one_sum = tie(mixed_rows, down_sum, one_sum)
    down_own, down_other = traded(down_sum, 1)
    one_own, one_other = traded(one_sum, 0)

    heads_grad = dot(full_out, mixed_rows, 0, 1).astype(BF16)
    dq, dkv, back = call(
        attend_back_kernel, info, (qkv, halo, heads_grad, lse, cos, sin),
        [((HEADS * HD, rows), BF16), ((2 * HD, rows), F32), ((2 * HD, LEAD), BF16)],
        [((KEYS, HD), BF16), ((KEYS, HD), BF16), ((HD, KEYS), BF16),
         ((TOGETHER, SLOT_LEN, CHUNK), F32), ((TOGETHER, SLOT_LEN, CHUNK), F32),
         ((KEYS, HD), F32), ((KEYS, HD), F32), ((HEADS * HD, SLOT_LEN), BF16)],
        "attend_back", 60,
    )
    back, down_other, one_other, *got = tie(back, down_other, one_other, *second[2:4])
    back_sent = along(back, -1)
    left, right, *sent = fold(*second[:2], *got)
    (out_part,) = outer(mixed_rows, heads, 1)
    dkv, back_sent, out_part, *sent = tie(dkv, back_sent, out_part, *sent)
    out_sum = reduced(out_part, 0)
    second = left, right, swap(sent[0], "y"), swap(sent[1], "x")
    (dkv_done,) = call(
        finish_kernel, info, (dkv, back_sent, cos, sin), [((2 * HD, rows), BF16)], [], "finish"
    )
    dqkv = jnp.concatenate((dq, dkv_done))
    terms = [(dqkv, full_heads, 0, 1, heads_cut)]
    high_part, acts_one = tie(product(terms, 1), acts_one)
    qkv_part, sums = outer(acts_one, dqkv, 1, full_heads, heads_cut)
    came, qkv_part, sums, two_sum, *got = tie(
        swap(high_part, "c"), qkv_part, sums, two_sum, *second[2:4]
    )
    two_own = half_of(two_sum, y_rank, 0)
    came, two_sent = tie(came, half_of(two_sum, other_y, 0))
    qkv_sum = reduced(qkv_part, 0)
    second = (*second[:2], *got)
    *norm_one, sums, two_other = spread_one(terms, came, sums, swap(two_sent, "y"))
    gains = jnp.stack((sums[:, 0] / gain_one, jnp.sum(gain_two_part, axis=0)))
    gains = over_z(gains, jnp.add)
    gains, down_own, down_other, one_own, one_other, head_peak, *second = tie(
        gains, down_own, down_other, one_own, one_other, head_peak, *second
    )
    down_grad = ordered(down_own, down_other, y_rank, 0).astype(F32)
    gate_w_grad = ordered(one_own, one_other, y_rank, 1).astype(F32)
    level = clip_level[0].astype(F32) * LEVEL_UNIT
    factor = level / jnp.maximum(level, head_peak)
    query_clipped = w_query.astype(F32) * jnp.repeat(jnp.sqrt(factor), HD)[None, :]
    result = (resid + RESIDUAL * own_mask * spread_three(second)).astype(BF16)
    *got, gains, out_sum, down_grad, gate_w_grad, query_clipped, result = tie(
        *norm_one[2:4], gains, out_sum, down_grad, gate_w_grad, query_clipped, result
    )
    gains = gains.reshape(2, lax.axis_size("z"), 2, 2, 2, -1)

    def halved(gains, dim, axis):
        at = lax.axis_index(axis)
        return (lax.dynamic_index_in_dim(gains, at, dim, keepdims=False),
                lax.dynamic_index_in_dim(gains, 1 - at, dim, keepdims=False))

    norm_one = spread_two((*norm_one[:2], *got), gains, folding=fold)
    gains = norm_one[4]
    out_own, out_sent = half_of(out_sum, y_rank, 0), half_of(out_sum, other_y, 0)
    own, qkv_sent = half_of(qkv_sum, y_rank, 0), half_of(qkv_sum, other_y, 0)
    kept, sent = halved(gains, 4, "c")
    kept, sent = halved(kept + swap(sent, "c"), 3, "x")
    *norm_one, qkv_sent, kept, sent, out_sent = tie(*norm_one[:4], qkv_sent, kept, sent, out_sent)
    other, out_other = swap(qkv_sent, "y"), swap(out_sent, "y")
    grad_input = input_back(*norm_one, grad_resid, layer_in, scale_one, gain_one[None, :])
    kept, sent = halved(kept + swap(sent, "x"), 2, "y")
    gains = lax.dynamic_index_in_dim(kept + swap(sent, "y"), z_rank, 1, keepdims=False)

    up_w_grad = ordered(two_own, two_other, y_rank, 1).astype(F32)
    out_grad = ordered(out_own.T, out_other.T, y_rank, 0).astype(F32)

    def columns(start, stop):
        return ordered(own[:, start:stop], other[:, start:stop], y_rank, 1).astype(F32)

    query_grad = columns(0, K_AT)
    key_grad = columns(K_AT, V_AT)
    value_grad = columns(V_AT, V_AT + HD)

    kv_factor = jnp.min(factor.reshape(-1, HEADS), axis=1)
    key_clipped = w_key.astype(F32) * jnp.repeat(jnp.sqrt(kv_factor), HD)[None, :]
    return (
        result,
        grad_input,
        gains[0],
        query_grad,
        key_grad,
        value_grad,
        out_grad,
        gains[1],
        gate_w_grad,
        up_w_grad,
        down_grad,
        query_clipped,
        key_clipped,
    )


def solution(mesh):
    fsdp, tp = mesh.shape["fsdp"], mesh.shape["tp"]
    fine = Mesh(mesh.devices.reshape(fsdp // 2, 2, tp // 2, 2), EVERY)
    rows, cols = ("z", "y"), ("x", "c")
    tokens, down, across = P(EVERY, None), P(rows, cols), P(cols, rows)
    in_specs = (
        tokens, P(), P(), P(), down, down, down, across, P(), down, down, across, tokens,
    )
    out_specs = (
        tokens, tokens, P(EVERY), down, down, down, across, P(EVERY), down, down, across,
        down, down,
    )
    return jax.shard_map(shards, mesh=fine, in_specs=in_specs, out_specs=out_specs, check_vma=False)
```

```python
import functools

import jax
import jax.numpy as jnp
from jax import lax
from jax.experimental import pallas as pl
from jax.experimental.pallas import tpu as pltpu
from jax.sharding import Mesh
from jax.sharding import PartitionSpec as P

HD = 64
HALF = HD // 2
SLOT_LEN = 2048
LEAD = 512
CHUNK = 512
BLOCK = 256
HEADS = 4

EPSILON = 1e-05
THETA = 10000000.0
MULTIPLIER = 0.015625
RESIDUAL = 0.22
LEVEL_UNIT = 0.125
NEGATIVE = -1e30
GROUP = ("y", "x", "c")
EVERY = ("z", "y", "x", "c")
F32 = jnp.float32
BF16 = jnp.bfloat16
FREE = pl.CostEstimate(flops=0, bytes_accessed=0, transcendentals=0)


def rounded(x):
    return lax.reduce_precision(x, exponent_bits=8, mantissa_bits=7)


def swap(x, axis):
    return lax.ppermute(x, axis, [(0, 1), (1, 0)])


def along(x, by):
    peers = lax.axis_size("z")
    return lax.ppermute(x, "z", [(i, (i + by) % peers) for i in range(peers)])


def dot(left, right, left_dim, right_dim):
    return lax.dot_general(
        left, right, (((left_dim,), (right_dim,)), ((), ())), preferred_element_type=F32
    )


def half_of(x, which, axis):
    size = x.shape[axis] // 2
    return lax.dynamic_slice_in_dim(x, which * size, size, axis)


def ordered(own, other, rank, axis):
    return jnp.where(
        rank == 0,
        jnp.concatenate((own, other), axis=axis),
        jnp.concatenate((other, own), axis=axis),
    )


def after(x, *others):
    return lax.optimization_barrier((x, *others))[0]


def tie(*xs):
    return lax.optimization_barrier(xs)


def gather_one(v, halves=None):
    half = v.shape[1] // 2
    halves = (v[:, :half], v[:, half:]) if halves is None else halves
    return v, swap(v, "c"), swap(halves[0], "x"), swap(halves[1], "y")


def gather_two(state):
    v, near, a01, b10 = state
    half = v.shape[1] // 2
    a1 = swap(jnp.concatenate((v[:, :half], a01)), "y")
    b1 = swap(jnp.concatenate((v[:, half:], b10)), "x")
    second = swap(jnp.concatenate((a01, b10)), "c")
    return v, near, a01, b10, second, a1, b1


def gather_three(state):
    size, half = state[0].shape[0], state[0].shape[1] // 2
    state = (state[0], *tie(*state[1:]))
    third = swap(jnp.concatenate(state[5:]), "c")
    spots = (
        (0, 0, size, 0, 0), (1, 0, size, 4 * size, 0), (2, 0, size, size, 0),
        (3, 0, size, 2 * size, half), (4, 0, size, 5 * size, 0),
        (4, size, size, 6 * size, half), (5, 0, 2 * size, 2 * size, 0),
        (6, 0, size, size, half), (6, size, size, 3 * size, half),
        (7, 0, 2 * size, 6 * size, 0), (7, 2 * size, size, 5 * size, half),
        (7, 3 * size, size, 7 * size, half),
    )
    return place((*state, third), spots, 8 * size)


def place_kernel(spots, count, *refs):
    pieces, out, held = refs[:count], refs[count], refs[count + 1 : 2 * count + 1]
    load_sems, sems = refs[-2:]
    loads = [
        pltpu.make_async_copy(piece, here, load_sems.at[i])
        for i, (piece, here) in enumerate(zip(pieces, held, strict=True))
    ]
    for load in loads:
        load.start()
    copies = []
    for i, load in enumerate(loads):
        load.wait()
        for at, (piece, start, size, row, col) in enumerate(spots):
            if piece == i:
                source = held[piece]
                copy = pltpu.make_async_copy(
                    source.at[pl.ds(start, size), :],
                    out.at[pl.ds(row, size), pl.ds(col, source.shape[1])],
                    sems.at[at],
                )
                copy.start()
                copies.append(copy)
    for copy in copies:
        copy.wait()


def place(pieces, spots, count):
    number = len(pieces)
    return pl.pallas_call(
        functools.partial(place_kernel, spots, number),
        out_shape=jax.ShapeDtypeStruct((count, pieces[0].shape[1]), BF16),
        in_specs=[pl.BlockSpec(memory_space=pl.ANY)] * number,
        out_specs=pl.BlockSpec(memory_space=pltpu.HBM),
        scratch_shapes=[pltpu.VMEM(piece.shape, BF16) for piece in pieces]
        + [pltpu.SemaphoreType.DMA((number,)), pltpu.SemaphoreType.DMA((len(spots),))],
        compiler_params=pltpu.CompilerParams(vmem_limit_bytes=60 * 2**20),
        cost_estimate=FREE,
        name="place",
    )(*pieces)


def product_kernel(terms, keep, *refs):
    count = len(terms)
    step = pl.program_id(0)
    flipped = sum(term[0] == 0 for term in terms)
    scratch = refs[len(refs) - flipped :]
    total, used = None, 0
    for at, (left_dim, right_dim, cut) in enumerate(terms):
        left, right = refs[2 * at], refs[2 * at + 1]
        if left_dim == 0:
            store = scratch[used]
            used += 1

            @pl.when(step == 0)
            def _(left=left, store=store):
                store[...] = upright(left[...])

            left = store
        block = right[...] if cut is None else right[:, cut[0] : cut[1]]
        one = dot(left[...], block, 1, right_dim)
        total = one if total is None else total + one
    if not keep:
        refs[2 * count][...] = total.astype(BF16)
        return
    came, left_out, right_out, x_out, y_out = refs[2 * count : 2 * count + 5]
    total = total + came[...].astype(F32)
    blocks = total.reshape(2, 2, total.shape[0] // 4, total.shape[1])
    half = pl.num_programs(0) // 2

    @pl.when(step < half)
    def _():
        left_out[...] = blocks[:, 0]
        x_out[...] = blocks[:, 1].astype(BF16)

    @pl.when(step >= half)
    def _():
        right_out[...] = blocks[0]
        y_out[...] = blocks[1].astype(BF16)


def product(terms, part, came=None):
    tile = 512
    args, specs, kinds, scratch = [], [], [], []
    for left, right, left_dim, right_dim, cut, *block in terms:
        whole = not isinstance(left, tuple)
        at = part if whole else 0
        left = left if whole else left[part]
        rows = left.shape[1 - left_dim] // (2 if whole else 1)
        depth = left.shape[left_dim]
        if left_dim == 1:
            specs.append(pl.BlockSpec((rows, depth), lambda n, at=at: (at, 0)))
        else:
            specs.append(pl.BlockSpec((depth, rows), lambda n: (0, part)))
            scratch.append(pltpu.VMEM((rows, depth), BF16))
        if right_dim == 1:
            width = right.shape[0]
            if block:
                specs.append(pl.BlockSpec((tile, depth), lambda n, to=block[0]: (n, to)))
            else:
                specs.append(pl.BlockSpec((tile, right.shape[1]), lambda n: (n, 0)))
        else:
            width = right.shape[1]
            specs.append(pl.BlockSpec((right.shape[0], tile), lambda n: (0, n)))
        args += [left, right]
        kinds.append((left_dim, right_dim, cut))
    if came is None:
        out_shape = jax.ShapeDtypeStruct((rows, width), BF16)
        out_specs = pl.BlockSpec((rows, tile), lambda n: (0, n))
    else:
        args.append(came)
        specs.append(pl.BlockSpec((rows, tile), lambda n: (0, n)))
        half = width // tile // 2
        shape = (2, rows // 4, width // 2)
        out_shape = [jax.ShapeDtypeStruct(shape, d) for d in (F32, F32, BF16, BF16)]
        first = pl.BlockSpec((2, rows // 4, tile), lambda n: (0, 0, jnp.minimum(n, half - 1)))
        last = pl.BlockSpec((2, rows // 4, tile), lambda n: (0, 0, jnp.maximum(n - half, 0)))
        out_specs = [first, last, first, last]
    return pl.pallas_call(
        functools.partial(product_kernel, kinds, came is not None),
        out_shape=out_shape,
        grid=(width // tile,),
        in_specs=specs,
        out_specs=out_specs,
        scratch_shapes=scratch,
        compiler_params=pltpu.CompilerParams(vmem_limit_bytes=56 * 2**20),
        cost_estimate=FREE,
        name="product",
    )(*args)


def spread_one(terms, came=None, *later):
    came = swap(product(terms, 1), "c") if came is None else came
    left, right, send_x, send_y = product(terms, 0, came)
    if later:
        send_x, send_y, *later = tie(send_x, send_y, *later)
    return left, right, swap(send_x, "x"), swap(send_y, "y"), *later


ROWS = 64


def fold_kernel(left, right, left_x, right_y, left_out, right_out, y_out, x_out):
    total = left[...] + left_x[...].astype(F32)
    left_out[...], y_out[...] = total[0], total[1].astype(BF16)
    total = right[...] + right_y[...].astype(F32)
    right_out[...], x_out[...] = total[0], total[1].astype(BF16)


def fold(*parts):
    rows, cols = parts[0].shape[1:]
    size = rows // 2
    return pl.pallas_call(
        fold_kernel,
        out_shape=[jax.ShapeDtypeStruct((rows, cols), d) for d in (F32, F32, BF16, BF16)],
        grid=(2,),
        in_specs=[pl.BlockSpec((2, size, cols), lambda i: (0, i, 0))] * 4,
        out_specs=[pl.BlockSpec((size, cols), lambda i: (i, 0))] * 4,
        cost_estimate=FREE,
        name="fold",
    )(*parts)


def resident(kernel, args, outs, name):
    spec = pl.BlockSpec(memory_space=pltpu.VMEM)
    return pl.pallas_call(
        kernel,
        out_shape=[jax.ShapeDtypeStruct(shape, kind) for shape, kind in outs],
        in_specs=[spec] * len(args),
        out_specs=[spec] * len(outs),
        compiler_params=pltpu.CompilerParams(vmem_limit_bytes=24 * 2**20),
        cost_estimate=FREE,
        name=name,
    )(*args)


def fold_loop_kernel(left, right, left_x, right_y, left_out, right_out, y_out, x_out):
    @pl.loop(0, left.shape[1] // ROWS)
    def _(i):
        here = pl.ds(pl.multiple_of(i * ROWS, ROWS), ROWS)
        total = left[:, here, :] + left_x[:, here, :].astype(F32)
        left_out[here, :], y_out[here, :] = total[0], total[1].astype(BF16)
        total = right[:, here, :] + right_y[:, here, :].astype(F32)
        right_out[here, :], x_out[here, :] = total[0], total[1].astype(BF16)


def fold_resident(*parts):
    shape = parts[0].shape[1:]
    return resident(fold_loop_kernel, parts, [(shape, d) for d in (F32, F32, BF16, BF16)], "fold")


def spread_two(state, *extra, folding=fold_resident):
    left, right, send_y, send_x = folding(*state[:4])
    if extra:
        send_y, send_x, *extra = tie(send_y, send_x, *extra)
    return left, right, swap(send_y, "y"), swap(send_x, "x"), *extra


def spread_three(state):
    left, right, left_y, right_x = state[:4]
    return jnp.concatenate((left + left_y.astype(F32), right + right_x.astype(F32)), axis=1)


def joined(left, right, left_y, right_x):
    return jnp.concatenate(
        (left[...] + left_y[...].astype(F32), right[...] + right_x[...].astype(F32)), axis=1
    )


def store_halves(value, out, left_out, right_out):
    half = value.shape[1] // 2
    out[...], left_out[...], right_out[...] = value, value[:, :half], value[:, half:]


def residual_kernel(*refs):
    values, mask, gain = (ref[...] for ref in refs[4:7])
    resid_out, scale_out = refs[7:9]
    resid = values.astype(F32) + RESIDUAL * mask * joined(*refs[:4])
    scale = lax.rsqrt(jnp.mean(resid * resid, axis=1, keepdims=True) + EPSILON)
    resid_out[...], scale_out[...] = resid, scale
    normal = (resid * scale).astype(BF16).astype(F32)
    store_halves((normal * gain).astype(BF16), *refs[9:12])


def residual_back_kernel(*refs):
    base, values, scale, gain, mask = (ref[...] for ref in refs[4:9])
    sums, grad_out = refs[9:11]
    upstream = joined(*refs[:4])
    normal = (values * scale).astype(BF16).astype(F32)
    share = normal * upstream
    sums[...] += jnp.sum(share.reshape(-1, 8, share.shape[1]), axis=0)
    grad = base.astype(F32) + norm_back(values, scale, gain * upstream)
    grad_out[...] = grad
    store_halves((RESIDUAL * mask * grad).astype(BF16), *refs[11:14])


def input_back_kernel(*refs):
    base, values, scale, gain = (ref[...] for ref in refs[4:8])
    grad = base + norm_back(values.astype(F32), scale, gain * joined(*refs[:4]))
    refs[8][...] = grad.astype(BF16)


def input_back(*args):
    rows, width = args[4].shape

    def spec(shape):
        if shape[0] == rows:
            return pl.BlockSpec((ROWS, shape[1]), lambda i: (i, 0))
        return pl.BlockSpec(shape, lambda i: (0, 0))

    return pl.pallas_call(
        input_back_kernel,
        out_shape=jax.ShapeDtypeStruct((rows, width), BF16),
        grid=(rows // ROWS,),
        in_specs=[spec(arg.shape) for arg in args],
        out_specs=spec((rows, width)),
        cost_estimate=FREE,
        name="input_back",
    )(*args)


def row_call(kernel, args, outs, name):
    rows = args[0].shape[0]

    def looped(*refs):
        for ref in refs[len(args) :]:
            if ref.shape[0] == 8:
                ref[...] = jnp.zeros(ref.shape, F32)

        @pl.loop(0, rows // ROWS)
        def _(i):
            here = pl.ds(pl.multiple_of(i * ROWS, ROWS), ROWS)
            kernel(*(ref.at[here, :] if ref.shape[0] == rows else ref for ref in refs))

    return resident(looped, args, outs, name)


def over_z(x, combine):
    peers, step = lax.axis_size("z"), 1
    assert peers & (peers - 1) == 0
    while step < peers:
        x = combine(x, along(x, step))
        step *= 2
    return x


def place_of(block, rank):
    j = jnp.bitwise_xor(block, rank)
    return jnp.bitwise_or(jnp.left_shift(jnp.bitwise_and(j, 1), 2), jnp.right_shift(j, 1))


def lanes_of(block, rank):
    return pl.ds(pl.multiple_of(place_of(block, rank) * BLOCK, BLOCK), BLOCK)


def rope_kernel(info, qkv, cos, sin, out):
    rank = info[0]

    @pl.loop(0, SLOT_LEN // BLOCK)
    def _(block):
        source = lanes_of(block, rank)
        target = pl.ds(pl.multiple_of(block * BLOCK, BLOCK), BLOCK)
        c, s = cos[:, target], sin[:, target]
        for head in range(HEADS + 1):
            first = qkv[pl.ds(head * HD, HALF), source]
            second = qkv[pl.ds(head * HD + HALF, HALF), source]
            scale = MULTIPLIER if head < HEADS else 1.0
            out[pl.ds(head * HD, HALF), target] = ((first * c - second * s).astype(BF16) * scale).astype(BF16)
            out[pl.ds(head * HD + HALF, HALF), target] = ((second * c + first * s).astype(BF16) * scale).astype(BF16)
        rest = (HEADS + 1) * HD
        out[pl.ds(rest, HD), target] = qkv[pl.ds(rest, HD), source].astype(BF16)


TOGETHER = 4
KEYS = SLOT_LEN + LEAD
K_AT = HEADS * HD
V_AT = K_AT + HD


def upright(x):
    return x.astype(F32).T.astype(BF16)


def causal():
    keys = lax.broadcasted_iota(jnp.int32, (CHUNK, CHUNK), 0)
    queries = lax.broadcasted_iota(jnp.int32, (CHUNK, CHUNK), 1)
    return keys <= queries


def key_range(step):
    last = step == SLOT_LEN // CHUNK - 1
    low = jnp.where(last, KEYS // CHUNK - 1, 0)
    high = jnp.where(last, KEYS // CHUNK, step + 2)
    return low, high


def chunk_of(i):
    return pl.ds(pl.multiple_of(i * CHUNK, CHUNK), CHUNK)


def head_rows(h):
    return pl.ds(pl.multiple_of(h * HD, HD), HD)


def attend_kernel(info, qkv, halo, heads_out, lse_out, peak_out, k_up, v_flat, scores):
    rank = info[0]
    k_up[pl.ds(0, LEAD), :] = upright(halo[pl.ds(0, HD), :])
    v_flat[:, pl.ds(0, LEAD)] = halo[pl.ds(HD, HD), :]
    v_flat[:, pl.ds(LEAD, SLOT_LEN)] = qkv[pl.ds(V_AT, HD), :]

    @pl.loop(0, SLOT_LEN // CHUNK)
    def _(i):
        k_up[pl.ds(pl.multiple_of(LEAD + i * CHUNK, CHUNK), CHUNK), :] = upright(
            qkv[pl.ds(K_AT, HD), chunk_of(i)]
        )

    peak_out[...] = jnp.full(peak_out.shape, NEGATIVE, F32)
    lse_out[...] = jnp.zeros(lse_out.shape, F32)

    @pl.loop(0, HEADS // TOGETHER)
    def _(group):
        @pl.loop(0, SLOT_LEN // CHUNK)
        def _(step):
            low, high = key_range(step)
            heads = [group * TOGETHER + i for i in range(TOGETHER)]
            query = [qkv[head_rows(h), chunk_of(step)] for h in heads]

            def raw(kc, i):
                return jnp.dot(k_up[chunk_of(kc), :], query[i], preferred_element_type=F32)

            def first(kc, tops):
                outs = []
                for i in range(TOGETHER):
                    s = raw(kc, i)
                    scores[i, chunk_of(kc - low)] = s
                    outs.append(jnp.maximum(tops[i], jnp.max(s, axis=0, keepdims=True)))
                return tuple(outs)

            tops = []
            for i in range(TOGETHER):
                s = jnp.where(causal(), raw(high - 1, i), NEGATIVE)
                scores[i, chunk_of(high - 1 - low)] = s
                tops.append(jnp.max(s, axis=0, keepdims=True))
            tops = lax.fori_loop(low, high - 1, first, tuple(tops))

            def second(kc, totals):
                outs = []
                for i in range(TOGETHER):
                    e = jnp.exp(scores[i, chunk_of(kc)] - tops[i])
                    scores[i, chunk_of(kc)] = e
                    outs.append(totals[i] + jnp.sum(e, axis=0, keepdims=True))
                return tuple(outs)

            totals = lax.fori_loop(0, high - low, second, (jnp.zeros((1, CHUNK), F32),) * TOGETHER)
            inverses = [1.0 / total for total in totals]

            def third(kc, mixed):
                outs = []
                for i in range(TOGETHER):
                    probs = (scores[i, chunk_of(kc)] * inverses[i]).astype(BF16)
                    more = jnp.dot(
                        v_flat[:, chunk_of(kc + low)], probs, preferred_element_type=F32
                    )
                    outs.append(mixed[i] + more)
                return tuple(outs)

            mixed_all = lax.fori_loop(
                0, high - low, third, (jnp.zeros((HD, CHUNK), F32),) * TOGETHER
            )
            last = step == SLOT_LEN // CHUNK - 1
            start = jnp.where(last, 0, LEAD + step * CHUNK)
            alive = jnp.where(last, info[2], info[1])
            spots = lax.broadcasted_iota(jnp.int32, (1, CHUNK), 1) + start
            for i, h in enumerate(heads):
                mixed = mixed_all[i].astype(BF16)
                for part in range(CHUNK // BLOCK):
                    there = lanes_of(step * (CHUNK // BLOCK) + part, rank)
                    heads_out[head_rows(h), there] = mixed[:, part * BLOCK : (part + 1) * BLOCK]
                lse_out[pl.ds(h, 1), chunk_of(step)] = tops[i] + jnp.log(totals[i])
                best = jnp.where(spots < alive, tops[i], NEGATIVE)
                best = jnp.max(best, axis=1, keepdims=True)
                peak_out[pl.ds(h, 1), :] = jnp.maximum(peak_out[pl.ds(h, 1), :], best)


def attend_back_kernel(
    info, qkv, halo, upstream, lse, cos, sin, dq_out, dkv_out, halo_out,
    k_up, v_up, k_flat, probs_s, grads_s, dk_s, dv_s, up_abs,
):
    rank = info[0]
    k_up[pl.ds(0, LEAD), :] = upright(halo[pl.ds(0, HD), :])
    v_up[pl.ds(0, LEAD), :] = upright(halo[pl.ds(HD, HD), :])
    k_flat[:, pl.ds(0, LEAD)] = halo[pl.ds(0, HD), :]
    k_flat[:, pl.ds(LEAD, SLOT_LEN)] = qkv[pl.ds(K_AT, HD), :]

    @pl.loop(0, SLOT_LEN // CHUNK)
    def _(i):
        rows = pl.ds(pl.multiple_of(LEAD + i * CHUNK, CHUNK), CHUNK)
        k_up[rows, :] = upright(qkv[pl.ds(K_AT, HD), chunk_of(i)])
        v_up[rows, :] = upright(qkv[pl.ds(V_AT, HD), chunk_of(i)])

    @pl.loop(0, SLOT_LEN // BLOCK)
    def _(block):
        target = pl.ds(pl.multiple_of(block * BLOCK, BLOCK), BLOCK)
        up_abs[:, target] = upstream[:, lanes_of(block, rank)]

    dk_s[...] = jnp.zeros(dk_s.shape, F32)
    dv_s[...] = jnp.zeros(dv_s.shape, F32)

    @pl.loop(0, HEADS // TOGETHER)
    def _(group):
        @pl.loop(0, SLOT_LEN // CHUNK)
        def _(step):
            low, high = key_range(step)
            here = chunk_of(step)
            heads = [group * TOGETHER + i for i in range(TOGETHER)]
            query = [qkv[head_rows(h), here] for h in heads]
            grad = [up_abs[head_rows(h), here] for h in heads]
            query_up, grad_up = [upright(x) for x in query], [upright(x) for x in grad]
            logs = [lse[pl.ds(h, 1), here] for h in heads]

            def spot(i, kc):
                return i, chunk_of(kc - low)

            def one(kc, masked):
                deltas, added = [], None
                for i in range(TOGETHER):
                    s = jnp.dot(k_up[chunk_of(kc), :], query[i], preferred_element_type=F32)
                    p = jnp.exp(s - logs[i])
                    if masked:
                        p = jnp.where(causal(), p, 0.0)
                    g = jnp.dot(v_up[chunk_of(kc), :], grad[i], preferred_element_type=F32)
                    probs_s[spot(i, kc)] = p
                    grads_s[spot(i, kc)] = g
                    more = jnp.dot(p.astype(BF16), grad_up[i], preferred_element_type=F32)
                    added = more if added is None else added + more
                    deltas.append(jnp.sum(p * g, axis=0, keepdims=True))
                dv_s[chunk_of(kc), :] += added
                return tuple(deltas)

            def both(kc, deltas):
                return tuple(d + e for d, e in zip(deltas, one(kc, False), strict=True))

            deltas = lax.fori_loop(low, high - 1, both, one(high - 1, True))

            def two(kc, dqs):
                outs, added = [], None
                for i in range(TOGETHER):
                    p, g = probs_s[spot(i, kc)], grads_s[spot(i, kc)]
                    ds = (p * (g - deltas[i])).astype(BF16)
                    more = jnp.dot(ds, query_up[i], preferred_element_type=F32)
                    added = more if added is None else added + more
                    outs.append(
                        dqs[i] + jnp.dot(k_flat[:, chunk_of(kc)], ds, preferred_element_type=F32)
                    )
                dk_s[chunk_of(kc), :] += added
                return tuple(outs)

            zero = jnp.zeros((HD, CHUNK), F32)
            dqs = lax.fori_loop(low, high, two, (zero,) * TOGETHER)
            c, s = cos[:, here], sin[:, here]
            for i in range(TOGETHER):
                dq = dqs[i] * MULTIPLIER
                u1, u2 = dq[:HALF], dq[HALF:]
                t1, t2 = (u1 * c + u2 * s).astype(BF16), (u2 * c - u1 * s).astype(BF16)
                at = heads[i] * HD
                for part in range(CHUNK // BLOCK):
                    there = lanes_of(step * (CHUNK // BLOCK) + part, rank)
                    cut = slice(part * BLOCK, (part + 1) * BLOCK)
                    dq_out[pl.ds(pl.multiple_of(at, HD), HALF), there] = t1[:, cut]
                    dq_out[pl.ds(pl.multiple_of(at + HALF, HALF), HALF), there] = t2[:, cut]

    halo_out[pl.ds(0, HD), :] = dk_s[pl.ds(0, LEAD), :].T.astype(BF16)
    halo_out[pl.ds(HD, HD), :] = dv_s[pl.ds(0, LEAD), :].T.astype(BF16)

    @pl.loop(0, SLOT_LEN // CHUNK)
    def _(i):
        rows = pl.ds(pl.multiple_of(LEAD + i * CHUNK, CHUNK), CHUNK)
        dkv_out[pl.ds(0, HD), chunk_of(i)] = dk_s[rows, :].T
        dkv_out[pl.ds(HD, HD), chunk_of(i)] = dv_s[rows, :].T


def finish_kernel(info, dkv, halo, cos, sin, out):
    rank = info[0]
    owned = (SLOT_LEN - LEAD) // BLOCK
    for block in range(SLOT_LEN // BLOCK):
        source = pl.ds(block * BLOCK, BLOCK)
        target = lanes_of(block, rank)
        c, s = cos[:, source], sin[:, source]
        u1, u2 = dkv[pl.ds(0, HALF), source], dkv[pl.ds(HALF, HALF), source]
        rest = dkv[pl.ds(HD, HD), source]
        if block >= owned:
            part = pl.ds((block - owned) * BLOCK, BLOCK)
            u1 = u1 + halo[pl.ds(0, HALF), part].astype(F32)
            u2 = u2 + halo[pl.ds(HALF, HALF), part].astype(F32)
            rest = rest + halo[pl.ds(HD, HD), part].astype(F32)
        out[pl.ds(0, HALF), target] = (u1 * c + u2 * s).astype(BF16)
        out[pl.ds(HALF, HALF), target] = (u2 * c - u1 * s).astype(BF16)
        out[pl.ds(HD, HD), target] = rest.astype(BF16)


def call(kernel, info, args, outs, scratch, name, limit=40):
    spec = pl.BlockSpec(memory_space=pltpu.VMEM)
    return pl.pallas_call(
        kernel,
        out_shape=[jax.ShapeDtypeStruct(s, d) for s, d in outs],
        in_specs=[pl.BlockSpec(memory_space=pltpu.SMEM)] + [spec] * len(args),
        out_specs=[spec] * len(outs),
        scratch_shapes=[pltpu.VMEM(s, d) for s, d in scratch],
        compiler_params=pltpu.CompilerParams(vmem_limit_bytes=limit * 2**20),
        cost_estimate=FREE,
        name=name,
    )(info, *args)


def hidden_kernel(rows, gate_w, up_w, gate_out, up_out, hidden_out):
    gate, up = dot(rows[...], gate_w[...], 1, 0), dot(rows[...], up_w[...], 1, 0)
    gate_out[...], up_out[...] = gate, up
    hidden_out[...] = (gate * jax.nn.sigmoid(gate) * up).astype(BF16)


def hidden_back_kernel(rows, weights, gates, ups, gate_out, up_out):
    grad = dot(rows[...], weights[...], 1, 1)
    gate = gates[...]
    sig = jax.nn.sigmoid(gate)
    gate_out[...] = (grad * ups[...] * sig * (1.0 + gate * (1.0 - sig))).astype(BF16)
    up_out[...] = (grad * gate * sig).astype(BF16)


def ffn_call(kernel, rows, weights, width, kinds, held, name, part=0, parts=1):
    high, wide = min(256 if held else 512, rows.shape[0]), min(1024, width)
    depth, steps = rows.shape[1], width // wide
    count = rows.shape[0] // parts
    skip = part * (count // high)
    tile = pl.BlockSpec((high, wide), lambda n, m: (m, n))
    held_tile = pl.BlockSpec((high, wide), lambda n, m: (m + skip, n))
    if held:
        specs = [pl.BlockSpec((wide, depth), lambda n, m: (n, 0))]
    else:
        specs = [pl.BlockSpec((depth, wide), lambda n, m: (0, n)),
                 pl.BlockSpec((depth, wide), lambda n, m: (0, n + steps))]
    return pl.pallas_call(
        kernel,
        out_shape=[jax.ShapeDtypeStruct((count, width), kind) for kind in kinds],
        grid=(steps, count // high),
        in_specs=[pl.BlockSpec((high, depth), lambda n, m: (m + skip, 0))]
        + specs
        + [held_tile] * len(held),
        out_specs=[tile] * len(kinds),
        compiler_params=pltpu.CompilerParams(vmem_limit_bytes=56 * 2**20),
        cost_estimate=FREE,
        name=name,
    )(rows, *([weights] * len(specs)), *held)


def outer_halves_kernel(left, low, high, out):
    rows = low.shape[0]
    total = dot(left[:rows], low[...], 0, 0) + dot(left[rows:], high[...], 0, 0)
    out[...] = total.astype(BF16)


def outer_halves(left, low, high):
    (depth, tall), wide = left.shape, low.shape[1]
    rows, cols = min(512, tall), min(1024, wide)
    half = pl.BlockSpec((depth // 2, cols), lambda n, m: (0, n))
    return pl.pallas_call(
        outer_halves_kernel,
        out_shape=jax.ShapeDtypeStruct((tall, wide), BF16),
        grid=(wide // cols, tall // rows),
        in_specs=[pl.BlockSpec((depth, rows), lambda n, m: (0, m)), half, half],
        out_specs=pl.BlockSpec((rows, cols), lambda n, m: (m, n)),
        compiler_params=pltpu.CompilerParams(vmem_limit_bytes=56 * 2**20),
        cost_estimate=FREE,
        name="outer_halves",
    )(left, low, high)


def outer_kernel(right_dim, left, right, out):
    out[...] = dot(left[...], right[...], 0, right_dim).astype(BF16)


def outer_gain_kernel(right_dim, cut, left, right, weights, out, gain):
    total = dot(left[...], right[...], 0, right_dim)
    out[...] = total.astype(BF16)
    scaled = total * weights[:, cut[0] : cut[1]].astype(F32)
    gain[...] = jnp.broadcast_to(jnp.sum(scaled, axis=1, keepdims=True), gain.shape)


def outer(left, right, right_dim, weights=None, cut=None):
    depth, high = left.shape
    wide = right.shape[1 - right_dim]
    rows, cols = min(512, high), min(1024, wide)
    right_block = (depth, cols) if right_dim == 0 else (cols, depth)
    right_map = (lambda n, m: (0, n)) if right_dim == 0 else (lambda n, m: (n, 0))
    specs = [pl.BlockSpec((depth, rows), lambda n, m: (0, m)), pl.BlockSpec(right_block, right_map)]
    outs = [jax.ShapeDtypeStruct((high, wide), BF16)]
    out_specs = [pl.BlockSpec((rows, cols), lambda n, m: (m, n))]
    args, kernel = (left, right), functools.partial(outer_kernel, right_dim)
    if weights is not None:
        args, kernel = (left, right, weights), functools.partial(outer_gain_kernel, right_dim, cut)
        specs.append(pl.BlockSpec((rows, weights.shape[1]), lambda n, m: (m, 0)))
        outs.append(jax.ShapeDtypeStruct((high, 128), F32))
        out_specs.append(pl.BlockSpec((rows, 128), lambda n, m: (m, 0)))
    return pl.pallas_call(
        kernel,
        out_shape=outs,
        grid=(wide // cols, high // rows),
        in_specs=specs,
        out_specs=out_specs,
        compiler_params=pltpu.CompilerParams(vmem_limit_bytes=56 * 2**20),
        cost_estimate=FREE,
        name="outer",
    )(*args)


def norm_back(values, scale, upstream):
    mean_term = jnp.mean(values * upstream, axis=1, keepdims=True)
    return scale * upstream - values * (scale * scale * scale) * mean_term


def shards(
    layer_in, lengths, clip_level, attn_gain, w_query, w_key, w_value, w_out,
    mlp_gain, w_gate, w_up, w_down, cotangent,
):
    tok_rows, width = layer_in.shape
    z_rank, y_rank = lax.axis_index("z"), lax.axis_index("y")
    rank = (y_rank * 2 + lax.axis_index("x")) * 2 + lax.axis_index("c")
    slots = lengths.shape[0]
    next_slot = (z_rank + 1) % slots
    info = jnp.stack(
        (rank, lax.dynamic_index_in_dim(lengths, z_rank, keepdims=False),
         lax.dynamic_index_in_dim(lengths, next_slot, keepdims=False))
    ).astype(jnp.int32)
    inner = rank * tok_rows + jnp.arange(tok_rows, dtype=jnp.int32) + LEAD
    own_mask = jnp.where(inner < SLOT_LEN, inner < info[1], inner - SLOT_LEN < info[2])
    own_mask = own_mask.astype(F32)[:, None]
    spots = ((jnp.arange(SLOT_LEN, dtype=jnp.int32) + LEAD) % SLOT_LEN).astype(F32)
    freq = THETA ** (-(jnp.arange(HALF, dtype=F32) * 2.0 / HD))
    angles = spots[None, :] * freq[:, None]
    cos, sin = jnp.cos(angles), jnp.sin(angles)
    def heads_part(which):
        return jnp.concatenate(
            (half_of(w_out, which, 0).T, half_of(w_query, which, 1), half_of(w_key, which, 1),
             half_of(w_value, which, 1)), 1
        )

    def ffn_part(which):
        return jnp.concatenate((half_of(w_gate, which, 1), half_of(w_up, which, 1)), 1)

    other_y = 1 - y_rank
    heads_w = ordered(heads_part(y_rank), swap(heads_part(other_y), "y"), y_rank, 0)
    full_heads = lax.all_gather(heads_w, "z", axis=0, tiled=True)
    out_cols = HEADS * HD
    heads_cut = (out_cols, full_heads.shape[1])

    ffn_own, ffn_sent = tie(ffn_part(y_rank), ffn_part(other_y))
    ffn_w = ordered(ffn_own, swap(ffn_sent, "y"), y_rank, 0)
    layer_f = layer_in.astype(F32)
    scale_one = lax.rsqrt(jnp.mean(layer_f * layer_f, axis=1, keepdims=True) + EPSILON)
    normal_one = rounded(layer_f * scale_one)
    gain_one = attn_gain.astype(F32)
    acts = gather_one(after((normal_one * gain_one[None, :]).astype(BF16), heads_w))
    acts = gather_two(acts)
    full_heads, ffn_w, *acts = tie(full_heads, ffn_w, *acts)
    full_out, full_qkv = full_heads[:, :out_cols], full_heads[:, out_cols:]
    acts_one = gather_three(acts)
    full_ffn = lax.all_gather(ffn_w, "z", axis=0, tiled=True)

    grad_out = cotangent.astype(F32)
    down_in = (RESIDUAL * own_mask * grad_out).astype(BF16)
    back_rows = gather_one(down_in)
    rows = acts_one.shape[0]
    flat = dot(full_qkv, acts_one, 0, 1)
    (qkv,) = call(
        rope_kernel, info, (flat, cos, sin), [((flat.shape[0], rows), BF16)], [], "rope"
    )
    halo = along(qkv[K_AT:, SLOT_LEN - LEAD :], 1)
    qkv, halo, *back_rows = tie(qkv, halo, *back_rows)
    down_other = swap(after(half_of(w_down, other_y, 0), back_rows[2], back_rows[3]), "y")
    back_rows = gather_two(back_rows)
    heads, lse, peak = call(
        attend_kernel, info, (qkv, halo),
        [((HEADS * HD, rows), BF16), ((8, rows), F32), ((8, 128), F32)],
        [((KEYS, HD), BF16), ((HD, KEYS), BF16), ((TOGETHER, SLOT_LEN, CHUNK), F32)],
        "attend",
    )
    heads, *back_rows = tie(heads, *back_rows)

    terms = [(heads, full_heads, 0, 1, (0, out_cols))]
    high_part, own_peak, down_other = tie(product(terms, 1), peak[:HEADS], down_other)
    came, other_peak = tie(swap(high_part, "c"), swap(own_peak, "y"))
    down_w = ordered(half_of(w_down, y_rank, 0), down_other, y_rank, 1)
    branch = spread_one(terms, came)
    head_peak = over_z(ordered(own_peak, other_peak, y_rank, 0), jnp.maximum)
    down_rows = gather_three(back_rows)
    *got, down_rows, down_w, head_peak = tie(*branch[2:4], down_rows, down_w, head_peak)
    head_peak = head_peak[:, 0]
    branch = spread_two((*branch[:2], *got))
    full_down = lax.all_gather(down_w, "z", axis=1, tiled=True)
    gain_two = mlp_gain.astype(F32)
    narrow = (tok_rows, width // 2)
    resid, scale_two, *acts = row_call(
        residual_kernel, (*branch[:4], layer_in, own_mask, gain_two[None, :]),
        [((tok_rows, width), F32), ((tok_rows, 1), F32), ((tok_rows, width), BF16),
         (narrow, BF16), (narrow, BF16)], "residual",
    )
    acts = gather_one(acts[0], acts[1:])
    full_ffn, *acts = tie(full_ffn, *acts)
    acts = gather_two(acts)
    acts_two = gather_three(acts)

    hid = full_ffn.shape[1] // 2
    gate_proj, up_proj, hidden = ffn_call(
        hidden_kernel, acts_two, full_ffn, hid, (F32, F32, BF16), (), "hidden"
    )

    def reduced(grad, axis):
        return lax.psum_scatter(grad, "z", scatter_dimension=axis, tiled=True)

    def traded(total, axis, *behind):
        total = after(total, *behind)
        return half_of(total, y_rank, axis), swap(half_of(total, other_y, axis), "y")

    (down_part,) = outer(hidden, down_rows, 0)
    down_sum = reduced(down_part, 1)
    down_rows = after(down_rows, down_part)
    def grads(part, rows):
        return ffn_call(
            hidden_back_kernel, rows, full_down, hid, (BF16, BF16), (gate_proj, up_proj),
            "hidden_back", part, 2,
        )

    def back_terms(gate_grad, up_grad):
        return [(gate_grad, full_ffn, 1, 1, None, 0), (up_grad, full_ffn, 1, 1, None, 1)]

    high_grads = grads(1, down_rows)
    high_part = product(back_terms(*((None, grad) for grad in high_grads)), 1)
    high_part, down_rows = tie(high_part, down_rows)
    low_grads = grads(0, down_rows)
    came, *low_grads = tie(swap(high_part, "c"), *low_grads)
    pairs = list(zip(low_grads, high_grads, strict=True))
    *norm_two, acts_two = spread_one(back_terms(*pairs), came, acts_two)
    ffn_parts = [outer_halves(acts_two, *pair) for pair in pairs]
    *got, ffn_parts[0], ffn_parts[1] = tie(*norm_two[2:4], *ffn_parts)
    one_sum, two_sum = [reduced(part, 0) for part in ffn_parts]
    norm_two = spread_two((*norm_two[:2], *got))
    gain_two_part, grad_resid, *mixed = row_call(
        residual_back_kernel,
        (*norm_two[:4], cotangent, resid, scale_two, gain_two[None, :], own_mask),
        [((8, width), F32), ((tok_rows, width), F32), ((tok_rows, width), BF16), (narrow, BF16),
         (narrow, BF16)], "residual_back",
    )
    mixed_in, hidden = tie(mixed[0], hidden)
    mixed = gather_one(mixed_in, mixed[1:])
    terms = [(hidden, full_down, 1, 0, None)]
    *got, high_part = tie(*mixed[2:4], product(terms, 1))
    mixed = gather_two((*mixed[:2], *got))
    low_part = product(terms, 0, swap(high_part, "c"))
    a1, b1, *low_part = tie(*mixed[5:], *low_part)
    mixed = (*mixed[:5], a1, b1)
    second = (*low_part[:2], swap(low_part[2], "x"), swap(low_part[3], "y"))
    mixed_rows = gather_three(mixed)
    mixed_rows, down_sum, one_sum = tie(mixed_rows, down_sum, one_sum)
    down_own, down_other = traded(down_sum, 1)
    one_own, one_other = traded(one_sum, 0)

    heads_grad = dot(full_out, mixed_rows, 0, 1).astype(BF16)
    dq, dkv, back = call(
        attend_back_kernel, info, (qkv, halo, heads_grad, lse, cos, sin),
        [((HEADS * HD, rows), BF16), ((2 * HD, rows), F32), ((2 * HD, LEAD), BF16)],
        [((KEYS, HD), BF16), ((KEYS, HD), BF16), ((HD, KEYS), BF16),
         ((TOGETHER, SLOT_LEN, CHUNK), F32), ((TOGETHER, SLOT_LEN, CHUNK), F32),
         ((KEYS, HD), F32), ((KEYS, HD), F32), ((HEADS * HD, SLOT_LEN), BF16)],
        "attend_back", 60,
    )
    back, down_other, one_other, *got = tie(back, down_other, one_other, *second[2:4])
    back_sent = along(back, -1)
    left, right, *sent = fold(*second[:2], *got)
    (out_part,) = outer(mixed_rows, heads, 1)
    dkv, back_sent, out_part, *sent = tie(dkv, back_sent, out_part, *sent)
    second = left, right, swap(sent[0], "y"), swap(sent[1], "x")
    (dkv_done,) = call(
        finish_kernel, info, (dkv, back_sent, cos, sin), [((2 * HD, rows), BF16)], [], "finish"
    )
    dqkv = jnp.concatenate((dq, dkv_done))
    terms = [(dqkv, full_heads, 0, 1, heads_cut)]
    high_part, acts_one = tie(product(terms, 1), acts_one)
    qkv_part, sums = outer(acts_one, dqkv, 1, full_heads, heads_cut)
    came, qkv_part, sums, two_sum, *got = tie(
        swap(high_part, "c"), qkv_part, sums, two_sum, *second[2:4]
    )
    two_own = half_of(two_sum, y_rank, 0)
    came, two_sent = tie(came, half_of(two_sum, other_y, 0))
    heads_sum = reduced(jnp.concatenate((out_part, qkv_part), axis=1), 0)
    second = (*second[:2], *got)
    *norm_one, sums, two_other = spread_one(terms, came, sums, swap(two_sent, "y"))
    gains = jnp.stack((sums[:, 0] / gain_one, jnp.sum(gain_two_part, axis=0)))
    gains = over_z(gains, jnp.add)
    gains, down_own, down_other, one_own, one_other, head_peak, *second = tie(
        gains, down_own, down_other, one_own, one_other, head_peak, *second
    )
    down_grad = ordered(down_own, down_other, y_rank, 0).astype(F32)
    gate_w_grad = ordered(one_own, one_other, y_rank, 1).astype(F32)
    level = clip_level[0].astype(F32) * LEVEL_UNIT
    factor = level / jnp.maximum(level, head_peak)
    query_clipped = w_query.astype(F32) * jnp.repeat(jnp.sqrt(factor), HD)[None, :]
    result = (resid + RESIDUAL * own_mask * spread_three(second)).astype(BF16)
    *got, gains, down_grad, gate_w_grad, query_clipped, result = tie(
        *norm_one[2:4], gains, down_grad, gate_w_grad, query_clipped, result
    )
    gains = gains.reshape(2, lax.axis_size("z"), 2, 2, 2, -1)

    def halved(gains, dim, axis):
        at = lax.axis_index(axis)
        return (lax.dynamic_index_in_dim(gains, at, dim, keepdims=False),
                lax.dynamic_index_in_dim(gains, 1 - at, dim, keepdims=False))

    norm_one = spread_two((*norm_one[:2], *got), gains, folding=fold)
    gains = norm_one[4]
    own, heads_sent = half_of(heads_sum, y_rank, 0), half_of(heads_sum, other_y, 0)
    kept, sent = halved(gains, 4, "c")
    kept, sent = halved(kept + swap(sent, "c"), 3, "x")
    *norm_one, heads_sent, kept, sent = tie(*norm_one[:4], heads_sent, kept, sent)
    other = swap(heads_sent, "y")
    out_own, out_other = own[:, :out_cols], other[:, :out_cols]
    own, other = own[:, out_cols:], other[:, out_cols:]
    grad_input = input_back(*norm_one, grad_resid, layer_in, scale_one, gain_one[None, :])
    kept, sent = halved(kept + swap(sent, "x"), 2, "y")
    gains = lax.dynamic_index_in_dim(kept + swap(sent, "y"), z_rank, 1, keepdims=False)

    up_w_grad = ordered(two_own, two_other, y_rank, 1).astype(F32)
    out_grad = ordered(out_own.T, out_other.T, y_rank, 0).astype(F32)

    def columns(start, stop):
        return ordered(own[:, start:stop], other[:, start:stop], y_rank, 1).astype(F32)

    query_grad = columns(0, K_AT)
    key_grad = columns(K_AT, V_AT)
    value_grad = columns(V_AT, V_AT + HD)

    kv_factor = jnp.min(factor.reshape(-1, HEADS), axis=1)
    key_clipped = w_key.astype(F32) * jnp.repeat(jnp.sqrt(kv_factor), HD)[None, :]
    return (
        result,
        grad_input,
        gains[0],
        query_grad,
        key_grad,
        value_grad,
        out_grad,
        gains[1],
        gate_w_grad,
        up_w_grad,
        down_grad,
        query_clipped,
        key_clipped,
    )


def solution(mesh):
    fsdp, tp = mesh.shape["fsdp"], mesh.shape["tp"]
    fine = Mesh(mesh.devices.reshape(fsdp // 2, 2, tp // 2, 2), EVERY)
    rows, cols = ("z", "y"), ("x", "c")
    tokens, down, across = P(EVERY, None), P(rows, cols), P(cols, rows)
    in_specs = (
        tokens, P(), P(), P(), down, down, down, across, P(), down, down, across, tokens,
    )
    out_specs = (
        tokens, tokens, P(EVERY), down, down, down, across, P(EVERY), down, down, across,
        down, down,
    )
    return jax.shard_map(shards, mesh=fine, in_specs=in_specs, out_specs=out_specs, check_vma=False)
```
